32 devices in a mesh: seq: 8 (over z, y), tp: 4 (over x, core).
Axes of the slice: x: 2, y: 2, z: 4, core: 2. Of those that a mesh axis runs over, the one named last changes fastest.
Arguments:
- layer_input: bfloat16 [4096, 1024], P('seq'), may hold values from -6 to 6
- seq_groups: int32 [16], replicated, may hold values from 1 to 16, 64 in all
- seq_pads: int32 [16], replicated, may hold values from 0 to 7
- norm_in: bfloat16 [1024], replicated, may hold values from 0.5 to 1.5
- w_query: bfloat16 [1024, 1024], P(None, 'tp'), may hold values from -0.1875 to 0.1875
- w_key: bfloat16 [1024, 1024], P(None, 'tp'), may hold values from -0.1875 to 0.1875
- w_value: bfloat16 [1024, 1024], P(None, 'tp'), may hold values from -0.1875 to 0.1875
- conv_query: bfloat16 [4, 1024], P(None, 'tp'), may hold values from -3 to 3
- conv_key: bfloat16 [4, 1024], P(None, 'tp'), may hold values from -3 to 3
- conv_value: bfloat16 [4, 1024], P(None, 'tp'), may hold values from -3 to 3
- w_beta: bfloat16 [1024, 8], P(None, 'tp'), may hold values from -0.1875 to 0.1875
- w_gate_out: bfloat16 [1024, 1024], P(None, 'tp'), may hold values from -0.1875 to 0.1875
- norm_head: bfloat16 [128], replicated, may hold values from 0.5 to 1.5
- w_out: bfloat16 [1024, 1024], P('tp'), may hold values from -0.1875 to 0.1875
- norm_mid: bfloat16 [1024], replicated, may hold values from 0.5 to 1.5
- w_gate: bfloat16 [1024, 2816], P(None, 'tp'), may hold values from -0.1875 to 0.1875
- w_up: bfloat16 [1024, 2816], P(None, 'tp'), may hold values from -0.1875 to 0.1875
- w_down: bfloat16 [2816, 1024], P('tp'), may hold values from -0.109375 to 0.109375
- cotangent: bfloat16 [4096, 1024], P('seq'), may hold values from -6 to 6
Outputs:
- block_out: bfloat16 [4096, 1024], P('seq')
- grad_input: float32 [4096, 1024], P('seq')
- grad_norm_in: float32 [1024], P('tp')
- grad_w_query: float32 [1024, 1024], P(None, 'tp')
- grad_w_key: float32 [1024, 1024], P(None, 'tp')
- grad_w_value: float32 [1024, 1024], P(None, 'tp')
- grad_conv_query: float32 [4, 1024], P(None, 'tp')
- grad_conv_key: float32 [4, 1024], P(None, 'tp')
- grad_conv_value: float32 [4, 1024], P(None, 'tp')
- grad_w_beta: float32 [1024, 8], P(None, 'tp')
- grad_w_gate_out: float32 [1024, 1024], P(None, 'tp')
- grad_norm_head: float32 [128], P('tp')
- grad_w_out: float32 [1024, 1024], P('tp')
- grad_norm_mid: float32 [1024], P('tp')
- grad_w_gate: float32 [1024, 2816], P(None, 'tp')
- grad_w_up: float32 [1024, 2816], P(None, 'tp')
- grad_w_down: float32 [2816, 1024], P('tp')
The draws below stay inside these ranges and needn't reach their ends.
Inputs may be any that keep to these rules, and one draw needn't show every extreme that they name: `seq_groups`: they sum to 64; the largest is exactly 16.
All inputs are finite; a program needn't handle non-finite values.
Results may differ from the reference program's by a relative error of at most 0.009.
The reference program's roundings to bfloat16 on the way count: a program that leaves them out, or rounds other values in their place, can miss the bound.
Values may be sent and summed in bfloat16 or wider, within the bound.
No kernel may reach another device: no remote copies, remote signals or barrier semaphores. Data moves between devices by JAX's collectives and lax.ppermute only.
A program may use at most 192 MiB of HBM per device.

```python
import math
import jax
import jax.numpy as jnp
import numpy as np
from jax import lax

D = 1024
H = 8
DH = 128
FF = 2816
KW = 4
GROUP = 64
PADS = 8
TOKENS = 4096
GROUPS_ALL = 64
MAX_GROUPS = 16
NSEQ = 16


def plant(entries, own_key, least, high):
    dims = entries.shape
    index_at = [jax.random.randint(jax.random.fold_in(own_key, axis), (), 0, dims[axis]) for axis in range(len(dims))]
    entries = entries.at[tuple(index_at)].set(least)
    longest = dims.index(max(dims))
    index_at[longest] = (index_at[longest] + 1) % dims[longest]
    return entries.at[tuple(index_at)].set(high)


def block_scale(rng, dims, cuts, low, top_value):
    def one(dim, parts):
        draws = jax.random.uniform(jax.random.fold_in(jax.random.fold_in(rng, 6), dim), (parts,), jnp.float32, low / len(cuts), top_value / len(cuts))
        return jnp.repeat(jnp.exp(draws), dims[dim] // parts).reshape((-1,) + (1,) * (len(dims) - dim - 1))

    level = one(*cuts[0])
    for cut in cuts[1:]:
        level = level * one(*cut)
    return level


def profile(count, total, reach, slope):
    loads = [(1 << 20) // math.isqrt(grade ** slope) + 1 for grade in range(2, count + 1)]
    surplus, counts = total - reach - (count - 1), [1] * (count - 1)
    while surplus > 0:
        movable = [i for i in range(count - 1) if counts[i] < reach]
        whole, left = sum([loads[i] for i in movable]), surplus
        for i in movable:
            addition = min(reach - counts[i], max(1, left * loads[i] // whole), surplus)
            counts[i] = counts[i] + addition
            surplus = surplus - addition
    return np.array([reach] + counts)


def ragged(own_key, count, total, most, slope):
    if count == 2:
        one = jax.random.randint(own_key, (), max(1, total - most), min(most, total - 1) + 1)
        return jnp.stack([one, total - one])
    lengths = jnp.asarray(profile(count, total, most, slope), jnp.int32)
    pairs = (count - 1) // 2
    donor, taker = lengths[1:1 + 2 * pairs:2], lengths[2:2 + 2 * pairs:2]
    slack = jnp.minimum(donor - 1, most - taker)
    shifted = jax.random.randint(jax.random.fold_in(own_key, 1), (pairs,), 0, 1 << 20) % (slack + 1)
    lengths = lengths.at[1:1 + 2 * pairs:2].set(donor - shifted).at[2:2 + 2 * pairs:2].set(taker + shifted)
    return lengths[jax.random.permutation(jax.random.fold_in(own_key, 2), count)]


def normal_values(own_key, shape, spread, most, cuts=(), held_as=jnp.bfloat16):
    entries = jax.random.normal(own_key, shape, jnp.float32) * spread
    if len(cuts) > 0:
        entries = block_scale(own_key, shape, cuts, -0.22, 0.18) * entries
    return jnp.clip(entries, min=-most, max=most).astype(held_as)


def setup_inputs(seed: int = 0) -> dict:
    arg_keys = jax.random.split(jax.random.key(seed), 20)
    layer_input = normal_values(arg_keys[0], (TOKENS, D), 1.0, 6.0, ((0, 8),))
    seq_groups = ragged(arg_keys[1], NSEQ, GROUPS_ALL, MAX_GROUPS, 2).astype(jnp.int32)
    seq_pads = plant(jax.random.randint(arg_keys[2], (NSEQ,), 0, PADS), jax.random.fold_in(arg_keys[2], 1), 0, PADS - 1).astype(jnp.int32)
    norm_in = jnp.clip(1.0 + 0.1 * jax.random.normal(arg_keys[3], (D,), jnp.float32), 0.5, 1.5).astype(jnp.bfloat16)
    w_query = normal_values(arg_keys[4], (D, D), D ** -0.5, 0.1875, ((1, 4),))
    w_key = normal_values(arg_keys[5], (D, D), D ** -0.5, 0.1875, ((1, 4),))
    w_value = normal_values(arg_keys[6], (D, D), D ** -0.5, 0.1875, ((1, 4),))
    conv_query = normal_values(arg_keys[7], (KW, D), KW ** -0.5, 3.0, ((1, 4),))
    conv_key = normal_values(arg_keys[8], (KW, D), KW ** -0.5, 3.0, ((1, 4),))
    conv_value = normal_values(arg_keys[9], (KW, D), KW ** -0.5, 3.0, ((1, 4),))
    w_beta = normal_values(arg_keys[10], (D, H), D ** -0.5, 0.1875, ((1, 4),))
    w_gate_out = normal_values(arg_keys[11], (D, D), D ** -0.5, 0.1875, ((1, 4),))
    norm_head = jnp.clip(1.0 + 0.1 * jax.random.normal(arg_keys[12], (DH,), jnp.float32), 0.5, 1.5).astype(jnp.bfloat16)
    w_out = normal_values(arg_keys[13], (D, D), D ** -0.5, 0.1875, ((0, 4),))
    norm_mid = jnp.clip(1.0 + 0.1 * jax.random.normal(arg_keys[14], (D,), jnp.float32), 0.5, 1.5).astype(jnp.bfloat16)
    w_gate = normal_values(arg_keys[15], (D, FF), D ** -0.5, 0.1875, ((1, 4),))
    w_up = normal_values(arg_keys[16], (D, FF), D ** -0.5, 0.1875, ((1, 4),))
    w_down = normal_values(arg_keys[17], (FF, D), FF ** -0.5, 0.109375, ((0, 4),))
    cotangent = normal_values(arg_keys[18], (TOKENS, D), 1.0, 6.0, ((0, 8),))
    return dict(layer_input=layer_input, seq_groups=seq_groups, seq_pads=seq_pads, norm_in=norm_in, w_query=w_query, w_key=w_key, w_value=w_value, conv_query=conv_query, conv_key=conv_key, conv_value=conv_value, w_beta=w_beta, w_gate_out=w_gate_out, norm_head=norm_head, w_out=w_out, norm_mid=norm_mid, w_gate=w_gate, w_up=w_up, w_down=w_down, cotangent=cotangent)


HIGHEST = lax.Precision.HIGHEST
row_epsilon = 1e-06
head_epsilon = 1e-05
unit_epsilon = 1e-06

@jax.custom_vjp
def low(v):
    return lax.optimization_barrier(v.astype(jnp.bfloat16)).astype(jnp.float32)

@jax.custom_vjp
def low_back(v):
    return v

def low_keep(v):
    return (low(v), None)

def low_pass(kept, grad):
    return (grad,)

def back_keep(v):
    return (v, None)

def back_low(kept, grad):
    return (low(grad),)
low.defvjp(low_keep, low_pass)
low_back.defvjp(back_keep, back_low)

def layout(seq_groups, seq_pads, group_count, first_group):
    seq_ends = jnp.cumsum(seq_groups, dtype=jnp.int32)
    starts = seq_ends - seq_groups
    group_ids = first_group + jnp.arange(group_count, dtype=jnp.int32)
    owner_table = ((group_ids[:, None] >= starts[None, :]) & (group_ids[:, None] < seq_ends[None, :])).astype(jnp.int32)
    start_of = lax.optimization_barrier(jnp.sum(owner_table * starts[None, :], axis=1, dtype=jnp.int32))
    length_of = lax.optimization_barrier(jnp.sum(owner_table * (seq_groups * GROUP - seq_pads)[None, :], axis=1, dtype=jnp.int32))
    restart = (group_ids == start_of).astype(jnp.float32)
    position = ((group_ids - start_of) * GROUP)[:, None] + jnp.arange(GROUP, dtype=jnp.int32)[None, :]
    live_rows = (position < length_of[:, None]).astype(jnp.float32)
    return (restart, position.reshape(-1), live_rows.reshape(-1))

def row_norm(values, gain):
    factor = lax.rsqrt(lax.optimization_barrier(jnp.mean(values * values, axis=-1, keepdims=True)) + row_epsilon)
    return values * factor * gain

def gated_norm(outputs, gain, gate_heads):
    factor = lax.rsqrt(lax.optimization_barrier(jnp.mean(outputs * outputs, axis=-1, keepdims=True)) + head_epsilon)
    return outputs * factor * gain * jax.nn.silu(gate_heads)

def causal_conv(extended, tap_table, position):
    row_count = position.shape[0]
    summed = jnp.zeros((row_count, extended.shape[1]), extended.dtype)
    for tap_number in range(KW):
        distance = KW - 1 - tap_number
        keep_mask = (position >= distance).astype(extended.dtype)[:, None]
        summed = summed + tap_table[tap_number] * extended[tap_number:tap_number + row_count] * keep_mask
    return summed

def activate(conv_out, model_width):
    acted = jax.nn.silu(conv_out)
    row_count = conv_out.shape[0]
    query_rows = acted[:, :model_width].reshape(row_count, -1, DH)
    key_rows = acted[:, model_width:2 * model_width].reshape(row_count, -1, DH)
    value_rows = acted[:, 2 * model_width:].reshape(row_count, -1, DH)
    query_rows = query_rows * lax.rsqrt(lax.optimization_barrier(jnp.sum(query_rows * query_rows, axis=-1, keepdims=True)) + unit_epsilon)
    key_rows = key_rows * lax.rsqrt(lax.optimization_barrier(jnp.sum(key_rows * key_rows, axis=-1, keepdims=True)) + unit_epsilon)
    return (query_rows, key_rows, value_rows)

def wy_parts(key_rows, value_rows, beta_rows):
    group_len = key_rows.shape[1]
    key_dots = jnp.einsum('nihd,njhd->nhij', key_rows, key_rows, precision=HIGHEST)
    strict = jnp.tril(jnp.ones((group_len, group_len), key_rows.dtype), -1)
    beta_heads = jnp.swapaxes(beta_rows, 1, 2)
    system = jnp.eye(group_len, dtype=key_rows.dtype) + strict * beta_heads[..., None] * key_dots
    scaled_keys = jnp.swapaxes(beta_rows[..., None] * key_rows, 1, 2)
    scaled_values = jnp.swapaxes(beta_rows[..., None] * value_rows, 1, 2)
    key_mix = jax.scipy.linalg.solve_triangular(system, scaled_keys, lower=True, unit_diagonal=True)
    value_mix = jax.scipy.linalg.solve_triangular(system, scaled_values, lower=True, unit_diagonal=True)
    return (key_mix, value_mix)

def group_apply(query_rows, key_rows, key_mix, value_mix, start_states):
    group_len = key_rows.shape[1]
    inclusive = jnp.tril(jnp.ones((group_len, group_len), key_rows.dtype))
    value_new = value_mix - jnp.einsum('nhcd,nhde->nhce', key_mix, start_states, precision=HIGHEST)
    scores = jnp.einsum('nihd,njhd->nhij', query_rows, key_rows, precision=HIGHEST) * inclusive
    produced = jnp.einsum('nihd,nhde->nihe', query_rows, start_states, precision=HIGHEST)
    produced = produced + jnp.einsum('nhij,nhje->nihe', scores, value_new, precision=HIGHEST)
    final_state = start_states + jnp.einsum('nihd,nhie->nhde', key_rows, value_new, precision=HIGHEST)
    return (produced, final_state)

def group_full(query_rows, key_rows, value_rows, beta_rows, start_states):
    key_mix, value_mix = wy_parts(key_rows, value_rows, beta_rows)
    return group_apply(query_rows, key_rows, key_mix, value_mix, start_states)

def forward(params, inputs, live_rows, position, restart):
    norm_in, w_query, w_key, w_value, conv_query, conv_key, conv_value, w_beta, w_gate_out, norm_head, w_out, norm_mid, w_gate, w_up, w_down = params
    total_rows = inputs.shape[0]
    block_rows = math.gcd(total_rows, 4096)
    blocks = total_rows // block_rows
    per_block = block_rows // GROUP
    proj_cat = jnp.concatenate([w_query, w_key, w_value], axis=1)
    tap_table = jnp.concatenate([conv_query, conv_key, conv_value], axis=1)

    def run_block(carried, pieces):
        state_now, tail_rows = carried
        rows_in, live_col, positions, restarts = pieces
        hidden = low(row_norm(rows_in, norm_in))
        projected = low_back(jnp.dot(hidden, proj_cat, precision=HIGHEST))
        gate_raw = low_back(jnp.dot(hidden, w_gate_out, precision=HIGHEST))
        beta_raw = low_back(jnp.dot(hidden, w_beta, precision=HIGHEST))
        conv_out = causal_conv(jnp.concatenate([tail_rows, projected], axis=0), tap_table, positions)
        query_rows, key_rows, value_rows = activate(conv_out, D)
        beta_rows = jax.nn.sigmoid(beta_raw) * live_col[:, None]

        def group_step(state_in, group_pieces):
            q_part, k_part, v_part, b_part, fresh_one = group_pieces
            start_state = state_in * (1.0 - fresh_one)
            produced, final_state = group_full(q_part[None], k_part[None], v_part[None], b_part[None], start_state[None])
            return (final_state[0], produced[0])
        state_now, produced = lax.scan(group_step, state_now, (query_rows.reshape(per_block, GROUP, H, DH), key_rows.reshape(per_block, GROUP, H, DH), value_rows.reshape(per_block, GROUP, H, DH), beta_rows.reshape(per_block, GROUP, H), restarts))
        heads_out = produced.reshape(block_rows, H, DH)
        normed = gated_norm(heads_out, norm_head, gate_raw.reshape(block_rows, H, DH))
        attended = low(normed.reshape(block_rows, D))
        branch = low_back(jnp.dot(attended, w_out, precision=HIGHEST))
        residual = rows_in + branch
        second = low(row_norm(residual, norm_mid))
        gate_val = low_back(jnp.dot(second, w_gate, precision=HIGHEST))
        up_val = low_back(jnp.dot(second, w_up, precision=HIGHEST))
        inner_act = low(jax.nn.silu(gate_val) * up_val)
        down_val = low_back(jnp.dot(inner_act, w_down, precision=HIGHEST))
        result = (residual + down_val) * live_col[:, None]
        return ((state_now, projected[block_rows - (KW - 1):]), result)
    initial = (jnp.zeros((H, DH, DH), jnp.float32), jnp.zeros((KW - 1, 3 * D), jnp.float32))
    _, outputs = lax.scan(jax.checkpoint(run_block), initial, (inputs.reshape(blocks, block_rows, D), live_rows.reshape(blocks, block_rows), position.reshape(blocks, block_rows), restart.reshape(blocks, per_block)))
    return outputs.reshape(total_rows, D)

def reference(layer_input, seq_groups, seq_pads, norm_in, w_query, w_key, w_value, conv_query, conv_key, conv_value, w_beta, w_gate_out, norm_head, w_out, norm_mid, w_gate, w_up, w_down, cotangent):
    restart, position, live_rows = layout(seq_groups, seq_pads, GROUPS_ALL, 0)
    params = (norm_in.astype(jnp.float32), w_query.astype(jnp.float32), w_key.astype(jnp.float32), w_value.astype(jnp.float32), conv_query.astype(jnp.float32), conv_key.astype(jnp.float32), conv_value.astype(jnp.float32), w_beta.astype(jnp.float32), w_gate_out.astype(jnp.float32), norm_head.astype(jnp.float32), w_out.astype(jnp.float32), norm_mid.astype(jnp.float32), w_gate.astype(jnp.float32), w_up.astype(jnp.float32), w_down.astype(jnp.float32))
    result, pullback = jax.vjp(lambda rows_in, weights: forward(weights, rows_in, live_rows, position, restart), layer_input.astype(jnp.float32), params)
    grad_input, gradients = pullback(cotangent.astype(jnp.float32))
    return (result.astype(jnp.bfloat16), grad_input, gradients[0], gradients[1], gradients[2], gradients[3], gradients[4], gradients[5], gradients[6], gradients[7], gradients[8], gradients[9], gradients[10], gradients[11], gradients[12], gradients[13], gradients[14])
```

```python
import jax
import jax.numpy as jnp
from jax import lax
from jax.experimental import pallas as pl
from jax.experimental.pallas import tpu as pltpu
from jax.sharding import PartitionSpec as P

DH = 128
KW = 4
GROUP = 64
TAIL = 16
LANES = 128

row_epsilon = 1e-06
head_epsilon = 1e-05
unit_epsilon = 1e-06
f32 = jnp.float32
bf16 = jnp.bfloat16


def dot(a, b, ca=1, cb=0):
    return lax.dot_general(a, b, (((ca,), (cb,)), ((), ())), preferred_element_type=f32)


def halves(a):
    high = a.astype(bf16)
    return high, (a - high.astype(f32)).astype(bf16)


def fdot(a, b, ca=1, cb=0):
    ah, al = halves(a)
    bh, bl = halves(b)
    return dot(
        jnp.concatenate([ah, al, ah], axis=ca), jnp.concatenate([bh, bh, bl], axis=cb), ca, cb
    )


def iota(shape, axis):
    return lax.broadcasted_iota(jnp.int32, shape, axis)


def rows_of(block, size):
    return pl.ds(pl.multiple_of(block * size, size), size)


def run(kernel, name, outs, args, smem=(), smem_out=(), hbm=(), scratch=(), flops=0, vmem=8):
    shapes = [jax.ShapeDtypeStruct(s, d) for s, d in outs]
    total = sum(a.size * a.dtype.itemsize for a in args)
    total += sum(s.size * s.dtype.itemsize for s in shapes)
    spaces = [
        pltpu.SMEM if i in smem else pltpu.HBM if i in hbm else pltpu.VMEM
        for i in range(len(args))
    ]
    return pl.pallas_call(
        kernel,
        name=name,
        out_shape=shapes,
        in_specs=[pl.BlockSpec(memory_space=space) for space in spaces],
        out_specs=[
            pl.BlockSpec(memory_space=pltpu.SMEM if i in smem_out else pltpu.VMEM)
            for i in range(len(outs))
        ],
        scratch_shapes=list(scratch),
        compiler_params=pltpu.CompilerParams(vmem_limit_bytes=vmem << 20),
        cost_estimate=pl.CostEstimate(flops=flops, bytes_accessed=total, transcendentals=0),
    )(*args)


def wide_gain(ref):
    return ref[...].astype(f32).reshape(1, ref.shape[0])


def live_mask(meta, block, size):
    parts = size // GROUP
    row = iota((size, 1), 0)
    limit = jnp.full((size, 1), 0, jnp.int32) + meta[1, block * parts]
    for part in range(1, parts):
        limit = jnp.where(row >= part * GROUP, meta[1, block * parts + part] + part * GROUP, limit)
    return row < limit


def rms_rows(values, gain):
    factor = lax.rsqrt(jnp.mean(values * values, axis=-1, keepdims=True) + row_epsilon)
    return values * factor * gain


def pre_kernel(first, tp, seq_groups, seq_pads, xh, coth, gain, wqh, wkh, wvh, wgh, wb, hidden, proj, gate, beta, grad_down, x_own, gd_own, meta, x, cot, wq, wk, wv, wg, sems):
    loads = [
        pltpu.make_async_copy(src, dst, sems.at[i])
        for i, (src, dst) in enumerate(
            ((xh, x), (wqh, wq), (wkh, wk), (wvh, wv), (wgh, wg), (coth, cot))
        )
    ]
    for load in loads:
        load.start()
    groups = x.shape[0] // GROUP
    for n in range(groups):
        meta[0, n] = 0
        meta[1, n] = 0

    def one(s, start):
        count = seq_groups[s]
        length = count * GROUP - seq_pads[s]
        for n in range(groups):
            gid = first[0] + n
            inside = (gid >= start) & (gid < start + count)
            here = jnp.clip(length - (gid - start) * GROUP, 0, GROUP)
            meta[0, n] = jnp.where(gid == start, 1, meta[0, n])
            meta[1, n] = jnp.where(inside, here, meta[1, n])
        return start + count

    lax.fori_loop(0, seq_groups.shape[0], one, jnp.int32(0))
    width = wq.shape[1]
    tile = 256
    share = x_own.shape[0]
    scale = wide_gain(gain)
    loads[0].wait()
    for t in range(x.shape[0] // tile):
        rows = slice(t * tile, (t + 1) * tile)
        hidden[rows] = rms_rows(x[rows].astype(f32), scale).astype(bf16)
    x_own[...] = x[rows_of(tp[0], share)]
    for t in range(x.shape[0] // tile):
        rows = slice(t * tile, (t + 1) * tile)
        beta[rows] = dot(hidden[rows], wb[...], 1, 1)
    for i, w in enumerate((wq, wk, wv, wg)):
        loads[1 + i].wait()
        for t in range(x.shape[0] // tile):
            rows = slice(t * tile, (t + 1) * tile)
            got = dot(hidden[rows], w[...])
            if i < 3:
                proj[rows, i * width : (i + 1) * width] = got
            else:
                gate[rows] = got
    loads[5].wait()
    for t in range(x.shape[0] // tile):
        rows = slice(t * tile, (t + 1) * tile)
        live = live_mask(meta, t, tile)
        grad_down[rows] = jnp.where(live, cot[rows].astype(f32), 0.0).astype(bf16)
    gd_own[...] = grad_down[rows_of(tp[0], share)]


def beta_col(beta, meta, n, h):
    raw = beta[pl.ds(pl.multiple_of(n * GROUP, GROUP), GROUP), h : h + 1]
    sig = jax.nn.sigmoid(raw)
    live = iota((GROUP, 1), 0) < meta[1, n]
    return jnp.where(live, sig, 0.0), sig, live


def unit(rows):
    return rows * lax.rsqrt(jnp.sum(rows * rows, axis=-1, keepdims=True) + unit_epsilon)


def tri_inverse(systems):
    size = systems[0].shape[0]
    eye = (iota((size, size), 0) == iota((size, size), 1)).astype(f32)
    blocks = [[eye[r : r + 8] for r in range(0, size, 8)] for _ in systems]
    lower = [[system[r : r + 8] for r in range(0, size, 8)] for system in systems]
    for j in range(size - 1):
        for low, part in zip(lower, blocks):
            line = part[j // 8][j % 8 : j % 8 + 1]
            for r in range((j + 1) // 8, size // 8):
                part[r] = part[r] - low[r][:, j : j + 1] * line
    return [jnp.concatenate(part, axis=0) for part in blocks]


def tap_table(*tables):
    values = [table[...].astype(f32) for table in tables]
    parts = values[0].shape[1] // DH
    return lambda j, c: values[c // parts][j : j + 1, (c % parts) * DH : (c % parts + 1) * DH]


def mix_kernel(meta, proj, tail, gain, wqh, wkh, wvh, cq, ck, cv, beta, ext, conv, qkv, wmix, umix, inv, score, amap, zst, dev, last, mout, oloc, badd, wq, wk, wv, sems):
    groups = proj.shape[0] // GROUP
    width = wq.shape[1]
    heads = width // DH
    loads = [
        pltpu.make_async_copy(src, dst, sems.at[i])
        for i, (src, dst) in enumerate(((wqh, wq), (wkh, wk), (wvh, wv)))
    ]
    for load in loads:
        load.start()
    ext[TAIL:] = proj[...]
    row = iota((GROUP, 1), 0)
    taps = tap_table(cq, ck, cv)
    low = rms_rows(tail[...].astype(f32), wide_gain(gain)).astype(bf16)

    def front(n):
        base = pl.multiple_of(n * GROUP, GROUP)
        for c in range(3 * heads):
            lanes = slice(c * DH, (c + 1) * DH)
            win = ext[pl.ds(pl.multiple_of(base + TAIL - 8, 8), GROUP + 8), lanes]
            acc = taps(KW - 1, c) * win[8:]
            for d in range(1, KW):
                part = jnp.where(row < meta[0, n] * d, 0.0, win[8 - d : 8 - d + GROUP])
                acc = acc + taps(KW - 1 - d, c) * part
            conv[pl.ds(base, GROUP), lanes] = acc
            acted = acc * jax.nn.sigmoid(acc)
            qkv[pl.ds(base, GROUP), lanes] = unit(acted) if c < 2 * heads else acted

    pl.loop(1, groups)(front)
    for i, w in enumerate((wq, wk, wv)):
        loads[i].wait()
        ext[0:TAIL, i * width : (i + 1) * width] = dot(low, w[...])
    front(0)
    r64 = iota((GROUP, GROUP), 0)
    c64 = iota((GROUP, GROUP), 1)
    eye = (iota((DH, DH), 0) == iota((DH, DH), 1)).astype(f32)

    def load(n, h):
        rows = pl.ds(pl.multiple_of(n * GROUP, GROUP), GROUP)
        return [qkv[rows, (i * heads + h) * DH : (i * heads + h + 1) * DH] for i in range(3)]

    def local(i, _):
        chains = [(2 * i + j, h) for j in range(2) for h in range(heads)]
        systems = []
        kept = []
        for n, h in chains:
            q, k, v = load(n, h)
            b = beta_col(beta, meta, n, h)[0]
            both = fdot(jnp.concatenate([k * b, q], axis=0), k, 1, 1)
            systems.append(jnp.where(r64 > c64, both[:GROUP], 0.0))
            score[n * heads + h] = jnp.where(r64 >= c64, both[GROUP:], 0.0)
            kept.append((k, b, v))
        inverses = tri_inverse(systems)
        for (n, h), inverse, (k, b, v) in zip(chains, inverses, kept):
            rows = pl.ds(pl.multiple_of(n * GROUP, GROUP), GROUP)
            inv[n * heads + h] = inverse
            wu = fdot(inverse, jnp.concatenate([k * b, v * b], axis=1))
            wmix[rows, h * DH : (h + 1) * DH] = wu[:, :DH]
            umix[rows, h * DH : (h + 1) * DH] = wu[:, DH:]
            kwu = fdot(k, wu, 0, 0)
            amap[n * heads + h] = eye - kwu[:, :DH]
            badd[n * heads + h] = kwu[:, DH:]
        return 0

    lax.fori_loop(0, groups // 2, local, 0)
    for h in range(heads):
        dev[h, :, :DH] = eye
        dev[h, :, DH:] = jnp.zeros((DH, DH), f32)

    def chain(n, _):
        keep = 1.0 - meta[0, n].astype(f32)
        for h in range(heads):
            start = dev[h] * keep
            zst[n * heads + h] = start
            moved = fdot(amap[n * heads + h], start)
            dev[h, :, :DH] = moved[:, :DH]
            dev[h, :, DH:] = moved[:, DH:] + badd[n * heads + h]
        return 0

    lax.fori_loop(0, groups, chain, 0)
    last[...] = dev[:, :, DH:]

    def outs(i, _):
        for n, h in [(2 * i + j, h) for j in range(2) for h in range(heads)]:
            rows = pl.ds(pl.multiple_of(n * GROUP, GROUP), GROUP)
            lanes = slice(h * DH, (h + 1) * DH)
            q = qkv[rows, lanes]
            both = fdot(jnp.concatenate([q, wmix[rows, lanes]], axis=0), zst[n * heads + h])
            lower = jnp.concatenate([-both[GROUP:, :DH], umix[rows, lanes] - both[GROUP:, DH:]], axis=1)
            made = both[:GROUP] + fdot(score[n * heads + h], lower)
            mout[rows, lanes] = made[:, :DH]
            oloc[rows, lanes] = made[:, DH:]
        return 0

    lax.fori_loop(0, groups // 2, outs, 0)


def fold_hops(hops, h):
    state = hops[-1][h]
    for hop in hops[-2::-1]:
        state = hop[h, :, DH:] + fdot(hop[h, :, :DH], state)
    return state


def out_kernel(hop_count, tp, *refs):
    hops, refs = refs[:hop_count], refs[hop_count:]
    mout, oloc, gate, nh, wo, heads_out, att, send, keep, entry = refs
    heads = gate.shape[1] // DH
    states = [fold_hops(hops, h) for h in range(heads)]
    for h in range(heads):
        entry[h] = states[h]
    share = mout.shape[0] // 4
    for rel in range(4):
        rows = rows_of(tp[0] ^ rel, share)
        lows = []
        for h in range(heads):
            lanes = slice(h * DH, (h + 1) * DH)
            o = oloc[rows, lanes] + fdot(mout[rows, lanes], states[h])
            heads_out[rows, lanes] = o
            factor = lax.rsqrt(jnp.mean(o * o, axis=-1, keepdims=True) + head_epsilon)
            g = gate[rows, lanes]
            lows.append((o * factor * wide_gain(nh) * (g * jax.nn.sigmoid(g))).astype(bf16))
        low = jnp.concatenate(lows, axis=1)
        att[rows] = low
        part = dot(low, wo[...])
        if rel % 2:
            send[rel // 2] = part.astype(bf16)
        else:
            keep[rel // 2] = part


def states_kernel(entry, zst, qkv, wmix, umix, score, states, vnew, qeff):
    groups = qkv.shape[0] // GROUP
    heads = wmix.shape[1] // DH

    def one(i, _):
        for n, h in [(2 * i + j, h) for j in range(2) for h in range(heads)]:
            rows = pl.ds(pl.multiple_of(n * GROUP, GROUP), GROUP)
            lanes = slice(h * DH, (h + 1) * DH)
            at = n * heads + h
            s = zst[at, :, DH:] + fdot(zst[at, :, :DH], entry[h])
            states[at] = s
            w = wmix[rows, lanes]
            vnew[rows, lanes] = umix[rows, lanes] - fdot(w, s)
            qeff[rows, lanes] = qkv[rows, lanes] - fdot(score[at], w)
        return 0

    lax.fori_loop(0, groups // 2, one, 0)


def mid_kernel(x, kept, got, gain, residual, second):
    total = x[...].astype(f32) + kept[...] + got[...].astype(f32)
    residual[...] = total
    second[...] = rms_rows(total, wide_gain(gain)).astype(bf16)


def ffn_kernel(tp, s0, s1, s2, s3, grad_down, wg, wu, wd, second, inner, dgate, dup, down_send, down_keep, send, keep):
    share = s0.shape[0]
    for half, pair in enumerate(((s0, s1), (s2, s3))):
        sec = jnp.concatenate([pair[0][...], pair[1][...]], axis=0)
        blocks = [rows_of(tp[0] ^ (2 * half + j), share) for j in range(2)]
        gd = jnp.concatenate([grad_down[b] for b in blocks], axis=0)
        gv = dot(sec, wg[...], 1, 1)
        uv = dot(sec, wu[...], 1, 1)
        sig = jax.nn.sigmoid(gv)
        act = gv * sig
        inn = (act * uv).astype(bf16)
        gi = dot(gd, wd[...], 1, 1)
        dg = (gi * uv * (sig * (1.0 + gv * (1.0 - sig)))).astype(bf16)
        du = (gi * act).astype(bf16)
        for j, b in enumerate(blocks):
            part = slice(j * share, (j + 1) * share)
            second[b] = sec[part]
            inner[b] = inn[part]
            dgate[b] = dg[part]
            dup[b] = du[part]
        grad = dot(dg, wg[...]) + dot(du, wu[...])
        keep[half] = grad[:share]
        send[half] = grad[share:].astype(bf16)
        down = dot(inn, wd[...])
        down_keep[half] = down[:share]
        down_send[half] = down[share:].astype(bf16)


def turn_kernel(kept, got, residual, gain, grad_y, grad_residual, branch, gain_part):
    gs = kept[...] + got[...].astype(f32)
    v = residual[...]
    g = wide_gain(gain)
    r = lax.rsqrt(jnp.mean(v * v, axis=-1, keepdims=True) + row_epsilon)
    gain_part[...] = jnp.sum(gs * v * r, axis=0, keepdims=True)
    e = gs * g
    back = r * e - v * (r * r * r) * jnp.mean(e * v, axis=-1, keepdims=True)
    total = grad_y[...].astype(f32) + back
    grad_residual[...] = total
    branch[...] = total.astype(bf16)


def flow_kernel(tp, meta, b0, b1, b2, b3, wo, heads_out, gate, nh, qeff, amap, branch, dgate, dout, rst, dev, last, nh_part, flows):
    share = b0.shape[0]
    heads = gate.shape[1] // DH
    groups = gate.shape[0] // GROUP
    gains = jnp.zeros((1, DH), f32)
    for half, pair in enumerate(((b0, b1), (b2, b3))):
        both = jnp.concatenate([pair[0][...], pair[1][...]], axis=0)
        ga = dot(both, wo[...], 1, 1)
        for j in range(2):
            rows = rows_of(tp[0] ^ (2 * half + j), share)
            branch[rows] = pair[j][...]
            for h in range(heads):
                lanes = slice(h * DH, (h + 1) * DH)
                gz = ga[j * share : (j + 1) * share, lanes]
                o = heads_out[rows, lanes]
                g = gate[rows, lanes]
                gain = wide_gain(nh)
                r = lax.rsqrt(jnp.mean(o * o, axis=-1, keepdims=True) + head_epsilon)
                sig = jax.nn.sigmoid(g)
                act = g * sig
                e = gz * gain * act
                base = gz * o * r
                gains = gains + jnp.sum(base * act, axis=0, keepdims=True)
                dgate[rows, lanes] = (base * gain * (sig * (1.0 + g * (1.0 - sig)))).astype(bf16)
                dout[rows, lanes] = r * e - o * (r * r * r) * jnp.mean(e * o, axis=-1, keepdims=True)
    nh_part[...] = gains

    def local(i, _):
        for n, h in [(2 * i + j, h) for j in range(2) for h in range(heads)]:
            rows = pl.ds(pl.multiple_of(n * GROUP, GROUP), GROUP)
            lanes = slice(h * DH, (h + 1) * DH)
            flows[n * heads + h] = fdot(qeff[rows, lanes], dout[rows, lanes], 0, 0)
        return 0

    lax.fori_loop(0, groups // 2, local, 0)
    eye = (iota((DH, DH), 0) == iota((DH, DH), 1)).astype(f32)
    for h in range(heads):
        dev[h, :, :DH] = eye
        dev[h, :, DH:] = jnp.zeros((DH, DH), f32)

    def chain(i, _):
        n = groups - 1 - i
        keep = 1.0 - meta[0, n].astype(f32)
        for h in range(heads):
            at = n * heads + h
            later = dev[h]
            rst[at] = later
            moved = fdot(amap[at], later, 0, 0)
            dev[h, :, :DH] = moved[:, :DH] * keep
            dev[h, :, DH:] = (moved[:, DH:] + flows[at]) * keep
        return 0

    lax.fori_loop(0, groups, chain, 0)
    last[...] = dev[:, :, DH:]


def side_kernel(qkv, dout, vnew, states, score, ndo, dq, dk):
    heads = dout.shape[1] // DH
    groups = dout.shape[0] // GROUP
    lower = iota((GROUP, GROUP), 0) >= iota((GROUP, GROUP), 1)

    def one(i, _):
        for n, h in [(2 * i + j, h) for j in range(2) for h in range(heads)]:
            rows = pl.ds(pl.multiple_of(n * GROUP, GROUP), GROUP)
            lanes = slice(h * DH, (h + 1) * DH)
            at = n * heads + h
            q = qkv[rows, lanes]
            k = qkv[rows, (heads + h) * DH : (heads + h + 1) * DH]
            do = dout[rows, lanes]
            ndo[rows, lanes] = fdot(score[at], do, 0, 0)
            dn = jnp.where(lower, fdot(do, vnew[rows, lanes], 1, 1), 0.0)
            dq[rows, lanes] = fdot(do, states[at], 1, 1) + fdot(dn, k)
            dk[rows, lanes] = fdot(dn, q, 0, 0)
        return 0

    lax.fori_loop(0, groups // 2, one, 0)


def unit_back(a, grad):
    r = lax.rsqrt(jnp.sum(a * a, axis=-1, keepdims=True) + unit_epsilon)
    return r * grad - a * (r * r * r) * jnp.sum(a * grad, axis=-1, keepdims=True)


def back_kernel(hop_count, meta, *refs):
    hops, refs = refs[:hop_count], refs[hop_count:]
    rst, qkv, conv, ext, cq, ck, cv, beta, inv, states, vnew, ndo, dq, dk1, gp, last, halo, dbeta, dtaps, dc = refs
    taps = tap_table(cq, ck, cv)
    heads = ndo.shape[1] // DH
    groups = ndo.shape[0] // GROUP
    total = ndo.shape[0]
    exits = [fold_hops(hops, h) for h in range(heads)]
    strict = iota((GROUP, GROUP), 0) > iota((GROUP, GROUP), 1)
    lane = iota((GROUP, LANES), 1)
    dc[total:] = jnp.zeros((8, dc.shape[1]), f32)

    def one(i, _):
        for j in range(2):
            n = 2 * i + j
            rows = pl.ds(pl.multiple_of(n * GROUP, GROUP), GROUP)
            raws = jnp.zeros((GROUP, LANES), f32)
            for h in range(heads):
                at = n * heads + h
                lanes = [slice((p * heads + h) * DH, (p * heads + h + 1) * DH) for p in range(3)]
                k = qkv[rows, lanes[1]]
                v = qkv[rows, lanes[2]]
                b, sig, live = beta_col(beta, meta, n, h)
                ds = rst[at, :, DH:] + fdot(rst[at, :, :DH], exits[h])
                dvn = ndo[rows, lanes[0]] + fdot(k, ds)
                d = fdot(inv[at], dvn, 0, 0)
                vn = vnew[rows, lanes[0]]
                dstate = fdot(d, states[at], 1, 1)
                vds = fdot(vn, ds, 1, 1)
                da = jnp.where(strict, -fdot(d, vn, 1, 1), 0.0)
                dak = fdot(da, k)
                datk = fdot(da, k * b, 0, 0)
                dk = dk1[rows, lanes[0]] + vds + b * (dak - dstate) + datk
                db = jnp.sum(d * v + (dak - dstate) * k, axis=-1, keepdims=True)
                db = jnp.where(live, db * sig * (1.0 - sig), 0.0)
                raws = jnp.where(lane == h, db, raws)
                grads = (dq[rows, lanes[0]], dk, d * b)
                for p in range(3):
                    c = conv[rows, lanes[p]]
                    s = jax.nn.sigmoid(c)
                    grad = unit_back(c * s, grads[p]) if p < 2 else grads[p]
                    dc[rows, lanes[p]] = grad * (s * (1.0 + c * (1.0 - s)))
            dbeta[rows] = raws.astype(bf16)
        return 0

    lax.fori_loop(0, groups // 2, one, 0)
    row = iota((GROUP, 1), 0)
    dtaps[...] = jnp.zeros(dtaps.shape, f32)

    def masked(win, d, here, after):
        front = jnp.where(iota((GROUP, 1), 0) < here * d, 0.0, win[:GROUP])
        if after is None:
            return front
        back = jnp.where(iota((8, 1), 0) < after * d, 0.0, win[GROUP:])
        return jnp.concatenate([front, back], axis=0)

    def taps_back(n, _):
        base = pl.multiple_of(n * GROUP, GROUP)
        here = meta[0, n]
        after = meta[0, jnp.minimum(n + 1, groups - 1)]
        for c in range(3 * heads):
            lanes = slice(c * DH, (c + 1) * DH)
            win = dc[pl.ds(base, GROUP + 8), lanes]
            old = ext[pl.ds(pl.multiple_of(base + TAIL - 8, 8), GROUP + 8), lanes]
            acc = taps(KW - 1, c) * win[:GROUP]
            dtaps[KW - 1 : KW, lanes] += jnp.sum(win[:GROUP] * old[8:], axis=0, keepdims=True)
            for d in range(1, KW):
                part = masked(win, d, here, after)
                j = KW - 1 - d
                acc = acc + taps(j, c) * part[d : d + GROUP]
                dtaps[j : j + 1, lanes] += jnp.sum(
                    part[:GROUP] * old[8 - d : 8 - d + GROUP], axis=0, keepdims=True
                )
            gp[pl.ds(base, GROUP), lanes] = acc.astype(bf16)

            @pl.when(n == groups - 1)
            def _():
                last[:, lanes] = acc[GROUP - TAIL :]

        return 0

    lax.fori_loop(0, groups, taps_back, 0)
    zero = jnp.zeros((8, DH), f32)
    for c in range(3 * heads):
        lanes = slice(c * DH, (c + 1) * DH)
        win = dc[0:8, lanes]
        acc = zero
        for d in range(1, KW):
            part = jnp.where(iota((8, 1), 0) < meta[0, 0] * d, 0.0, win)
            j = KW - 1 - d
            acc = acc + taps(j, c) * jnp.concatenate([zero, part], axis=0)[d : d + 8]
        halo[:, lanes] = acc


def hid_kernel(tp, gp_in, last, incoming, dgate, dbeta, wq, wk, wv, wg, wb, gp, send, keep):
    total = gp.shape[0]
    width = wq.shape[1]
    gp[: total - TAIL] = gp_in[: total - TAIL]
    fixed = jnp.concatenate([last[: TAIL - 8], last[TAIL - 8 :] + incoming[...]], axis=0)
    gp[total - TAIL :] = fixed.astype(bf16)
    share = total // 4
    for half in range(2):
        blocks = [rows_of(tp[0] ^ (2 * half + j), share) for j in range(2)]
        cat = lambda ref: jnp.concatenate([ref[b] for b in blocks], axis=0)
        grads = cat(gp)
        acc = dot(cat(dgate), wg[...], 1, 1)
        small = cat(dbeta).astype(f32)
        for h in range(wb.shape[0]):
            acc = acc + small[:, h : h + 1] * wb[h : h + 1].astype(f32)
        for i, w in enumerate((wq, wk, wv)):
            acc = acc + dot(grads[:, i * width : (i + 1) * width], w[...], 1, 1)
        keep[half] = acc[:share]
        send[half] = acc[share:].astype(bf16)


def in_kernel(kept, got, x, gain, grad_residual, grad_in, gain_part):
    gh = kept[...] + got[...].astype(f32)
    v = x[...].astype(f32)
    g = wide_gain(gain)
    r = lax.rsqrt(jnp.mean(v * v, axis=-1, keepdims=True) + row_epsilon)
    gain_part[...] = jnp.sum(gh * v * r, axis=0, keepdims=True)
    e = gh * g
    back = r * e - v * (r * r * r) * jnp.mean(e * v, axis=-1, keepdims=True)
    grad_in[...] = (grad_residual[...] + back).astype(bf16)


def outblock_kernel(tp, meta, kept, got, residual, out):
    total = residual[...] + kept[...] + got[...].astype(f32)
    live = live_mask(meta, tp[0], total.shape[0])
    out[...] = jnp.where(live, total, 0.0).astype(bf16)


def place_kernel(tp, a0, a1, a2, a3, out):
    for rel, part in enumerate((a0, a1, a2, a3)):
        out[rows_of(tp[0] ^ rel, part.shape[0])] = part[...].astype(out.dtype)


def swap(value, bit, axis="tp"):
    count = lax.axis_size(axis)
    return lax.ppermute(value, axis, [(i, i ^ bit) for i in range(count)])


def add_kernel(keep, got, kept, send):
    half = kept.shape[0]
    kept[...] = keep[:half] + got[:half].astype(f32)
    send[...] = (keep[half:] + got[half:].astype(f32)).astype(bf16)


def last_kernel(keep, got, own):
    own[...] = (keep[...] + got[...].astype(f32)).astype(bf16)


def pack_kernel(a, b, out):
    half = a.shape[0]
    out[:half] = a[...]
    out[half:] = b[...]


def fold(keep, got, name):
    half = (keep.shape[0] // 2, *keep.shape[1:])
    return run(add_kernel, name, [(half, f32), (half, bf16)], [keep, got])


def scatter_sum(send, keep):
    kept, send = fold(keep, swap(send, 1), "fold_tp")
    return kept[0], swap(send, 2)[0]


def spread(place, keep, send, acc, base, rows):
    blocks = 2 * keep.shape[0]
    width = blocks.bit_length() - 1
    size = rows // blocks
    for m in range(blocks):
        at = sum(((m >> (i + 1)) & 1) << (width - 2 - i) for i in range(width - 1))
        block = acc[pl.ds(pl.multiple_of((m ^ place) * size, 8), size)]
        if m & 1:
            send[at, base : base + size] = block.astype(bf16)
        else:
            keep[at, base : base + size] = block


def grads_kernel(count, place, *refs):
    pairs, (keep, send, acc) = refs[: 2 * count], refs[2 * count :]
    base = 0
    for i in range(count):
        left, right = pairs[2 * i : 2 * i + 2]
        rows = left.shape[1]
        acc[:rows] = dot(left[...], right[...], 0, 0)
        spread(place[0], keep, send, acc, base, rows)
        base += rows // (2 * keep.shape[0])


def hidden_grads_kernel(place, hidden, gp, dgate, keep, send, acc):
    wide = gp.shape[1]
    rows = hidden.shape[1]
    acc[:, :wide] = dot(hidden[...], gp[...], 0, 0)
    acc[:, wide:] = dot(hidden[...], dgate[...], 0, 0)
    spread(place[0], keep, send, acc, 0, rows)


def grads(place, pairs, blocks, name):
    size = sum(p[0].shape[1] for p in pairs) // blocks
    most = max(p[0].shape[1] for p in pairs)
    cols = pairs[0][1].shape[1]
    half = (blocks // 2, size, cols)
    args = [a for p in pairs for a in p]
    return run(
        lambda *r: grads_kernel(len(pairs), *r),
        name,
        [(half, f32), (half, bf16)],
        [place, *args],
        smem=(0,),
        scratch=[pltpu.VMEM((most, cols), f32)],
        flops=2 * pairs[0][0].shape[0] * size * blocks * cols,
        vmem=16,
    )


def sum_seq(keep, send, blocks, tag):
    count = lax.axis_size("seq")
    step = 1
    while step < blocks // 2:
        keep, send = fold(keep, swap(send, step, "seq"), tag + "_fold")
        step *= 2
    got = swap(send, step, "seq")
    (own,) = run(last_kernel, tag + "_last", [(keep.shape, bf16)], [keep, got])
    more = blocks
    while more < count:
        own = (own.astype(f32) + swap(own, more, "seq").astype(f32)).astype(bf16)
        more *= 2
    while step > 1:
        twice = (2 * own.shape[0], *own.shape[1:])
        (own,) = run(pack_kernel, tag + "_pack", [(twice, bf16)], [own, swap(own, step, "seq")])
        step //= 2
    return own, swap(own, 1, "seq")


def settle(place, near, far, outs):
    blocks = 2 * near.shape[0]
    width = blocks.bit_length() - 1
    for m in range(blocks):
        at = sum(((m >> (i + 1)) & 1) << i for i in range(width - 1))
        at = sum(((at >> i) & 1) << (width - 2 - i) for i in range(width - 1))
        source = far if m & 1 else near
        row = 0
        for out, size, lanes in outs:
            out[pl.ds(pl.multiple_of((m ^ place) * size, 8), size)] = source[
                at, row : row + size, lanes
            ].astype(f32)
            row = row + size if lanes == slice(None) else row


def settle_kernel(place, near, far, *outs):
    sizes = [out.shape[0] // (2 * near.shape[0]) for out in outs]
    settle(place[0], near, far, [(o, n, slice(None)) for o, n in zip(outs, sizes)])


def settle_cols_kernel(place, near, far, *outs):
    size = near.shape[1]
    wide = outs[0].shape[1]
    settle(
        place[0],
        near,
        far,
        [(o, size, slice(i * wide, (i + 1) * wide)) for i, o in enumerate(outs)],
    )


def gather_rel(own):
    near = swap(own, 1)
    far = swap(own, 2)
    return own, near, far, swap(far, 1)


def shift(value, steps):
    count = lax.axis_size("seq")
    pairs = [(i, i + steps) for i in range(count) if 0 <= i + steps < count]
    return lax.ppermute(value, "seq", pairs)


def hops_of(dev, last, sign, reach):
    return [shift(dev, sign * k) for k in range(1, reach)] + [shift(last, sign * reach)]


def small_kernel(dtaps, dbeta, hidden, in_part, mid_part, head_part, taps_out, gains_out):
    wide = dtaps.shape[1]
    taps_out[...] = jnp.zeros(taps_out.shape, f32)
    taps_out[0:KW, :wide] = dtaps[...]
    product = dot(dbeta[...], hidden[...], 0, 0)
    taps_out[KW : KW + 4] = product[:4]
    gains_out[...] = jnp.zeros(gains_out.shape, f32)
    gains_out[0:1] = in_part[...]
    gains_out[1:2] = mid_part[...]
    gains_out[2:3, : head_part.shape[1]] = head_part[...]


def plus_kernel(a, b, out):
    out[...] = a[...] + b[...]


def plus(a, b):
    return run(plus_kernel, "plus", [(a.shape, f32)], [a, b])[0]


def shards(
    layer_input,
    seq_groups,
    seq_pads,
    norm_in,
    w_query,
    w_key,
    w_value,
    conv_query,
    conv_key,
    conv_value,
    w_beta,
    w_gate_out,
    norm_head,
    w_out,
    norm_mid,
    w_gate,
    w_up,
    w_down,
    cotangent,
):
    total, model = layer_input.shape
    width = w_query.shape[1]
    heads = width // DH
    groups = total // GROUP
    share = total // 4
    ffw = w_gate.shape[1]
    seq_count = lax.axis_size("seq")
    reach = max(1, seq_count // 4)
    tp_rank = lax.axis_index("tp")
    tp = tp_rank.astype(jnp.int32).reshape(1)
    blocks = min(8, seq_count)
    place = (lax.axis_index("seq") % blocks).astype(jnp.int32).reshape(1)
    first = (lax.axis_index("seq") * groups).astype(jnp.int32).reshape(1)
    taps = (conv_query, conv_key, conv_value)
    wb = w_beta.T
    tail = shift(layer_input[total - TAIL :], 1)
    chains = groups * heads
    wide = (total, width)
    mats = 2 * total * model
    weight = pltpu.VMEM((model, width), bf16)
    rows = pltpu.VMEM((total, model), bf16)

    hidden, proj, gate_raw, beta_raw, grad_down, x_own, gd_own, meta = run(
        pre_kernel,
        "pre",
        [
            ((total, model), bf16),
            ((total, 3 * width), f32),
            (wide, f32),
            ((total, heads), f32),
            ((total, model), bf16),
            ((share, model), bf16),
            ((share, model), bf16),
            ((2, groups), jnp.int32),
        ],
        [first, tp, seq_groups, seq_pads, layer_input, cotangent, norm_in, w_query, w_key, w_value, w_gate_out, wb],
        smem=(0, 1, 2, 3),
        smem_out=(7,),
        hbm=(4, 5, 7, 8, 9, 10),
        scratch=[rows, rows, weight, weight, weight, weight, pltpu.SemaphoreType.DMA((6,))],
        flops=mats * 4 * width,
        vmem=12,
    )
    ext, conv, qkv, wmix, umix, inv, score, amap, zst, dev, last, mout, oloc = run(
        mix_kernel,
        "mix",
        [
            ((total + TAIL, 3 * width), f32),
            ((total, 3 * width), f32),
            ((total, 3 * width), f32),
            (wide, f32),
            (wide, f32),
            ((chains, GROUP, GROUP), f32),
            ((chains, GROUP, GROUP), f32),
            ((chains, DH, DH), f32),
            ((chains, DH, 2 * DH), f32),
            ((heads, DH, 2 * DH), f32),
            ((heads, DH, DH), f32),
            (wide, f32),
            (wide, f32),
        ],
        [meta, proj, tail, norm_in, w_query, w_key, w_value, *taps, beta_raw],
        smem=(0,),
        hbm=(4, 5, 6),
        scratch=[pltpu.VMEM((chains, DH, DH), f32), weight, weight, weight, pltpu.SemaphoreType.DMA((3,))],
        flops=6 * mats * width,
    )
    hops = hops_of(dev, last, 1, reach)
    heads_out, attended, send, keep, entry = run(
        lambda *r: out_kernel(reach, *r),
        "out",
        [(wide, f32), (wide, bf16), ((2, share, model), bf16), ((2, share, model), f32), ((heads, DH, DH), f32)],
        [tp, *hops, mout, oloc, gate_raw, norm_head, w_out],
        smem=(0,),
        flops=mats * width,
    )
    kept, got = scatter_sum(send, keep)
    states, vnew, qeff = run(
        states_kernel,
        "states",
        [((chains, DH, DH), f32), (wide, f32), (wide, f32)],
        [entry, zst, qkv, wmix, umix, score],
        flops=mats * width,
    )
    x_own, states = lax.optimization_barrier((x_own, states))
    residual, second_own = run(
        mid_kernel,
        "mid",
        [((share, model), f32), ((share, model), bf16)],
        [x_own, kept, got, norm_mid],
    )
    second, inner, dgate, dup, down_send, down_keep, send, keep = run(
        ffn_kernel,
        "ffn",
        [
            ((total, model), bf16),
            ((total, ffw), bf16),
            ((total, ffw), bf16),
            ((total, ffw), bf16),
            ((2, share, model), bf16),
            ((2, share, model), f32),
            ((2, share, model), bf16),
            ((2, share, model), f32),
        ],
        [tp, *gather_rel(second_own), grad_down, w_gate.T, w_up.T, w_down],
        smem=(0,),
        flops=6 * mats * ffw,
        vmem=16,
    )
    keep_a, send_a = grads(place, ((inner, grad_down), (dgate, second)), blocks, "grads_a")
    kept, got = scatter_sum(send, keep)
    residual, send_a = lax.optimization_barrier((residual, send_a))
    near_a, far_a = sum_seq(keep_a, send_a, blocks, "a")
    grad_residual, branch_own, mid_part = run(
        turn_kernel,
        "turn",
        [((share, model), f32), ((share, model), bf16), ((1, model), f32)],
        [kept, got, residual, norm_mid, gd_own],
    )
    branch, dgate_raw, dout, rst, dev, last, head_part = run(
        flow_kernel,
        "flow",
        [
            ((total, model), bf16),
            (wide, bf16),
            (wide, f32),
            ((chains, DH, 2 * DH), f32),
            ((heads, DH, 2 * DH), f32),
            ((heads, DH, DH), f32),
            ((1, DH), f32),
        ],
        [tp, meta, *gather_rel(branch_own), w_out, heads_out, gate_raw, norm_head, qeff, amap],
        smem=(0, 1),
        scratch=[pltpu.VMEM((chains, DH, DH), f32)],
        flops=3 * mats * width,
    )
    hops = hops_of(dev, last, -1, reach)
    ndo, dq, dk = run(
        side_kernel,
        "side",
        [(wide, f32)] * 3,
        [qkv, dout, vnew, states, score],
        flops=mats * width,
    )
    keep_b, send_b = grads(place, ((dup, second), (attended, branch)), blocks, "grads_b")
    ndo, send_b = lax.optimization_barrier((ndo, send_b))
    near_b, far_b = sum_seq(keep_b, send_b, blocks, "b")
    gp, last, halo, dbeta, dtaps = run(
        lambda *r: back_kernel(reach, *r),
        "back",
        [
            ((total, 3 * width), bf16),
            ((TAIL, 3 * width), f32),
            ((8, 3 * width), f32),
            ((total, LANES), bf16),
            ((KW, 3 * width), f32),
        ],
        [meta, *hops, rst, qkv, conv, ext, *taps, beta_raw, inv, states, vnew, ndo, dq, dk],
        smem=(0,),
        scratch=[pltpu.VMEM((total + 8, 3 * width), f32)],
        flops=3 * mats * width,
    )
    incoming = shift(halo, -1)
    gp, send, keep = run(
        hid_kernel,
        "hid",
        [((total, 3 * width), bf16), ((2, share, model), bf16), ((2, share, model), f32)],
        [tp, gp, last, incoming, dgate_raw, dbeta, w_query, w_key, w_value, w_gate_out, wb],
        smem=(0,),
        flops=mats * 4 * width,
        vmem=12,
    )
    half = (blocks // 2, model // blocks, 4 * width)
    keep_c, send_c = run(
        hidden_grads_kernel,
        "grads_c",
        [(half, f32), (half, bf16)],
        [place, hidden, gp, dgate_raw],
        smem=(0,),
        scratch=[pltpu.VMEM((model, 4 * width), f32)],
        flops=mats * 4 * width,
        vmem=16,
    )
    near_c, far_c = sum_seq(keep_c, send_c, blocks, "c")
    kept, got = scatter_sum(send, keep)
    grad_in_own, in_part = run(
        in_kernel,
        "inp",
        [((share, model), bf16), ((1, model), f32)],
        [kept, got, x_own, norm_in, grad_residual],
    )
    (grad_input,) = run(
        place_kernel,
        "place_in",
        [((total, model), f32)],
        [tp, *gather_rel(grad_in_own)],
        smem=(0,),
    )
    kept, got = scatter_sum(down_send, down_keep)
    (out_own,) = run(
        outblock_kernel,
        "outblk",
        [((share, model), bf16)],
        [tp, meta, kept, got, residual],
        smem=(0, 1),
    )
    (block_out,) = run(
        place_kernel,
        "place_out",
        [((total, model), bf16)],
        [tp, *gather_rel(out_own)],
        smem=(0,),
    )
    row8 = ((8, model), f32)
    small, gains = run(
        small_kernel, "small", [row8, row8], [dtaps, dbeta, hidden, in_part, mid_part, head_part]
    )
    for axis in ("tp", "seq"):
        step = 1
        while step < lax.axis_size(axis):
            gains = plus(gains, swap(gains, step, axis))
            if axis == "seq":
                small = plus(small, swap(small, step, axis))
            step *= 2
    grad_down_w, grad_gate_w = run(
        settle_kernel,
        "settle_a",
        [((ffw, model), f32), ((ffw, model), f32)],
        [place, near_a, far_a],
        smem=(0,),
    )
    grad_up_w, grad_out_w = run(
        settle_kernel,
        "settle_b",
        [((ffw, model), f32), ((width, model), f32)],
        [place, near_b, far_b],
        smem=(0,),
    )
    hidden_sums = run(
        settle_cols_kernel,
        "settle_c",
        [((model, width), f32)] * 4,
        [place, near_c, far_c],
        smem=(0,),
    )
    cut = model // 4
    head_cut = DH // 4
    gain_of = lambda row, size: lax.dynamic_slice(gains, (row, tp_rank * size), (1, size)).reshape(size)
    tap_of = lambda i: small[:KW, i * width : (i + 1) * width]
    return (
        block_out,
        grad_input,
        gain_of(0, cut),
        hidden_sums[0],
        hidden_sums[1],
        hidden_sums[2],
        tap_of(0),
        tap_of(1),
        tap_of(2),
        small[KW : KW + heads].T,
        hidden_sums[3],
        gain_of(2, head_cut),
        grad_out_w,
        gain_of(1, cut),
        grad_gate_w.T,
        grad_up_w.T,
        grad_down_w,
    )


def solution(mesh):
    rows = P("seq", None)
    cols = P(None, "tp")
    return jax.shard_map(
        shards,
        mesh=mesh,
        in_specs=(rows, P(), P(), P(), cols, cols, cols, cols, cols, cols, cols, cols, P(), P("tp", None), P(), cols, cols, P("tp", None), rows),
        out_specs=(rows, rows, P("tp"), cols, cols, cols, cols, cols, cols, cols, cols, P("tp"), P("tp", None), P("tp"), cols, cols, P("tp", None)),
        check_vma=False,
    )
```

```python
import jax
import jax.numpy as jnp
from jax import lax
from jax.experimental import pallas as pl
from jax.experimental.pallas import tpu as pltpu
from jax.sharding import PartitionSpec as P

DH = 128
KW = 4
GROUP = 64
TAIL = 16
LANES = 128

row_epsilon = 1e-06
head_epsilon = 1e-05
unit_epsilon = 1e-06
f32 = jnp.float32
bf16 = jnp.bfloat16


def dot(a, b, ca=1, cb=0):
    return lax.dot_general(a, b, (((ca,), (cb,)), ((), ())), preferred_element_type=f32)


def halves(a):
    high = a.astype(bf16)
    return high, (a - high.astype(f32)).astype(bf16)


def fdot(a, b, ca=1, cb=0):
    ah, al = halves(a)
    bh, bl = halves(b)
    return dot(
        jnp.concatenate([ah, al, ah], axis=ca), jnp.concatenate([bh, bh, bl], axis=cb), ca, cb
    )


def iota(shape, axis):
    return lax.broadcasted_iota(jnp.int32, shape, axis)


def rows_of(block, size):
    return pl.ds(pl.multiple_of(block * size, size), size)


class Order:
    def __init__(self):
        self.last = None

    def run(self, kernel, name, outs, args, smem=(), smem_out=(), hbm=(), hbm_out=(), pin=(), scratch=(), flops=0, vmem=8):
        shapes = [jax.ShapeDtypeStruct(s, d) for s, d in outs]
        total = sum(a.size * a.dtype.itemsize for a in args)
        total += sum(s.size * s.dtype.itemsize for s in shapes)
        args = list(args)
        if self.last is not None:
            at = next(i for i in range(len(args)) if i not in smem and i not in pin)
            args[at], _ = lax.optimization_barrier((args[at], self.last))
        for i in pin:
            args[i] = pltpu.with_memory_space_constraint(args[i], pltpu.HBM)
        space = lambda i, low, far: pltpu.SMEM if i in low else pltpu.HBM if i in far else pltpu.VMEM
        made = pl.pallas_call(
            kernel,
            name=name,
            out_shape=shapes,
            in_specs=[pl.BlockSpec(memory_space=space(i, smem, hbm)) for i in range(len(args))],
            out_specs=[
                pl.BlockSpec(memory_space=space(i, smem_out, hbm_out)) for i in range(len(outs))
            ],
            scratch_shapes=list(scratch),
            compiler_params=pltpu.CompilerParams(vmem_limit_bytes=vmem << 20),
            cost_estimate=pl.CostEstimate(flops=flops, bytes_accessed=total, transcendentals=0),
        )(*args)
        self.last = next(o for i, o in enumerate(made) if i not in smem_out and i not in hbm_out)
        return made


def wide_gain(ref):
    return ref[...].astype(f32).reshape(1, ref.shape[0])


def live_mask(meta, block, size):
    parts = size // GROUP
    row = iota((size, 1), 0)
    limit = jnp.full((size, 1), 0, jnp.int32) + meta[1, block * parts]
    for part in range(1, parts):
        limit = jnp.where(row >= part * GROUP, meta[1, block * parts + part] + part * GROUP, limit)
    return row < limit


def rms_rows(values, gain):
    factor = lax.rsqrt(jnp.mean(values * values, axis=-1, keepdims=True) + row_epsilon)
    return values * factor * gain


def beta_col(beta, meta, n, h):
    raw = beta[pl.ds(pl.multiple_of(n * GROUP, GROUP), GROUP), h : h + 1]
    sig = jax.nn.sigmoid(raw)
    live = iota((GROUP, 1), 0) < meta[1, n]
    return jnp.where(live, sig, 0.0), sig, live


def unit(rows):
    return rows * lax.rsqrt(jnp.sum(rows * rows, axis=-1, keepdims=True) + unit_epsilon)


def tri_inverse(systems):
    size = systems[0].shape[0]
    eye = (iota((size, size), 0) == iota((size, size), 1)).astype(f32)
    blocks = [[eye[r : r + 8] for r in range(0, size, 8)] for _ in systems]
    lower = [[system[r : r + 8] for r in range(0, size, 8)] for system in systems]
    for j in range(size - 1):
        for low, part in zip(lower, blocks):
            line = part[j // 8][j % 8 : j % 8 + 1]
            for r in range((j + 1) // 8, size // 8):
                part[r] = part[r] - low[r][:, j : j + 1] * line
    return [jnp.concatenate(part, axis=0) for part in blocks]


def tap_table(*tables):
    values = [table[...].astype(f32) for table in tables]
    parts = values[0].shape[1] // DH
    return lambda j, c: values[c // parts][j : j + 1, (c % parts) * DH : (c % parts + 1) * DH]


def front_kernel(first, tp, seq_groups, seq_pads, xh, coth, gain, wqh, wkh, wvh, wgh, wb, tail, cq, ck, cv, gate, beta, meta, qkv, wmix, umix, score, zst, dev, last, mout, oloc, hidden_h, gd_h, x_own, gd_own, ext_h, conv_h, inv_h, amap_h, x, cot, wq, wk, wv, wg, hidden, gd, ext, conv, inv, amap, badd, sems, out_sems):
    loads = [
        pltpu.make_async_copy(src, dst, sems.at[i])
        for i, (src, dst) in enumerate(
            ((xh, x), (wqh, wq), (wkh, wk), (wvh, wv), (wgh, wg), (coth, cot))
        )
    ]
    for load in loads:
        load.start()
    groups = x.shape[0] // GROUP
    for n in range(groups):
        meta[0, n] = 0
        meta[1, n] = 0

    def one(s, start):
        count = seq_groups[s]
        length = count * GROUP - seq_pads[s]
        for n in range(groups):
            gid = first[0] + n
            inside = (gid >= start) & (gid < start + count)
            here = jnp.clip(length - (gid - start) * GROUP, 0, GROUP)
            meta[0, n] = jnp.where(gid == start, 1, meta[0, n])
            meta[1, n] = jnp.where(inside, here, meta[1, n])
        return start + count

    lax.fori_loop(0, seq_groups.shape[0], one, jnp.int32(0))
    width = wq.shape[1]
    heads = width // DH
    tile = 256
    share = x_own.shape[0]
    scale = wide_gain(gain)
    own = rows_of(tp[0], share)
    stores = []

    def store(src, dst):
        copy = pltpu.make_async_copy(src, dst, out_sems.at[len(stores)])
        copy.start()
        stores.append(copy)

    loads[0].wait()
    store(x.at[own], x_own)
    tiles = [slice(t * tile, (t + 1) * tile) for t in range(x.shape[0] // tile)]
    for rows in tiles:
        hidden[rows] = rms_rows(x[rows].astype(f32), scale).astype(bf16)
    store(hidden, hidden_h)
    low = rms_rows(tail[...].astype(f32), scale).astype(bf16)
    for rows in tiles:
        beta[rows] = dot(hidden[rows], wb[...], 1, 1)
    for i, w in enumerate((wq, wk, wv, wg)):
        loads[1 + i].wait()
        lanes = slice(i * width, (i + 1) * width)
        for rows in tiles:
            got = dot(hidden[rows], w[...])
            if i < 3:
                ext[TAIL + rows.start : TAIL + rows.stop, lanes] = got
            else:
                gate[rows] = got
        if i < 3:
            ext[0:TAIL, lanes] = dot(low, w[...])
    store(ext, ext_h)
    loads[5].wait()
    for t, rows in enumerate(tiles):
        live = live_mask(meta, t, tile)
        gd[rows] = jnp.where(live, cot[rows].astype(f32), 0.0).astype(bf16)
    store(gd, gd_h)
    store(gd.at[own], gd_own)
    row = iota((GROUP, 1), 0)
    taps = tap_table(cq, ck, cv)

    def front(n):
        base = pl.multiple_of(n * GROUP, GROUP)
        for c in range(3 * heads):
            lanes = slice(c * DH, (c + 1) * DH)
            win = ext[pl.ds(pl.multiple_of(base + TAIL - 8, 8), GROUP + 8), lanes]
            acc = taps(KW - 1, c) * win[8:]
            for d in range(1, KW):
                part = jnp.where(row < meta[0, n] * d, 0.0, win[8 - d : 8 - d + GROUP])
                acc = acc + taps(KW - 1 - d, c) * part
            conv[pl.ds(base, GROUP), lanes] = acc
            acted = acc * jax.nn.sigmoid(acc)
            qkv[pl.ds(base, GROUP), lanes] = unit(acted) if c < 2 * heads else acted

    pl.loop(0, groups)(front)
    store(conv, conv_h)
    r64 = iota((GROUP, GROUP), 0)
    c64 = iota((GROUP, GROUP), 1)
    eye = (iota((DH, DH), 0) == iota((DH, DH), 1)).astype(f32)

    def load(n, h):
        rows = pl.ds(pl.multiple_of(n * GROUP, GROUP), GROUP)
        return [qkv[rows, (i * heads + h) * DH : (i * heads + h + 1) * DH] for i in range(3)]

    def local(i, _):
        chains = [(2 * i + j, h) for j in range(2) for h in range(heads)]
        systems = []
        kept = []
        for n, h in chains:
            q, k, v = load(n, h)
            b = beta_col(beta, meta, n, h)[0]
            both = fdot(jnp.concatenate([k * b, q], axis=0), k, 1, 1)
            systems.append(jnp.where(r64 > c64, both[:GROUP], 0.0))
            score[n * heads + h] = jnp.where(r64 >= c64, both[GROUP:], 0.0)
            kept.append((k, b, v))
        inverses = tri_inverse(systems)
        for (n, h), inverse, (k, b, v) in zip(chains, inverses, kept):
            rows = pl.ds(pl.multiple_of(n * GROUP, GROUP), GROUP)
            inv[n * heads + h] = inverse
            wu = fdot(inverse, jnp.concatenate([k * b, v * b], axis=1))
            wmix[rows, h * DH : (h + 1) * DH] = wu[:, :DH]
            umix[rows, h * DH : (h + 1) * DH] = wu[:, DH:]
            kwu = fdot(k, wu, 0, 0)
            amap[n * heads + h] = eye - kwu[:, :DH]
            badd[n * heads + h] = kwu[:, DH:]
        return 0

    lax.fori_loop(0, groups // 2, local, 0)
    store(inv, inv_h)
    store(amap, amap_h)
    for h in range(heads):
        dev[h, :, :DH] = eye
        dev[h, :, DH:] = jnp.zeros((DH, DH), f32)

    def chain(n, _):
        keep = 1.0 - meta[0, n].astype(f32)
        for h in range(heads):
            start = dev[h] * keep
            zst[n * heads + h] = start
            moved = fdot(amap[n * heads + h], start)
            dev[h, :, :DH] = moved[:, :DH]
            dev[h, :, DH:] = moved[:, DH:] + badd[n * heads + h]
        return 0

    lax.fori_loop(0, groups, chain, 0)
    last[...] = dev[:, :, DH:]

    def outs(i, _):
        for n, h in [(2 * i + j, h) for j in range(2) for h in range(heads)]:
            rows = pl.ds(pl.multiple_of(n * GROUP, GROUP), GROUP)
            lanes = slice(h * DH, (h + 1) * DH)
            q = qkv[rows, lanes]
            both = fdot(jnp.concatenate([q, wmix[rows, lanes]], axis=0), zst[n * heads + h])
            lower = jnp.concatenate([-both[GROUP:, :DH], umix[rows, lanes] - both[GROUP:, DH:]], axis=1)
            made = both[:GROUP] + fdot(score[n * heads + h], lower)
            mout[rows, lanes] = made[:, :DH]
            oloc[rows, lanes] = made[:, DH:]
        return 0

    lax.fori_loop(0, groups // 2, outs, 0)
    for copy in stores:
        copy.wait()


def fold_hops(hops, h):
    state = hops[-1][h]
    for hop in hops[-2::-1]:
        state = hop[h, :, DH:] + fdot(hop[h, :, :DH], state)
    return state


def out_kernel(hop_count, tp, *refs):
    hops, refs = refs[:hop_count], refs[hop_count:]
    mout, oloc, gate, nh, wo, heads_out, att, send, keep, entry = refs
    heads = gate.shape[1] // DH
    states = [fold_hops(hops, h) for h in range(heads)]
    for h in range(heads):
        entry[h] = states[h]
    share = mout.shape[0] // 4
    for rel in range(4):
        rows = rows_of(tp[0] ^ rel, share)
        lows = []
        for h in range(heads):
            lanes = slice(h * DH, (h + 1) * DH)
            o = oloc[rows, lanes] + fdot(mout[rows, lanes], states[h])
            heads_out[rows, lanes] = o
            factor = lax.rsqrt(jnp.mean(o * o, axis=-1, keepdims=True) + head_epsilon)
            g = gate[rows, lanes]
            lows.append((o * factor * wide_gain(nh) * (g * jax.nn.sigmoid(g))).astype(bf16))
        low = jnp.concatenate(lows, axis=1)
        att[rows] = low
        part = dot(low, wo[...])
        if rel % 2:
            send[rel // 2] = part.astype(bf16)
        else:
            keep[rel // 2] = part


def states_kernel(entry, zst, qkv, wmix, umix, score, states, vnew, qeff):
    groups = qkv.shape[0] // GROUP
    heads = wmix.shape[1] // DH

    def one(i, _):
        for n, h in [(2 * i + j, h) for j in range(2) for h in range(heads)]:
            rows = pl.ds(pl.multiple_of(n * GROUP, GROUP), GROUP)
            lanes = slice(h * DH, (h + 1) * DH)
            at = n * heads + h
            s = zst[at, :, DH:] + fdot(zst[at, :, :DH], entry[h])
            states[at] = s
            w = wmix[rows, lanes]
            vnew[rows, lanes] = umix[rows, lanes] - fdot(w, s)
            qeff[rows, lanes] = qkv[rows, lanes] - fdot(score[at], w)
        return 0

    lax.fori_loop(0, groups // 2, one, 0)


def mid_kernel(x, kept, got, gain, residual, second):
    total = x[...].astype(f32) + kept[...] + got[...].astype(f32)
    residual[...] = total
    second[...] = rms_rows(total, wide_gain(gain)).astype(bf16)


def ffn_kernel(plans, tp, place, s0, s1, s2, s3, grad_down, wg, wu, wd, down_send, down_keep, send, keep, *refs):
    sums, (second, inner, dgate, dup, acc) = refs[:-5], refs[-5:]
    share = s0.shape[0]
    for half, pair in enumerate(((s0, s1), (s2, s3))):
        sec = jnp.concatenate([pair[0][...], pair[1][...]], axis=0)
        blocks = [rows_of(tp[0] ^ (2 * half + j), share) for j in range(2)]
        gd = jnp.concatenate([grad_down[b] for b in blocks], axis=0)
        gv = dot(sec, wg[...], 1, 1)
        uv = dot(sec, wu[...], 1, 1)
        sig = jax.nn.sigmoid(gv)
        act = gv * sig
        inn = (act * uv).astype(bf16)
        gi = dot(gd, wd[...], 1, 1)
        dg = (gi * uv * (sig * (1.0 + gv * (1.0 - sig)))).astype(bf16)
        du = (gi * act).astype(bf16)
        for j, b in enumerate(blocks):
            part = slice(j * share, (j + 1) * share)
            second[b] = sec[part]
            inner[b] = inn[part]
            dgate[b] = dg[part]
            dup[b] = du[part]
        grad = dot(dg, wg[...]) + dot(du, wu[...])
        keep[half] = grad[:share]
        send[half] = grad[share:].astype(bf16)
        down = dot(inn, wd[...])
        down_keep[half] = down[:share]
        down_send[half] = down[share:].astype(bf16)
    for left, right, plan in ((inner, grad_down, 0), (dgate, second, 1), (dup, second, 2)):
        acc[...] = dot(left[...], right[...], 0, 0)
        put(acc, place[0], plans[plan], sums)


def turn_kernel(kept, got, residual, gain, grad_y, grad_residual, branch, gain_part):
    gs = kept[...] + got[...].astype(f32)
    v = residual[...]
    g = wide_gain(gain)
    r = lax.rsqrt(jnp.mean(v * v, axis=-1, keepdims=True) + row_epsilon)
    gain_part[...] = jnp.sum(gs * v * r, axis=0, keepdims=True)
    e = gs * g
    back = r * e - v * (r * r * r) * jnp.mean(e * v, axis=-1, keepdims=True)
    total = grad_y[...].astype(f32) + back
    grad_residual[...] = total
    branch[...] = total.astype(bf16)


def flow_kernel(tp, meta, b0, b1, b2, b3, wo, heads_out, gate, nh, qeff, amap, branch, dgate, dout, rst, dev, last, nh_part, flows):
    share = b0.shape[0]
    heads = gate.shape[1] // DH
    groups = gate.shape[0] // GROUP
    gains = jnp.zeros((1, DH), f32)
    for half, pair in enumerate(((b0, b1), (b2, b3))):
        both = jnp.concatenate([pair[0][...], pair[1][...]], axis=0)
        ga = dot(both, wo[...], 1, 1)
        for j in range(2):
            rows = rows_of(tp[0] ^ (2 * half + j), share)
            branch[rows] = pair[j][...]
            for h in range(heads):
                lanes = slice(h * DH, (h + 1) * DH)
                gz = ga[j * share : (j + 1) * share, lanes]
                o = heads_out[rows, lanes]
                g = gate[rows, lanes]
                gain = wide_gain(nh)
                r = lax.rsqrt(jnp.mean(o * o, axis=-1, keepdims=True) + head_epsilon)
                sig = jax.nn.sigmoid(g)
                act = g * sig
                e = gz * gain * act
                base = gz * o * r
                gains = gains + jnp.sum(base * act, axis=0, keepdims=True)
                dgate[rows, lanes] = (base * gain * (sig * (1.0 + g * (1.0 - sig)))).astype(bf16)
                dout[rows, lanes] = r * e - o * (r * r * r) * jnp.mean(e * o, axis=-1, keepdims=True)
    nh_part[...] = gains

    def local(i, _):
        for n, h in [(2 * i + j, h) for j in range(2) for h in range(heads)]:
            rows = pl.ds(pl.multiple_of(n * GROUP, GROUP), GROUP)
            lanes = slice(h * DH, (h + 1) * DH)
            flows[n * heads + h] = fdot(qeff[rows, lanes], dout[rows, lanes], 0, 0)
        return 0

    lax.fori_loop(0, groups // 2, local, 0)
    eye = (iota((DH, DH), 0) == iota((DH, DH), 1)).astype(f32)
    for h in range(heads):
        dev[h, :, :DH] = eye
        dev[h, :, DH:] = jnp.zeros((DH, DH), f32)

    def chain(i, _):
        n = groups - 1 - i
        keep = 1.0 - meta[0, n].astype(f32)
        for h in range(heads):
            at = n * heads + h
            later = dev[h]
            rst[at] = later
            moved = fdot(amap[at], later, 0, 0)
            dev[h, :, :DH] = moved[:, :DH] * keep
            dev[h, :, DH:] = (moved[:, DH:] + flows[at]) * keep
        return 0

    lax.fori_loop(0, groups, chain, 0)
    last[...] = dev[:, :, DH:]


def side_kernel(qkv, dout, vnew, states, score, ndo, dq, dk):
    heads = dout.shape[1] // DH
    groups = dout.shape[0] // GROUP
    lower = iota((GROUP, GROUP), 0) >= iota((GROUP, GROUP), 1)

    def one(i, _):
        for n, h in [(2 * i + j, h) for j in range(2) for h in range(heads)]:
            rows = pl.ds(pl.multiple_of(n * GROUP, GROUP), GROUP)
            lanes = slice(h * DH, (h + 1) * DH)
            at = n * heads + h
            q = qkv[rows, lanes]
            k = qkv[rows, (heads + h) * DH : (heads + h + 1) * DH]
            do = dout[rows, lanes]
            ndo[rows, lanes] = fdot(score[at], do, 0, 0)
            dn = jnp.where(lower, fdot(do, vnew[rows, lanes], 1, 1), 0.0)
            dq[rows, lanes] = fdot(do, states[at], 1, 1) + fdot(dn, k)
            dk[rows, lanes] = fdot(dn, q, 0, 0)
        return 0

    lax.fori_loop(0, groups // 2, one, 0)


def unit_back(a, grad):
    r = lax.rsqrt(jnp.sum(a * a, axis=-1, keepdims=True) + unit_epsilon)
    return r * grad - a * (r * r * r) * jnp.sum(a * grad, axis=-1, keepdims=True)


def back_kernel(hop_count, meta, *refs):
    hops, refs = refs[:hop_count], refs[hop_count:]
    rst, qkv, conv, ext, cq, ck, cv, beta, inv, states, vnew, ndo, dq, dk1, gp, last, halo, dbeta, dtaps, dc = refs
    taps = tap_table(cq, ck, cv)
    heads = ndo.shape[1] // DH
    groups = ndo.shape[0] // GROUP
    total = ndo.shape[0]
    exits = [fold_hops(hops, h) for h in range(heads)]
    strict = iota((GROUP, GROUP), 0) > iota((GROUP, GROUP), 1)
    lane = iota((GROUP, LANES), 1)
    dc[total:] = jnp.zeros((8, dc.shape[1]), f32)

    def one(i, _):
        for j in range(2):
            n = 2 * i + j
            rows = pl.ds(pl.multiple_of(n * GROUP, GROUP), GROUP)
            raws = jnp.zeros((GROUP, LANES), f32)
            for h in range(heads):
                at = n * heads + h
                lanes = [slice((p * heads + h) * DH, (p * heads + h + 1) * DH) for p in range(3)]
                k = qkv[rows, lanes[1]]
                v = qkv[rows, lanes[2]]
                b, sig, live = beta_col(beta, meta, n, h)
                ds = rst[at, :, DH:] + fdot(rst[at, :, :DH], exits[h])
                dvn = ndo[rows, lanes[0]] + fdot(k, ds)
                d = fdot(inv[at], dvn, 0, 0)
                vn = vnew[rows, lanes[0]]
                dstate = fdot(d, states[at], 1, 1)
                vds = fdot(vn, ds, 1, 1)
                da = jnp.where(strict, -fdot(d, vn, 1, 1), 0.0)
                dak = fdot(da, k)
                datk = fdot(da, k * b, 0, 0)
                dk = dk1[rows, lanes[0]] + vds + b * (dak - dstate) + datk
                db = jnp.sum(d * v + (dak - dstate) * k, axis=-1, keepdims=True)
                db = jnp.where(live, db * sig * (1.0 - sig), 0.0)
                raws = jnp.where(lane == h, db, raws)
                grads = (dq[rows, lanes[0]], dk, d * b)
                for p in range(3):
                    c = conv[rows, lanes[p]]
                    s = jax.nn.sigmoid(c)
                    grad = unit_back(c * s, grads[p]) if p < 2 else grads[p]
                    dc[rows, lanes[p]] = grad * (s * (1.0 + c * (1.0 - s)))
            dbeta[rows] = raws.astype(bf16)
        return 0

    lax.fori_loop(0, groups // 2, one, 0)
    row = iota((GROUP, 1), 0)
    dtaps[...] = jnp.zeros(dtaps.shape, f32)

    def masked(win, d, here, after):
        front = jnp.where(iota((GROUP, 1), 0) < here * d, 0.0, win[:GROUP])
        if after is None:
            return front
        back = jnp.where(iota((8, 1), 0) < after * d, 0.0, win[GROUP:])
        return jnp.concatenate([front, back], axis=0)

    def taps_back(n, _):
        base = pl.multiple_of(n * GROUP, GROUP)
        here = meta[0, n]
        after = meta[0, jnp.minimum(n + 1, groups - 1)]
        for c in range(3 * heads):
            lanes = slice(c * DH, (c + 1) * DH)
            win = dc[pl.ds(base, GROUP + 8), lanes]
            old = ext[pl.ds(pl.multiple_of(base + TAIL - 8, 8), GROUP + 8), lanes]
            acc = taps(KW - 1, c) * win[:GROUP]
            dtaps[KW - 1 : KW, lanes] += jnp.sum(win[:GROUP] * old[8:], axis=0, keepdims=True)
            for d in range(1, KW):
                part = masked(win, d, here, after)
                j = KW - 1 - d
                acc = acc + taps(j, c) * part[d : d + GROUP]
                dtaps[j : j + 1, lanes] += jnp.sum(
                    part[:GROUP] * old[8 - d : 8 - d + GROUP], axis=0, keepdims=True
                )
            gp[pl.ds(base, GROUP), lanes] = acc.astype(bf16)

            @pl.when(n == groups - 1)
            def _():
                last[:, lanes] = acc[GROUP - TAIL :]

        return 0

    lax.fori_loop(0, groups, taps_back, 0)
    zero = jnp.zeros((8, DH), f32)
    for c in range(3 * heads):
        lanes = slice(c * DH, (c + 1) * DH)
        win = dc[0:8, lanes]
        acc = zero
        for d in range(1, KW):
            part = jnp.where(iota((8, 1), 0) < meta[0, 0] * d, 0.0, win)
            j = KW - 1 - d
            acc = acc + taps(j, c) * jnp.concatenate([zero, part], axis=0)[d : d + 8]
        halo[:, lanes] = acc


def hid_kernel(tp, gp_in, last, incoming, dgate, dbeta, wq, wk, wv, wg, wb, gp, send, keep):
    total = gp.shape[0]
    width = wq.shape[1]
    gp[: total - TAIL] = gp_in[: total - TAIL]
    fixed = jnp.concatenate([last[: TAIL - 8], last[TAIL - 8 :] + incoming[...]], axis=0)
    gp[total - TAIL :] = fixed.astype(bf16)
    share = total // 4
    for half in range(2):
        blocks = [rows_of(tp[0] ^ (2 * half + j), share) for j in range(2)]
        cat = lambda ref: jnp.concatenate([ref[b] for b in blocks], axis=0)
        grads = cat(gp)
        acc = dot(cat(dgate), wg[...], 1, 1)
        small = cat(dbeta).astype(f32)
        for h in range(wb.shape[0]):
            acc = acc + small[:, h : h + 1] * wb[h : h + 1].astype(f32)
        for i, w in enumerate((wq, wk, wv)):
            acc = acc + dot(grads[:, i * width : (i + 1) * width], w[...], 1, 1)
        keep[half] = acc[:share]
        send[half] = acc[share:].astype(bf16)


def in_kernel(kept, got, x, gain, grad_residual, grad_in, gain_part):
    gh = kept[...] + got[...].astype(f32)
    v = x[...].astype(f32)
    g = wide_gain(gain)
    r = lax.rsqrt(jnp.mean(v * v, axis=-1, keepdims=True) + row_epsilon)
    gain_part[...] = jnp.sum(gh * v * r, axis=0, keepdims=True)
    e = gh * g
    back = r * e - v * (r * r * r) * jnp.mean(e * v, axis=-1, keepdims=True)
    grad_in[...] = (grad_residual[...] + back).astype(bf16)


def outblock_kernel(tp, meta, kept, got, residual, out):
    total = residual[...] + kept[...] + got[...].astype(f32)
    live = live_mask(meta, tp[0], total.shape[0])
    out[...] = jnp.where(live, total, 0.0).astype(bf16)


def place_kernel(tp, a0, a1, a2, a3, out):
    for rel, part in enumerate((a0, a1, a2, a3)):
        out[rows_of(tp[0] ^ rel, part.shape[0])] = part[...].astype(out.dtype)


def swap(value, bit, axis="tp"):
    count = lax.axis_size(axis)
    return lax.ppermute(value, axis, [(i, i ^ bit) for i in range(count)])


def add_kernel(keep, got, kept, send):
    half = kept.shape[0]
    kept[...] = keep[:half] + got[:half].astype(f32)
    send[...] = (keep[half:] + got[half:].astype(f32)).astype(bf16)


def last_kernel(keep, got, own):
    own[...] = (keep[...] + got[...].astype(f32)).astype(bf16)


def pack_kernel(a, b, out):
    half = a.shape[0]
    out[:half] = a[...]
    out[half:] = b[...]


def fold(order, keep, got, name):
    half = (keep.shape[0] // 2, *keep.shape[1:])
    return order.run(add_kernel, name, [(half, f32), (half, bf16)], [keep, got])


def rank_of(m, bits):
    at = 0
    for bit in bits:
        at = 2 * at + ((m >> bit) & 1)
    return at


class Plan:
    def __init__(self, index, bits, base, size, start=0, folds=1):
        self.index, self.bits, self.base, self.size = index, bits, base, size
        self.start, self.folds = start, folds


def put(acc, place, plan, sums):
    for part in plan if isinstance(plan, (list, tuple)) else (plan,):
        keep, send = sums[2 * part.index : 2 * part.index + 2]
        blocks = 1 << len(part.bits)
        height = part.size // part.folds
        wide = acc.shape[1]
        for m in range(blocks):
            at = rank_of(m, part.bits[1:])
            low = (m >> part.bits[0]) & 1
            for i in range(part.folds):
                begin = part.start + (m ^ place) * part.size + i * height
                block = acc[pl.ds(pl.multiple_of(begin, 8), height)]
                rows = slice(part.base, part.base + height)
                lanes = slice(i * wide, (i + 1) * wide)
                if low:
                    send[at, rows, lanes] = block.astype(bf16)
                else:
                    keep[at, rows, lanes] = block


def take(out, place, part, bits, near, far):
    blocks = 1 << len(bits)
    height = part.size // part.folds
    wide = out.shape[1]
    for m in range(blocks):
        source = far if (m >> bits[-1]) & 1 else near
        at = rank_of(m, bits[-2::-1])
        for i in range(part.folds):
            begin = part.start + (m ^ place) * part.size + i * height
            out[pl.ds(pl.multiple_of(begin, 8), height)] = source[
                at, part.base : part.base + height, i * wide : (i + 1) * wide
            ].astype(f32)


class Sum:
    def __init__(self, order, keep, send, scatter, gather, tag):
        self.order, self.tag, self.gather = order, tag, gather
        self.keep, self.left = keep, list(scatter)
        self.swap(send)
        self.own = self.near = None

    def swap(self, send):
        self.got = swap(send, 1 << self.left.pop(0), "seq")

    def step(self):
        order, tag = self.order, self.tag
        if self.own is None and self.left:
            self.keep, send = fold(order, self.keep, self.got, tag + "_fold")
            self.swap(send)
            return
        if self.own is None:
            (self.own,) = order.run(
                last_kernel, tag + "_last", [(self.keep.shape, bf16)], [self.keep, self.got]
            )
            more = 1 << len(self.gather)
            while more < lax.axis_size("seq"):
                other = swap(self.own, more, "seq")
                self.own = (self.own.astype(f32) + other.astype(f32)).astype(bf16)
                more *= 2
            self.left = list(self.gather)
        else:
            twice = (2 * self.own.shape[0], *self.own.shape[1:])
            (self.own,) = order.run(
                pack_kernel, tag + "_pack", [(twice, bf16)], [self.own, self.got]
            )
        self.swap(self.own)

    def settle(self, plans, outs, name):
        count = len(outs)

        def kernel(place, near, far, *refs):
            for part, out in zip(plans, refs):
                take(out, place[0], part, self.gather, near, far)

        return self.order.run(
            kernel, name, [(o, f32) for o in outs], [self.place, self.own, self.got], smem=(0,)
        )


def scatter_first(order, keep, send):
    return fold(order, keep, swap(send, 1), "fold_tp")


def grads_b_kernel(plans, place, attended, branch, hidden, dgate, *refs):
    sums, (acc, acc2) = refs[:-2], refs[-2:]
    acc[...] = dot(attended[...], branch[...], 0, 0)
    put(acc, place[0], plans[0], sums)
    acc2[...] = dot(hidden[...], dgate[...], 0, 0)
    put(acc2, place[0], plans[1], sums)


def grads_c_kernel(plans, place, hidden, gp, *refs):
    sums, acc = refs[:-1], refs[-1]
    acc[...] = dot(hidden[...], gp[...], 0, 0)
    for plan in plans:
        put(acc, place[0], plan, sums)


def sum_shapes(blocks, rows, cols):
    return [((blocks // 2, rows, cols), f32), ((blocks // 2, rows, cols), bf16)]


def gather_rel(own):
    near = swap(own, 1)
    far = swap(own, 2)
    return own, near, far, swap(far, 1)


def shift(value, steps):
    count = lax.axis_size("seq")
    pairs = [(i, i + steps) for i in range(count) if 0 <= i + steps < count]
    return lax.ppermute(value, "seq", pairs)


def hops_of(dev, last, sign, reach):
    return [shift(dev, sign * k) for k in range(1, reach)] + [shift(last, sign * reach)]


def small_kernel(dtaps, dbeta, hidden, in_part, mid_part, head_part, taps_out, gains_out):
    wide = dtaps.shape[1]
    taps_out[...] = jnp.zeros(taps_out.shape, f32)
    taps_out[0:KW, :wide] = dtaps[...]
    product = dot(dbeta[...], hidden[...], 0, 0)
    taps_out[KW : KW + 4] = product[:4]
    gains_out[...] = jnp.zeros(gains_out.shape, f32)
    gains_out[0:1] = in_part[...]
    gains_out[1:2] = mid_part[...]
    gains_out[2:3, : head_part.shape[1]] = head_part[...]


def plus_kernel(a, b, out):
    out[...] = a[...] + b[...]


def plus(order, a, b):
    return order.run(plus_kernel, "plus", [(a.shape, f32)], [a, b])[0]


def shards(
    layer_input,
    seq_groups,
    seq_pads,
    norm_in,
    w_query,
    w_key,
    w_value,
    conv_query,
    conv_key,
    conv_value,
    w_beta,
    w_gate_out,
    norm_head,
    w_out,
    norm_mid,
    w_gate,
    w_up,
    w_down,
    cotangent,
):
    total, model = layer_input.shape
    width = w_query.shape[1]
    heads = width // DH
    groups = total // GROUP
    share = total // 4
    ffw = w_gate.shape[1]
    seq_count = lax.axis_size("seq")
    reach = max(1, seq_count // 4)
    tp_rank = lax.axis_index("tp")
    tp = tp_rank.astype(jnp.int32).reshape(1)
    blocks = 8
    place = (lax.axis_index("seq") % blocks).astype(jnp.int32).reshape(1)
    first = (lax.axis_index("seq") * groups).astype(jnp.int32).reshape(1)
    taps = (conv_query, conv_key, conv_value)
    wb = w_beta.T
    tail = shift(layer_input[total - TAIL :], 1)
    chains = groups * heads
    wide = (total, width)
    mats = 2 * total * model
    order = Order()
    run = order.run

    def begin(keep, send, scatter, gather, tag):
        made = Sum(order, keep, send, scatter, gather, tag)
        made.place = place
        return made

    weight = pltpu.VMEM((model, width), bf16)
    rows = pltpu.VMEM((total, model), bf16)
    ext_shape = (total + TAIL, 3 * width)
    conv_shape = (total, 3 * width)
    inv_shape = (chains, GROUP, GROUP)
    map_shape = (chains, DH, DH)
    (
        gate_raw, beta_raw, meta, qkv, wmix, umix, score, zst, dev, last, mout, oloc,
        hidden, grad_down, x_own, gd_own, ext, conv, inv, amap,
    ) = run(
        front_kernel,
        "front",
        [
            (wide, f32),
            ((total, heads), f32),
            ((2, groups), jnp.int32),
            (conv_shape, f32),
            (wide, f32),
            (wide, f32),
            (inv_shape, f32),
            ((chains, DH, 2 * DH), f32),
            ((heads, DH, 2 * DH), f32),
            ((heads, DH, DH), f32),
            (wide, f32),
            (wide, f32),
            ((total, model), bf16),
            ((total, model), bf16),
            ((share, model), bf16),
            ((share, model), bf16),
            (ext_shape, f32),
            (conv_shape, f32),
            (inv_shape, f32),
            (map_shape, f32),
        ],
        [first, tp, seq_groups, seq_pads, layer_input, cotangent, norm_in, w_query, w_key, w_value, w_gate_out, wb, tail, *taps],
        smem=(0, 1, 2, 3),
        smem_out=(2,),
        hbm=(4, 5, 7, 8, 9, 10),
        hbm_out=tuple(range(12, 20)),
        pin=(2, 3, 4, 5, 6, 7, 8, 9, 10, 11, 13, 14, 15),
        scratch=[
            rows, rows, weight, weight, weight, weight, rows, rows,
            pltpu.VMEM(ext_shape, f32),
            pltpu.VMEM(conv_shape, f32),
            pltpu.VMEM(inv_shape, f32),
            pltpu.VMEM(map_shape, f32),
            pltpu.VMEM(map_shape, f32),
            pltpu.SemaphoreType.DMA((6,)),
            pltpu.SemaphoreType.DMA((8,)),
        ],
        flops=mats * 10 * width,
        vmem=20,
    )
    hops = hops_of(dev, last, 1, reach)
    heads_out, attended, send, keep, entry = run(
        lambda *r: out_kernel(reach, *r),
        "out",
        [(wide, f32), (wide, bf16), ((2, share, model), bf16), ((2, share, model), f32), ((heads, DH, DH), f32)],
        [tp, *hops, mout, oloc, gate_raw, norm_head, w_out],
        smem=(0,),
        flops=mats * width,
    )
    kept, far = scatter_first(order, keep, send)
    got = swap(far, 2)
    states, vnew, qeff = run(
        states_kernel,
        "states",
        [(map_shape, f32), (wide, f32), (wide, f32)],
        [entry, zst, qkv, wmix, umix, score],
        flops=mats * width,
    )
    residual, second_own = run(
        mid_kernel,
        "mid",
        [((share, model), f32), ((share, model), bf16)],
        [x_own, kept[0], got[0], norm_mid],
    )
    size = ffw // blocks
    bits = [(0, 1, 2), (1, 0, 2), (0, 1, 2), (0, 1, 2), (1, 0, 2)]
    gathers = [(2, 1, 0), (2, 0, 1), (2, 1, 0), (2, 1, 0), (2, 0, 1)]
    cut_rows = ffw // 2
    plans_a = [
        Plan(0, bits[0], 0, size),
        Plan(1, bits[1], 0, size),
        Plan(2, bits[2], 0, size),
    ]
    down_send, down_keep, send, keep, *sums = run(
        lambda *r: ffn_kernel(plans_a, *r),
        "ffn",
        [
            ((2, share, model), bf16),
            ((2, share, model), f32),
            ((2, share, model), bf16),
            ((2, share, model), f32),
            *(sum_shapes(blocks, size, model) * 3),
        ],
        [tp, place, *gather_rel(second_own), grad_down, w_gate.T, w_up.T, w_down],
        smem=(0, 1),
        scratch=[
            rows,
            pltpu.VMEM((total, ffw), bf16),
            pltpu.VMEM((total, ffw), bf16),
            pltpu.VMEM((total, ffw), bf16),
            pltpu.VMEM((ffw, model), f32),
        ],
        flops=9 * mats * ffw,
        vmem=24,
    )
    near = swap(send, 1)
    a1 = begin(sums[0], sums[1], bits[0], gathers[0], "a1")
    a2 = begin(sums[2], sums[3], bits[1], gathers[1], "a2")
    kept, far = fold(order, keep, near, "fold_tp")
    got = swap(far, 2)
    grad_residual, branch_own, mid_part = run(
        turn_kernel,
        "turn",
        [((share, model), f32), ((share, model), bf16), ((1, model), f32)],
        [kept[0], got[0], residual, norm_mid, gd_own],
    )
    branch_all = gather_rel(branch_own)
    a3 = begin(sums[4], sums[5], bits[2], gathers[2], "a3")
    branch, dgate_raw, dout, rst, dev, last, head_part = run(
        flow_kernel,
        "flow",
        [
            ((total, model), bf16),
            (wide, bf16),
            (wide, f32),
            ((chains, DH, 2 * DH), f32),
            ((heads, DH, 2 * DH), f32),
            ((heads, DH, DH), f32),
            ((1, DH), f32),
        ],
        [tp, meta, *branch_all, w_out, heads_out, gate_raw, norm_head, qeff, amap],
        smem=(0, 1),
        scratch=[pltpu.VMEM(map_shape, f32)],
        flops=3 * mats * width,
    )
    hops = hops_of(dev, last, -1, reach)
    ndo, dq, dk = run(
        side_kernel,
        "side",
        [(wide, f32)] * 3,
        [qkv, dout, vnew, states, score],
        flops=mats * width,
    )
    a1.step()
    a2.step()
    plans_b = [
        Plan(0, bits[3], 0, width // blocks),
        Plan(0, bits[3], width // blocks, model // blocks, folds=model // width),
    ]
    sums = run(
        lambda *r: grads_b_kernel(plans_b, *r),
        "grads_b",
        sum_shapes(blocks, 2 * width // blocks, model),
        [place, attended, branch, hidden, dgate_raw],
        smem=(0,),
        scratch=[pltpu.VMEM((width, model), f32), pltpu.VMEM((model, width), f32)],
        flops=2 * mats * width,
    )
    b1 = begin(*sums, bits[3], gathers[3], "b1")
    gp, last, halo, dbeta, dtaps = run(
        lambda *r: back_kernel(reach, *r),
        "back",
        [
            (conv_shape, bf16),
            ((TAIL, 3 * width), f32),
            ((8, 3 * width), f32),
            ((total, LANES), bf16),
            ((KW, 3 * width), f32),
        ],
        [meta, *hops, rst, qkv, conv, ext, *taps, beta_raw, inv, states, vnew, ndo, dq, dk],
        smem=(0,),
        scratch=[pltpu.VMEM((total + 8, 3 * width), f32)],
        flops=3 * mats * width,
    )
    incoming = shift(halo, -1)
    a1.step()
    a2.step()
    a3.step()
    gp, send, keep = run(
        hid_kernel,
        "hid",
        [(conv_shape, bf16), ((2, share, model), bf16), ((2, share, model), f32)],
        [tp, gp, last, incoming, dgate_raw, dbeta, w_query, w_key, w_value, w_gate_out, wb],
        smem=(0,),
        flops=mats * 4 * width,
        vmem=12,
    )
    near = swap(send, 1)
    half = model // 2
    plans_c = [
        Plan(0, bits[3], 0, half // blocks),
        Plan(1, bits[4], 0, half // blocks, start=half),
    ]
    sums = run(
        lambda *r: grads_c_kernel(plans_c, *r),
        "grads_c",
        sum_shapes(blocks, half // blocks, 3 * width) * 2,
        [place, hidden, gp],
        smem=(0,),
        scratch=[pltpu.VMEM((model, 3 * width), f32)],
        flops=mats * 3 * width,
        vmem=16,
    )
    c1 = begin(sums[0], sums[1], bits[3], gathers[3], "c1")
    c2 = begin(sums[2], sums[3], bits[4], gathers[4], "c2")
    kept, far = fold(order, keep, near, "fold_tp")
    got = swap(far, 2)
    b1.step()
    a1.step()
    a2.step()
    grad_in_own, in_part = run(
        in_kernel,
        "inp",
        [((share, model), bf16), ((1, model), f32)],
        [kept[0], got[0], x_own, norm_in, grad_residual],
    )
    grad_in_all = gather_rel(grad_in_own)
    row8 = ((8, model), f32)
    small, gains = run(
        small_kernel, "small", [row8, row8], [dtaps, dbeta, hidden, in_part, mid_part, head_part]
    )
    down_near = swap(down_send, 1)
    a3.step()
    b1.step()
    c1.step()
    c2.step()
    kept, far = fold(order, down_keep, down_near, "fold_tp")
    got = swap(far, 2)
    a1.step()
    a2.step()
    (grad_input,) = run(
        place_kernel,
        "place_in",
        [((total, model), f32)],
        [tp, *grad_in_all],
        smem=(0,),
    )
    (out_own,) = run(
        outblock_kernel,
        "outblk",
        [((share, model), bf16)],
        [tp, meta, kept[0], got[0], residual],
        smem=(0, 1),
    )
    out_all = gather_rel(out_own)
    a3.step()
    b1.step()
    c1.step()
    c2.step()
    a1.step()
    a2.step()
    gains = plus(order, gains, swap(gains, 1))
    a3.step()
    b1.step()
    c1.step()
    c2.step()
    gains = plus(order, gains, swap(gains, 2))
    step = 1
    small = jnp.concatenate([small, gains], axis=0)
    (block_out,) = run(
        place_kernel,
        "place_out",
        [((total, model), bf16)],
        [tp, *out_all],
        smem=(0,),
    )
    a3.step()
    b1.step()
    c1.step()
    c2.step()
    while step < seq_count:
        small = plus(order, small, swap(small, step, "seq"))
        step *= 2
    c1.step()
    c2.step()
    (grad_down_w,) = a1.settle([plans_a[0]], [(ffw, model)], "settle_a1")
    (grad_gate_w,) = a2.settle([plans_a[1]], [(ffw, model)], "settle_a2")
    (grad_up_w,) = a3.settle([plans_a[2]], [(ffw, model)], "settle_a3")
    grad_out_w, grad_gate_out_w = b1.settle(
        plans_b, [(width, model), (model, width)], "settle_b1"
    )

    def settle_c(place, near1, far1, near2, far2, *outs):
        for plan, gather, near, far in (
            (plans_c[0], gathers[3], near1, far1),
            (plans_c[1], gathers[4], near2, far2),
        ):
            for m in range(blocks):
                source = far if (m >> gather[-1]) & 1 else near
                at = rank_of(m, gather[-2::-1])
                begin = plan.start + (m ^ place[0]) * plan.size
                for i, out in enumerate(outs):
                    out[pl.ds(pl.multiple_of(begin, 8), plan.size)] = source[
                        at, :, i * width : (i + 1) * width
                    ].astype(f32)

    hidden_sums = run(
        settle_c,
        "settle_c",
        [((model, width), f32)] * 3,
        [place, c1.own, c1.got, c2.own, c2.got],
        smem=(0,),
    )
    cut = model // 4
    head_cut = DH // 4
    gain_of = lambda row, size: lax.dynamic_slice(small, (8 + row, tp_rank * size), (1, size)).reshape(size)
    tap_of = lambda i: small[:KW, i * width : (i + 1) * width]
    return (
        block_out,
        grad_input,
        gain_of(0, cut),
        hidden_sums[0],
        hidden_sums[1],
        hidden_sums[2],
        tap_of(0),
        tap_of(1),
        tap_of(2),
        small[KW : KW + heads].T,
        grad_gate_out_w,
        gain_of(2, head_cut),
        grad_out_w,
        gain_of(1, cut),
        grad_gate_w.T,
        grad_up_w.T,
        grad_down_w,
    )


def solution(mesh):
    rows = P("seq", None)
    cols = P(None, "tp")
    return jax.shard_map(
        shards,
        mesh=mesh,
        in_specs=(rows, P(), P(), P(), cols, cols, cols, cols, cols, cols, cols, cols, P(), P("tp", None), P(), cols, cols, P("tp", None), rows),
        out_specs=(rows, rows, P("tp"), cols, cols, cols, cols, cols, cols, cols, cols, P("tp"), P("tp", None), P("tp"), cols, cols, P("tp", None)),
        check_vma=False,
    )
```

```python
import jax
import jax.numpy as jnp
from jax import lax
from jax.experimental import pallas as pl
from jax.experimental.pallas import tpu as pltpu
from jax.sharding import PartitionSpec as P

DH = 128
KW = 4
GROUP = 64
TAIL = 16
LANES = 128

row_epsilon = 1e-06
head_epsilon = 1e-05
unit_epsilon = 1e-06
f32 = jnp.float32
bf16 = jnp.bfloat16


def dot(a, b, ca=1, cb=0):
    return lax.dot_general(a, b, (((ca,), (cb,)), ((), ())), preferred_element_type=f32)


def halves(a):
    high = a.astype(bf16)
    return high, (a - high.astype(f32)).astype(bf16)


def fdot(a, b, ca=1, cb=0):
    ah, al = halves(a)
    bh, bl = halves(b)
    return dot(
        jnp.concatenate([ah, al, ah], axis=ca), jnp.concatenate([bh, bh, bl], axis=cb), ca, cb
    )


def gdot(a, b, ca=1, cb=0):
    return dot(a.astype(bf16), b.astype(bf16), ca, cb)


def iota(shape, axis):
    return lax.broadcasted_iota(jnp.int32, shape, axis)


def rows_of(block, size):
    return pl.ds(pl.multiple_of(block * size, size), size)


COST = 1153500


class Order:
    def __init__(self):
        self.last = None
        self.also = ()

    def wait(self, *values):
        self.also = values

    def run(self, kernel, name, outs, args, smem=(), smem_out=(), hbm=(), pin=(), scratch=(), flops=COST, vmem=8):
        held = {"far": pltpu.HBM, "near": pltpu.VMEM}
        shapes = [
            held[o[2]](o[0], o[1]) if len(o) > 2 else jax.ShapeDtypeStruct(*o) for o in outs
        ]
        hbm_out = [i for i, o in enumerate(outs) if o[2:] == ("far",)]
        args = list(args)
        if self.last is not None:
            at = next(i for i in range(len(args)) if i not in smem and i not in pin)
            args[at] = lax.optimization_barrier((args[at], self.last, *self.also))[0]
            self.also = ()
        for i in pin:
            args[i] = pltpu.with_memory_space_constraint(args[i], pltpu.HBM)
        space = lambda i, low, far: pltpu.SMEM if i in low else pltpu.HBM if i in far else pltpu.VMEM
        made = pl.pallas_call(
            kernel,
            name=name,
            out_shape=shapes,
            in_specs=[pl.BlockSpec(memory_space=space(i, smem, hbm)) for i in range(len(args))],
            out_specs=[
                pl.BlockSpec(memory_space=space(i, smem_out, hbm_out)) for i in range(len(outs))
            ],
            scratch_shapes=list(scratch),
            compiler_params=pltpu.CompilerParams(vmem_limit_bytes=vmem << 20),
            cost_estimate=pl.CostEstimate(flops=flops, bytes_accessed=1, transcendentals=0),
        )(*args)
        self.last = next(o for i, o in enumerate(made) if i not in smem_out and i not in hbm_out)
        return made


def wide_gain(ref):
    return ref[...].astype(f32).reshape(1, ref.shape[0])


def live_mask(meta, block, size):
    parts = size // GROUP
    row = iota((size, 1), 0)
    limit = jnp.full((size, 1), 0, jnp.int32) + meta[1, block * parts]
    for part in range(1, parts):
        limit = jnp.where(row >= part * GROUP, meta[1, block * parts + part] + part * GROUP, limit)
    return row < limit


def rms_rows(values, gain):
    factor = lax.rsqrt(jnp.mean(values * values, axis=-1, keepdims=True) + row_epsilon)
    return values * factor * gain


def beta_col(beta, meta, n, h):
    raw = beta[pl.ds(pl.multiple_of(n * GROUP, GROUP), GROUP), h : h + 1]
    sig = jax.nn.sigmoid(raw)
    live = iota((GROUP, 1), 0) < meta[1, n]
    return jnp.where(live, sig, 0.0), sig, live


def unit(rows):
    return rows * lax.rsqrt(jnp.sum(rows * rows, axis=-1, keepdims=True) + unit_epsilon)


def tri_inverse(systems, block=16):
    size = systems[0].shape[0]
    row = iota((size, size), 0)
    col = iota((size, size), 1)
    eye = (row == col).astype(f32)
    tiles = [[eye[r : r + 8] for r in range(0, size, 8)] for _ in systems]
    lower = [[system[r : r + 8] for r in range(0, size, 8)] for system in systems]
    for step in range(block - 1):
        for low, part in zip(lower, tiles):
            for start in range(0, size, block):
                j = start + step
                line = part[j // 8][j % 8 : j % 8 + 1]
                for r in range((j + 1) // 8, (start + block) // 8):
                    part[r] = part[r] - low[r][:, j : j + 1] * line
    inverses = [jnp.concatenate(part, axis=0) for part in tiles]
    while block < size:
        pick = ((row // block) % 2 == 1) & (col // block == row // block - 1)
        mids = [
            fdot(inverse, jnp.where(pick, system, 0.0))
            for inverse, system in zip(inverses, systems)
        ]
        inverses = [inverse - fdot(mid, inverse) for mid, inverse in zip(mids, inverses)]
        block *= 2
    return inverses


def tap_table(*tables):
    values = [table[...].astype(f32) for table in tables]
    parts = values[0].shape[1] // DH
    return lambda j, c: values[c // parts][j : j + 1, (c % parts) * DH : (c % parts + 1) * DH]


def front_kernel(first, tp, seq_groups, seq_pads, xh, coth, gain, wqh, wkh, wvh, wgh, wb, tail, cq, ck, cv, gate, beta, meta, qkv, wmix, umix, score, zst, dev, last, hidden_h, gd_h, x_own, gd_own, ext_h, conv_h, inv_h, amap_h, x, cot, wq, wk, wv, wg, hidden, gd, ext, conv, inv, amap, badd, sems, out_sems):
    loads = [
        pltpu.make_async_copy(src, dst, sems.at[i])
        for i, (src, dst) in enumerate(
            ((xh, x), (wqh, wq), (wkh, wk), (wvh, wv), (wgh, wg), (coth, cot))
        )
    ]
    for load in loads:
        load.start()
    groups = x.shape[0] // GROUP
    for n in range(groups):
        meta[0, n] = 0
        meta[1, n] = 0

    def one(s, start):
        count = seq_groups[s]
        length = count * GROUP - seq_pads[s]
        for n in range(groups):
            gid = first[0] + n
            inside = (gid >= start) & (gid < start + count)
            here = jnp.clip(length - (gid - start) * GROUP, 0, GROUP)
            meta[0, n] = jnp.where(gid == start, 1, meta[0, n])
            meta[1, n] = jnp.where(inside, here, meta[1, n])
        return start + count

    lax.fori_loop(0, seq_groups.shape[0], one, jnp.int32(0))
    width = wq.shape[1]
    heads = width // DH
    tile = 256
    share = x_own.shape[0]
    scale = wide_gain(gain)
    own = rows_of(tp[0], share)
    stores = []

    def store(src, dst):
        copy = pltpu.make_async_copy(src, dst, out_sems.at[len(stores)])
        copy.start()
        stores.append(copy)

    loads[0].wait()
    store(x.at[own], x_own)
    tiles = [slice(t * tile, (t + 1) * tile) for t in range(x.shape[0] // tile)]
    for rows in tiles:
        hidden[rows] = rms_rows(x[rows].astype(f32), scale).astype(bf16)
    store(hidden, hidden_h)
    low = rms_rows(tail[...].astype(f32), scale).astype(bf16)
    for rows in tiles:
        beta[rows] = dot(hidden[rows], wb[...], 1, 1)
    for i, w in enumerate((wq, wk, wv, wg)):
        loads[1 + i].wait()
        lanes = slice(i * width, (i + 1) * width)
        for rows in tiles:
            got = dot(hidden[rows], w[...])
            if i < 3:
                ext[TAIL + rows.start : TAIL + rows.stop, lanes] = got
            else:
                gate[rows] = got
        if i < 3:
            ext[0:TAIL, lanes] = dot(low, w[...])
    store(ext, ext_h)
    loads[5].wait()
    for t, rows in enumerate(tiles):
        live = live_mask(meta, t, tile)
        gd[rows] = jnp.where(live, cot[rows].astype(f32), 0.0).astype(bf16)
    store(gd, gd_h)
    store(gd.at[own], gd_own)
    row = iota((GROUP, 1), 0)
    taps = tap_table(cq, ck, cv)

    def front(n):
        base = pl.multiple_of(n * GROUP, GROUP)
        for c in range(3 * heads):
            lanes = slice(c * DH, (c + 1) * DH)
            win = ext[pl.ds(pl.multiple_of(base + TAIL - 8, 8), GROUP + 8), lanes]
            acc = taps(KW - 1, c) * win[8:]
            for d in range(1, KW):
                part = jnp.where(row < meta[0, n] * d, 0.0, win[8 - d : 8 - d + GROUP])
                acc = acc + taps(KW - 1 - d, c) * part
            conv[pl.ds(base, GROUP), lanes] = acc
            acted = acc * jax.nn.sigmoid(acc)
            qkv[pl.ds(base, GROUP), lanes] = unit(acted) if c < 2 * heads else acted

    pl.loop(0, groups)(front)
    store(conv, conv_h)
    r64 = iota((GROUP, GROUP), 0)
    c64 = iota((GROUP, GROUP), 1)
    eye = (iota((DH, DH), 0) == iota((DH, DH), 1)).astype(f32)

    def load(n, h):
        rows = pl.ds(pl.multiple_of(n * GROUP, GROUP), GROUP)
        return [qkv[rows, (i * heads + h) * DH : (i * heads + h + 1) * DH] for i in range(3)]

    def local(i, _):
        chains = [(j, h) for j in range(groups) for h in range(heads)]
        systems = []
        kept = []
        for n, h in chains:
            q, k, v = load(n, h)
            b = beta_col(beta, meta, n, h)[0]
            both = fdot(jnp.concatenate([k * b, q], axis=0), k, 1, 1)
            systems.append(jnp.where(r64 > c64, both[:GROUP], 0.0))
            score[n * heads + h] = jnp.where(r64 >= c64, both[GROUP:], 0.0)
            kept.append((k, b, v))
        inverses = tri_inverse(systems)
        for (n, h), inverse, (k, b, v) in zip(chains, inverses, kept):
            rows = pl.ds(pl.multiple_of(n * GROUP, GROUP), GROUP)
            inv[n * heads + h] = inverse
            wu = fdot(inverse, jnp.concatenate([k * b, v * b], axis=1))
            wmix[rows, h * DH : (h + 1) * DH] = wu[:, :DH]
            umix[rows, h * DH : (h + 1) * DH] = wu[:, DH:]
            kwu = fdot(k, wu, 0, 0)
            amap[n * heads + h] = eye - kwu[:, :DH]
            badd[n * heads + h] = kwu[:, DH:]
        return 0

    local(0, 0)
    store(inv, inv_h)
    store(amap, amap_h)
    for h in range(heads):
        dev[h, :, :DH] = eye
        dev[h, :, DH:] = jnp.zeros((DH, DH), f32)

    def chain(n, _):
        keep = 1.0 - meta[0, n].astype(f32)
        for h in range(heads):
            start = dev[h] * keep
            zst[n * heads + h] = start
            moved = fdot(amap[n * heads + h], start)
            dev[h, :, :DH] = moved[:, :DH]
            dev[h, :, DH:] = moved[:, DH:] + badd[n * heads + h]
        return 0

    lax.fori_loop(0, groups, chain, 0)
    last[...] = dev[:, :, DH:]

    for copy in stores:
        copy.wait()


def local_kernel(qkv, wmix, umix, score, zst, mout, oloc):
    groups = qkv.shape[0] // GROUP
    heads = wmix.shape[1] // DH

    def one(i, _):
        for n, h in [(2 * i + j, h) for j in range(2) for h in range(heads)]:
            rows = pl.ds(pl.multiple_of(n * GROUP, GROUP), GROUP)
            lanes = slice(h * DH, (h + 1) * DH)
            q = qkv[rows, lanes]
            both = fdot(jnp.concatenate([q, wmix[rows, lanes]], axis=0), zst[n * heads + h])
            lower = jnp.concatenate(
                [-both[GROUP:, :DH], umix[rows, lanes] - both[GROUP:, DH:]], axis=1
            )
            made = both[:GROUP] + fdot(score[n * heads + h], lower)
            mout[rows, lanes] = made[:, :DH]
            oloc[rows, lanes] = made[:, DH:]
        return 0

    lax.fori_loop(0, groups // 2, one, 0)


def fold_hops(hops, h):
    state = hops[-1][h]
    for hop in hops[-2::-1]:
        state = hop[h, :, DH:] + fdot(hop[h, :, :DH], state)
    return state


def out_kernel(hop_count, tp, *refs):
    hops, refs = refs[:hop_count], refs[hop_count:]
    mout, oloc, gate, nh, wo, heads_out, att, send, keep, entry = refs
    heads = gate.shape[1] // DH
    states = [fold_hops(hops, h) for h in range(heads)]
    for h in range(heads):
        entry[h] = states[h]
    share = mout.shape[0] // 4
    for rel in range(4):
        rows = rows_of(tp[0] ^ rel, share)
        lows = []
        for h in range(heads):
            lanes = slice(h * DH, (h + 1) * DH)
            o = oloc[rows, lanes] + fdot(mout[rows, lanes], states[h])
            heads_out[rows, lanes] = o
            factor = lax.rsqrt(jnp.mean(o * o, axis=-1, keepdims=True) + head_epsilon)
            g = gate[rows, lanes]
            lows.append((o * factor * wide_gain(nh) * (g * jax.nn.sigmoid(g))).astype(bf16))
        low = jnp.concatenate(lows, axis=1)
        att[rows] = low
        part = dot(low, wo[...])
        if rel % 2:
            send[rel // 2] = part.astype(bf16)
        else:
            keep[rel // 2] = part


def states_kernel(entry, zst, qkv, wmix, umix, score, states, vnew, qeff):
    groups = qkv.shape[0] // GROUP
    heads = wmix.shape[1] // DH

    def one(i, _):
        for n, h in [(2 * i + j, h) for j in range(2) for h in range(heads)]:
            rows = pl.ds(pl.multiple_of(n * GROUP, GROUP), GROUP)
            lanes = slice(h * DH, (h + 1) * DH)
            at = n * heads + h
            s = zst[at, :, DH:] + fdot(zst[at, :, :DH], entry[h])
            states[at] = s
            w = wmix[rows, lanes]
            vnew[rows, lanes] = umix[rows, lanes] - fdot(w, s)
            qeff[rows, lanes] = qkv[rows, lanes] - fdot(score[at], w)
        return 0

    lax.fori_loop(0, groups // 2, one, 0)


def mid_kernel(x, kept, got, gain, residual, second):
    total = x[...].astype(f32) + kept[...] + got[...].astype(f32)
    residual[...] = total
    second[...] = rms_rows(total, wide_gain(gain)).astype(bf16)


def ffn_kernel(plans, tp, place, s0, s1, s2, s3, gdh, wgh, wuh, wdh, down_send, down_keep, send, keep, *refs):
    sums, (second, inner, dgate, dup, acc, wg, wu, grad_down, wd, sems) = refs[:-10], refs[-10:]
    loads = [
        pltpu.make_async_copy(src, dst, sems.at[i])
        for i, (src, dst) in enumerate(((wgh, wg), (wuh, wu), (gdh, grad_down), (wdh, wd)))
    ]
    for load in loads:
        load.start()
    share = s0.shape[0]
    for half, pair in enumerate(((s0, s1), (s2, s3))):
        sec = jnp.concatenate([pair[0][...], pair[1][...]], axis=0)
        blocks = [rows_of(tp[0] ^ (2 * half + j), share) for j in range(2)]
        if half == 0:
            loads[0].wait()
        gv = dot(sec, wg[...], 1, 1)
        if half == 0:
            loads[1].wait()
        uv = dot(sec, wu[...], 1, 1)
        if half == 0:
            loads[2].wait()
            loads[3].wait()
        gd = jnp.concatenate([grad_down[b] for b in blocks], axis=0)
        sig = jax.nn.sigmoid(gv)
        act = gv * sig
        inn = (act * uv).astype(bf16)
        gi = dot(gd, wd[...], 1, 1)
        dg = (gi * uv * (sig * (1.0 + gv * (1.0 - sig)))).astype(bf16)
        du = (gi * act).astype(bf16)
        for j, b in enumerate(blocks):
            part = slice(j * share, (j + 1) * share)
            second[b] = sec[part]
            inner[b] = inn[part]
            dgate[b] = dg[part]
            dup[b] = du[part]
        grad = dot(dg, wg[...]) + dot(du, wu[...])
        keep[half] = grad[:share]
        send[half] = grad[share:].astype(bf16)
        down = dot(inn, wd[...])
        down_keep[half] = down[:share]
        down_send[half] = down[share:].astype(bf16)
    for left, right, plan in ((inner, grad_down, 0), (dgate, second, 1), (dup, second, 2)):
        acc[...] = dot(left[...], right[...], 0, 0)
        put(acc, acc.shape[1], place[0], plans[plan], sums)


def turn_kernel(kept, got, residual, gain, grad_y, grad_residual, branch, gain_part):
    gs = kept[...] + got[...].astype(f32)
    v = residual[...]
    g = wide_gain(gain)
    r = lax.rsqrt(jnp.mean(v * v, axis=-1, keepdims=True) + row_epsilon)
    gain_part[...] = jnp.sum(gs * v * r, axis=0, keepdims=True)
    e = gs * g
    back = r * e - v * (r * r * r) * jnp.mean(e * v, axis=-1, keepdims=True)
    total = grad_y[...].astype(f32) + back
    grad_residual[...] = total
    branch[...] = total.astype(bf16)


def flow_kernel(tp, meta, b0, b1, b2, b3, wo, heads_out, gate, nh, qeff, amap, branch, dgate, dout, rst, dev, last, nh_part, flows):
    share = b0.shape[0]
    heads = gate.shape[1] // DH
    groups = gate.shape[0] // GROUP
    gains = jnp.zeros((1, DH), f32)
    for half, pair in enumerate(((b0, b1), (b2, b3))):
        both = jnp.concatenate([pair[0][...], pair[1][...]], axis=0)
        ga = dot(both, wo[...], 1, 1)
        for j in range(2):
            rows = rows_of(tp[0] ^ (2 * half + j), share)
            branch[rows] = pair[j][...]
            for h in range(heads):
                lanes = slice(h * DH, (h + 1) * DH)
                gz = ga[j * share : (j + 1) * share, lanes]
                o = heads_out[rows, lanes]
                g = gate[rows, lanes]
                gain = wide_gain(nh)
                r = lax.rsqrt(jnp.mean(o * o, axis=-1, keepdims=True) + head_epsilon)
                sig = jax.nn.sigmoid(g)
                act = g * sig
                e = gz * gain * act
                base = gz * o * r
                gains = gains + jnp.sum(base * act, axis=0, keepdims=True)
                dgate[rows, lanes] = (base * gain * (sig * (1.0 + g * (1.0 - sig)))).astype(bf16)
                dout[rows, lanes] = r * e - o * (r * r * r) * jnp.mean(e * o, axis=-1, keepdims=True)
    nh_part[...] = gains

    def local(i, _):
        for n, h in [(2 * i + j, h) for j in range(2) for h in range(heads)]:
            rows = pl.ds(pl.multiple_of(n * GROUP, GROUP), GROUP)
            lanes = slice(h * DH, (h + 1) * DH)
            flows[n * heads + h] = fdot(qeff[rows, lanes], dout[rows, lanes], 0, 0)
        return 0

    lax.fori_loop(0, groups // 2, local, 0)
    eye = (iota((DH, DH), 0) == iota((DH, DH), 1)).astype(f32)
    for h in range(heads):
        dev[h, :, :DH] = eye
        dev[h, :, DH:] = jnp.zeros((DH, DH), f32)

    def chain(i, _):
        n = groups - 1 - i
        keep = 1.0 - meta[0, n].astype(f32)
        for h in range(heads):
            at = n * heads + h
            later = dev[h]
            rst[at] = later
            moved = fdot(amap[at], later, 0, 0)
            dev[h, :, :DH] = moved[:, :DH] * keep
            dev[h, :, DH:] = (moved[:, DH:] + flows[at]) * keep
        return 0

    lax.fori_loop(0, groups, chain, 0)
    last[...] = dev[:, :, DH:]


def side_kernel(qkv, dout, vnew, states, score, ndo, dq, dk):
    heads = dout.shape[1] // DH
    groups = dout.shape[0] // GROUP
    lower = iota((GROUP, GROUP), 0) >= iota((GROUP, GROUP), 1)

    def one(i, _):
        for n, h in [(2 * i + j, h) for j in range(2) for h in range(heads)]:
            rows = pl.ds(pl.multiple_of(n * GROUP, GROUP), GROUP)
            lanes = slice(h * DH, (h + 1) * DH)
            at = n * heads + h
            q = qkv[rows, lanes]
            k = qkv[rows, (heads + h) * DH : (heads + h + 1) * DH]
            do = dout[rows, lanes]
            ndo[rows, lanes] = fdot(score[at], do, 0, 0)
            dn = jnp.where(lower, fdot(do, vnew[rows, lanes], 1, 1), 0.0)
            dq[rows, lanes] = fdot(do, states[at], 1, 1) + fdot(dn, k)
            dk[rows, lanes] = fdot(dn, q, 0, 0)
        return 0

    lax.fori_loop(0, groups // 2, one, 0)


def unit_back(a, grad):
    r = lax.rsqrt(jnp.sum(a * a, axis=-1, keepdims=True) + unit_epsilon)
    return r * grad - a * (r * r * r) * jnp.sum(a * grad, axis=-1, keepdims=True)


def back_kernel(hop_count, meta, *refs):
    hops, refs = refs[:hop_count], refs[hop_count:]
    rst, qkv, conv, cq, ck, cv, beta, inv, states, vnew, ndo, dq, dk1, dc, halo, dbeta = refs
    taps = tap_table(cq, ck, cv)
    heads = ndo.shape[1] // DH
    groups = ndo.shape[0] // GROUP
    total = ndo.shape[0]
    exits = [fold_hops(hops, h) for h in range(heads)]
    strict = iota((GROUP, GROUP), 0) > iota((GROUP, GROUP), 1)
    lane = iota((GROUP, LANES), 1)
    dc[total:] = jnp.zeros((8, dc.shape[1]), f32)

    def one(i, _):
        for j in range(2):
            n = 2 * i + j
            rows = pl.ds(pl.multiple_of(n * GROUP, GROUP), GROUP)
            raws = jnp.zeros((GROUP, LANES), f32)
            for h in range(heads):
                at = n * heads + h
                lanes = [slice((p * heads + h) * DH, (p * heads + h + 1) * DH) for p in range(3)]
                k = qkv[rows, lanes[1]]
                v = qkv[rows, lanes[2]]
                b, sig, live = beta_col(beta, meta, n, h)
                ds = rst[at, :, DH:] + gdot(rst[at, :, :DH], exits[h])
                dvn = ndo[rows, lanes[0]] + gdot(k, ds)
                d = gdot(inv[at], dvn, 0, 0)
                vn = vnew[rows, lanes[0]]
                both = gdot(d, jnp.concatenate([states[at], vn], axis=0), 1, 1)
                dstate = both[:, :DH]
                vds = gdot(vn, ds, 1, 1)
                da = jnp.where(strict, -both[:, DH:], 0.0)
                dak = gdot(da, k)
                datk = gdot(da, k * b, 0, 0)
                dk = dk1[rows, lanes[0]] + vds + b * (dak - dstate) + datk
                db = jnp.sum(d * v + (dak - dstate) * k, axis=-1, keepdims=True)
                db = jnp.where(live, db * sig * (1.0 - sig), 0.0)
                raws = jnp.where(lane == h, db, raws)
                grads = (dq[rows, lanes[0]], dk, d * b)
                for p in range(3):
                    c = conv[rows, lanes[p]]
                    s = jax.nn.sigmoid(c)
                    grad = unit_back(c * s, grads[p]) if p < 2 else grads[p]
                    dc[rows, lanes[p]] = grad * (s * (1.0 + c * (1.0 - s)))
            dbeta[rows] = raws.astype(bf16)
        return 0

    lax.fori_loop(0, groups // 2, one, 0)
    zero = jnp.zeros((8, DH), f32)
    for c in range(3 * heads):
        lanes = slice(c * DH, (c + 1) * DH)
        win = dc[0:8, lanes]
        acc = zero
        for d in range(1, KW):
            part = jnp.where(iota((8, 1), 0) < meta[0, 0] * d, 0.0, win)
            j = KW - 1 - d
            acc = acc + taps(j, c) * jnp.concatenate([zero, part], axis=0)[d : d + 8]
        halo[:, lanes] = acc


def taps_kernel(meta, dc, ext, cq, ck, cv, gp, last, dtaps):
    heads = cq.shape[1] // DH
    groups = gp.shape[0] // GROUP
    taps = tap_table(cq, ck, cv)
    dtaps[...] = jnp.zeros(dtaps.shape, f32)

    def masked(win, d, here, after):
        front = jnp.where(iota((GROUP, 1), 0) < here * d, 0.0, win[:GROUP])
        if after is None:
            return front
        back = jnp.where(iota((8, 1), 0) < after * d, 0.0, win[GROUP:])
        return jnp.concatenate([front, back], axis=0)

    def taps_back(n, _):
        base = pl.multiple_of(n * GROUP, GROUP)
        here = meta[0, n]
        after = meta[0, jnp.minimum(n + 1, groups - 1)]
        for c in range(3 * heads):
            lanes = slice(c * DH, (c + 1) * DH)
            win = dc[pl.ds(base, GROUP + 8), lanes]
            old = ext[pl.ds(pl.multiple_of(base + TAIL - 8, 8), GROUP + 8), lanes]
            acc = taps(KW - 1, c) * win[:GROUP]
            dtaps[KW - 1 : KW, lanes] += jnp.sum(win[:GROUP] * old[8:], axis=0, keepdims=True)
            for d in range(1, KW):
                part = masked(win, d, here, after)
                j = KW - 1 - d
                acc = acc + taps(j, c) * part[d : d + GROUP]
                dtaps[j : j + 1, lanes] += jnp.sum(
                    part[:GROUP] * old[8 - d : 8 - d + GROUP], axis=0, keepdims=True
                )
            gp[pl.ds(base, GROUP), lanes] = acc.astype(bf16)

            @pl.when(n == groups - 1)
            def _():
                last[:, lanes] = acc[GROUP - TAIL :]

        return 0

    lax.fori_loop(0, groups, taps_back, 0)


def hid_kernel(tp, gp_in, last, incoming, dgate, dbeta, wq, wk, wv, wg, wb, x, gp, send, keep, gain_part):
    total = gp.shape[0]
    width = wq.shape[1]
    gp[: total - TAIL] = gp_in[: total - TAIL]
    fixed = jnp.concatenate([last[: TAIL - 8], last[TAIL - 8 :] + incoming[...]], axis=0)
    gp[total - TAIL :] = fixed.astype(bf16)
    share = total // 4
    for half in range(2):
        blocks = [rows_of(tp[0] ^ (2 * half + j), share) for j in range(2)]
        cat = lambda ref: jnp.concatenate([ref[b] for b in blocks], axis=0)
        grads = cat(gp)
        acc = dot(cat(dgate), wg[...], 1, 1)
        small = cat(dbeta).astype(f32)
        for h in range(wb.shape[0]):
            acc = acc + small[:, h : h + 1] * wb[h : h + 1].astype(f32)
        for i, w in enumerate((wq, wk, wv)):
            acc = acc + dot(grads[:, i * width : (i + 1) * width], w[...], 1, 1)
        v = cat(x).astype(f32)
        r = lax.rsqrt(jnp.mean(v * v, axis=-1, keepdims=True) + row_epsilon)
        part = jnp.sum(acc * (v * r), axis=0, keepdims=True)
        gain_part[...] = part if half == 0 else gain_part[...] + part
        keep[half] = acc[:share]
        send[half] = acc[share:].astype(bf16)


def in_kernel(kept, got, x, gain, grad_residual, grad_in):
    gh = kept[...] + got[...].astype(f32)
    v = x[...].astype(f32)
    g = wide_gain(gain)
    r = lax.rsqrt(jnp.mean(v * v, axis=-1, keepdims=True) + row_epsilon)
    e = gh * g
    back = r * e - v * (r * r * r) * jnp.mean(e * v, axis=-1, keepdims=True)
    grad_in[...] = (grad_residual[...] + back).astype(bf16)


def outblock_kernel(tp, meta, kept, got, residual, out):
    total = residual[...] + kept[...] + got[...].astype(f32)
    live = live_mask(meta, tp[0], total.shape[0])
    out[...] = jnp.where(live, total, 0.0).astype(bf16)


def place_kernel(tp, a0, a1, a2, a3, out):
    for rel, part in enumerate((a0, a1, a2, a3)):
        out[rows_of(tp[0] ^ rel, part.shape[0])] = part[...].astype(out.dtype)


def swap(value, bit, axis="tp"):
    count = lax.axis_size(axis)
    return lax.ppermute(value, axis, [(i, i ^ bit) for i in range(count)])


def add_kernel(keep, got, kept, send):
    half = kept.shape[0]
    kept[...] = keep[:half] + got[:half].astype(f32)
    send[...] = (keep[half:] + got[half:].astype(f32)).astype(bf16)


def last_kernel(keep, got, own):
    own[...] = (keep[...] + got[...].astype(f32)).astype(bf16)


def pack_kernel(a, b, out):
    half = a.shape[0]
    out[:half] = a[...]
    out[half:] = b[...]


def fold(order, keep, got, name):
    half = (keep.shape[0] // 2, *keep.shape[1:])
    return order.run(add_kernel, name, [(half, f32), (half, bf16)], [keep, got])


def rank_of(m, bits):
    at = 0
    for bit in bits:
        at = 2 * at + ((m >> bit) & 1)
    return at


class Plan:
    def __init__(self, index, bits, base, size, start=0, folds=1, lane=0):
        self.index, self.bits, self.base, self.size = index, bits, base, size
        self.start, self.folds, self.lane = start, folds, lane


def put(acc, wide, place, plans, sums):
    for part in plans:
        keep, send = sums[2 * part.index : 2 * part.index + 2]
        height = part.size // part.folds
        for m in range(1 << len(part.bits)):
            at = rank_of(m, part.bits[1:])
            low = (m >> part.bits[0]) & 1
            for i in range(part.folds):
                begin = part.start + (m ^ place) * part.size + i * height
                block = acc[pl.ds(pl.multiple_of(begin, 8), height), part.lane : part.lane + wide]
                rows = slice(part.base, part.base + height)
                lanes = slice(i * wide, (i + 1) * wide)
                if low:
                    send[at, rows, lanes] = block.astype(bf16)
                else:
                    keep[at, rows, lanes] = block


def take(out, place, part, bits, near, far):
    height = part.size // part.folds
    wide = out.shape[1]
    for m in range(1 << len(bits)):
        source = far if (m >> bits[-1]) & 1 else near
        at = rank_of(m, bits[-2::-1])
        for i in range(part.folds):
            begin = part.start + (m ^ place) * part.size + i * height
            out[pl.ds(pl.multiple_of(begin, 8), height)] = source[
                at, part.base : part.base + height, i * wide : (i + 1) * wide
            ].astype(f32)


class Sum:
    def __init__(self, order, keep, send, scatter, gather, tag):
        self.order, self.tag, self.gather = order, tag, gather
        self.keep, self.left = keep, list(scatter)
        self.swap(send)
        self.own = self.near = None

    def swap(self, send):
        self.got = swap(send, 1 << self.left.pop(0), "seq")

    def step(self):
        order, tag = self.order, self.tag
        if self.own is None and self.left:
            self.keep, send = fold(order, self.keep, self.got, tag + "_fold")
            self.swap(send)
            return
        if self.own is None:
            (self.own,) = order.run(
                last_kernel, tag + "_last", [(self.keep.shape, bf16)], [self.keep, self.got]
            )
            more = 1 << len(self.gather)
            while more < lax.axis_size("seq"):
                other = swap(self.own, more, "seq")
                self.own = (self.own.astype(f32) + other.astype(f32)).astype(bf16)
                more *= 2
            self.left = list(self.gather)
        else:
            twice = (2 * self.own.shape[0], *self.own.shape[1:])
            (self.own,) = order.run(
                pack_kernel, tag + "_pack", [(twice, bf16)], [self.own, self.got]
            )
        self.swap(self.own)


def scatter_first(order, keep, send):
    return fold(order, keep, swap(send, 1), "fold_tp")


def grads_c_kernel(plans, place, hidden, gp, *refs):
    sums, acc = refs[:-1], refs[-1]
    acc[...] = dot(hidden[...], gp[...], 0, 0)
    put(acc, acc.shape[1] // 3, place[0], plans, sums)


def grads_d_kernel(plans, way, base, place, attended, branch, hidden, dgate, small, gains, keep, send, acc, acc2, both):
    sums = (keep, send)
    acc[...] = dot(attended[...], branch[...], 0, 0)
    put(acc, acc.shape[1], place[0], plans[:1], sums)
    acc2[...] = dot(hidden[...], dgate[...], 0, 0)
    put(acc2, acc2.shape[1], place[0], plans[1:], sums)
    both[...] = small[...] + gains[...]
    for m in range(1 << len(way)):
        line = both[pl.ds(m ^ place[0], 1)] + jnp.zeros((8, both.shape[1]), f32)
        at = rank_of(m, way[1:])
        if (m >> way[0]) & 1:
            send[at, base : base + 8] = line.astype(bf16)
        else:
            keep[at, base : base + 8] = line


def settle_kernel(jobs, line_at, place, *refs):
    count = 1 + max(part.index for parts in jobs for part, _ in parts)
    pairs, outs = refs[: 2 * count], refs[2 * count :]
    for parts, out in zip(jobs, outs):
        for part, way in parts:
            take(out, place[0], part, way, *pairs[2 * part.index : 2 * part.index + 2])
    if line_at is not None:
        index, way, base = line_at
        near, far = pairs[2 * index : 2 * index + 2]
        for m in range(1 << len(way)):
            source = far if (m >> way[-1]) & 1 else near
            at = rank_of(m, way[-2::-1])
            outs[-1][pl.ds(m ^ place[0], 1)] = source[at, base : base + 8].astype(f32)[:1]


def sum_shapes(blocks, rows, cols):
    return [((blocks // 2, rows, cols), f32), ((blocks // 2, rows, cols), bf16)]


def gather_rel(own):
    near = swap(own, 1)
    far = swap(own, 2)
    return own, near, far, swap(far, 1)


def shift(value, steps):
    count = lax.axis_size("seq")
    pairs = [(i, i + steps) for i in range(count) if 0 <= i + steps < count]
    return lax.ppermute(value, "seq", pairs)


def hops_of(dev, last, sign, reach):
    return [shift(dev, sign * k) for k in range(1, reach)] + [shift(last, sign * reach)]


def small_kernel(dtaps, dbeta, hidden, in_part, mid_part, head_part, local, gains):
    wide = dtaps.shape[1]
    local[...] = jnp.zeros(local.shape, f32)
    local[0:KW, :wide] = dtaps[...]
    local[KW : KW + 2] = dot(dbeta[...], hidden[...], 0, 0)[:2]
    gains[...] = jnp.zeros(gains.shape, f32)
    gains[KW + 2 : KW + 3] = in_part[...]
    gains[KW + 3 : KW + 4] = mid_part[...]
    gains[0:1, wide : wide + head_part.shape[1]] = head_part[...]


def plus_kernel(a, b, out):
    out[...] = a[...] + b[...]


def plus(order, a, b):
    return order.run(plus_kernel, "plus", [(a.shape, f32)], [a, b])[0]


def shards(
    layer_input,
    seq_groups,
    seq_pads,
    norm_in,
    w_query,
    w_key,
    w_value,
    conv_query,
    conv_key,
    conv_value,
    w_beta,
    w_gate_out,
    norm_head,
    w_out,
    norm_mid,
    w_gate,
    w_up,
    w_down,
    cotangent,
):
    total, model = layer_input.shape
    width = w_query.shape[1]
    heads = width // DH
    groups = total // GROUP
    share = total // 4
    ffw = w_gate.shape[1]
    seq_count = lax.axis_size("seq")
    reach = max(1, seq_count // 4)
    tp_rank = lax.axis_index("tp")
    tp = tp_rank.astype(jnp.int32).reshape(1)
    blocks = 8
    place = (lax.axis_index("seq") % blocks).astype(jnp.int32).reshape(1)
    first = (lax.axis_index("seq") * groups).astype(jnp.int32).reshape(1)
    taps = (conv_query, conv_key, conv_value)
    wb = w_beta.T
    tail = shift(layer_input[total - TAIL :], 1)
    chains = groups * heads
    wide = (total, width)
    mats = 2 * total * model
    order = Order()
    run = order.run

    def begin(keep, send, scatter, gather, tag):
        made = Sum(order, keep, send, scatter, gather, tag)
        made.place = place
        return made

    weight = pltpu.VMEM((model, width), bf16)
    rows = pltpu.VMEM((total, model), bf16)
    ext_shape = (total + TAIL, 3 * width)
    conv_shape = (total, 3 * width)
    inv_shape = (chains, GROUP, GROUP)
    map_shape = (chains, DH, DH)
    zst_shape = (chains, DH, 2 * DH)
    dev_shapes = [((heads, DH, 2 * DH), f32), ((heads, DH, DH), f32)]
    near = "near"
    far = "far"
    tp_sums = [((2, share, model), bf16), ((2, share, model), f32)]
    (
        gate_raw, beta_raw, meta, qkv, wmix, umix, score, zst, dev, last,
        hidden, grad_down, x_own, gd_own, ext, conv, inv, amap,
    ) = run(
        front_kernel,
        "front",
        [
            (wide, f32, near),
            ((total, heads), f32, near),
            ((2, groups), jnp.int32),
            (conv_shape, f32, near),
            (wide, f32, near),
            (wide, f32, near),
            (inv_shape, f32, near),
            (zst_shape, f32, near),
            *dev_shapes,
            ((total, model), bf16, far),
            ((total, model), bf16, far),
            ((share, model), bf16, far),
            ((share, model), bf16, far),
            (ext_shape, f32, far),
            (conv_shape, f32, far),
            (inv_shape, f32, far),
            (map_shape, f32, far),
        ],
        [first, tp, seq_groups, seq_pads, layer_input, cotangent, norm_in, w_query, w_key, w_value, w_gate_out, wb, tail, *taps],
        smem=(0, 1, 2, 3),
        smem_out=(2,),
        hbm=(4, 5, 7, 8, 9, 10),
        pin=(2, 3, 4, 5, 6, 7, 8, 9, 10, 11, 13, 14, 15),
        scratch=[
            rows, rows, weight, weight, weight, weight, rows, rows,
            pltpu.VMEM(ext_shape, f32),
            pltpu.VMEM(conv_shape, f32),
            pltpu.VMEM(inv_shape, f32),
            pltpu.VMEM(map_shape, f32),
            pltpu.VMEM(map_shape, f32),
            pltpu.SemaphoreType.DMA((6,)),
            pltpu.SemaphoreType.DMA((8,)),
        ],
        vmem=22,
    )
    hops = hops_of(dev, last, 1, reach)
    mout, oloc = run(
        local_kernel, "local", [(wide, f32, near)] * 2, [qkv, wmix, umix, score, zst]
    )
    heads_out, attended, send, keep, entry = run(
        lambda *r: out_kernel(reach, *r),
        "out",
        [(wide, f32, near), (wide, bf16, near), *tp_sums, ((heads, DH, DH), f32)],
        [tp, *hops, mout, oloc, gate_raw, norm_head, w_out],
        smem=(0,),
    )
    kept, cross = scatter_first(order, keep, send)
    got = swap(cross, 2)
    states, vnew, qeff = run(
        states_kernel,
        "states",
        [(map_shape, f32, near), (wide, f32, near), (wide, f32, near)],
        [entry, zst, qkv, wmix, umix, score],
    )
    residual, second_own = run(
        mid_kernel,
        "mid",
        [((share, model), f32, near), ((share, model), bf16)],
        [x_own, kept[0], got[0], norm_mid],
    )
    size = ffw // blocks
    ways = [
        ((0, 1, 2), (2, 1, 0)),
        ((1, 0, 2), (2, 0, 1)),
        ((0, 1, 2), (1, 2, 0)),
        ((1, 0, 2), (2, 0, 1)),
    ]
    near_up = size // 16 * 8
    far_up = size - near_up
    down_parts = [Plan(0, ways[0][0], 0, size)]
    gate_parts = [Plan(1, ways[1][0], 0, size)]
    up_parts = [
        Plan(0, ways[0][0], size, near_up),
        Plan(1, ways[1][0], size, far_up, start=near_up * blocks),
    ]
    plans_a = (down_parts, gate_parts, up_parts)
    f1_rows, f2_rows = size + near_up, size + far_up
    all_rows = gather_rel(second_own)
    down_send, down_keep, send, keep, *sums = run(
        lambda *r: ffn_kernel(plans_a, *r),
        "ffn",
        [*tp_sums, *tp_sums, *sum_shapes(blocks, f1_rows, model), *sum_shapes(blocks, f2_rows, model)],
        [tp, place, *all_rows, grad_down, w_gate.T, w_up.T, w_down],
        smem=(0, 1),
        hbm=(6, 7, 8, 9),
        pin=(6, 7, 8, 9),
        scratch=[
            rows,
            *[pltpu.VMEM((total, ffw), bf16)] * 3,
            pltpu.VMEM((ffw, model), f32),
            *[pltpu.VMEM((ffw, model), bf16)] * 2,
            rows,
            pltpu.VMEM((ffw, model), bf16),
            pltpu.SemaphoreType.DMA((4,)),
        ],
        vmem=28,
    )
    beside = swap(send, 1)
    f1 = begin(sums[0], sums[1], *ways[0], "f1")
    f2 = begin(sums[2], sums[3], *ways[1], "f2")
    kept, cross = fold(order, keep, beside, "fold_tp")
    got = swap(cross, 2)
    grad_residual, branch_own, mid_part = run(
        turn_kernel,
        "turn",
        [((share, model), f32), ((share, model), bf16), ((1, model), f32)],
        [kept[0], got[0], residual, norm_mid, gd_own],
    )
    branch_all = gather_rel(branch_own)
    branch, dgate_raw, dout, rst, dev, last, head_part = run(
        flow_kernel,
        "flow",
        [
            ((total, model), bf16),
            (wide, bf16),
            (wide, f32),
            (zst_shape, f32),
            *dev_shapes,
            ((1, DH), f32),
        ],
        [tp, meta, *branch_all, w_out, heads_out, gate_raw, norm_head, qeff, amap],
        smem=(0, 1),
        scratch=[pltpu.VMEM(map_shape, f32)],
    )
    hops = hops_of(dev, last, -1, reach)
    down_near = swap(down_send, 1)
    ndo, dq, dk = run(
        side_kernel,
        "side",
        [(wide, f32)] * 3,
        [qkv, dout, vnew, states, score],
    )
    down_kept, cross = fold(order, down_keep, down_near, "fold_tp")
    down_got = swap(cross, 2)
    order.wait(*hops)
    f1.step()
    f2.step()
    dc, halo, dbeta = run(
        lambda *r: back_kernel(reach, *r),
        "back",
        [((total + 8, 3 * width), f32), ((8, 3 * width), f32), ((total, LANES), bf16)],
        [meta, *hops, rst, qkv, conv, *taps, beta_raw, inv, states, vnew, ndo, dq, dk],
        smem=(0,),
    )
    incoming = shift(halo, -1)
    gp, last, dtaps = run(
        taps_kernel,
        "taps",
        [(conv_shape, bf16), ((TAIL, 3 * width), f32), ((KW, 3 * width), f32)],
        [meta, dc, ext, *taps],
        smem=(0,),
    )
    (out_own,) = run(
        outblock_kernel,
        "outblk",
        [((share, model), bf16)],
        [tp, meta, down_kept[0], down_got[0], residual],
        smem=(0, 1),
    )
    f1.step()
    f2.step()
    gp, send, keep, in_part = run(
        hid_kernel,
        "hid",
        [(conv_shape, bf16), *tp_sums, ((1, model), f32)],
        [tp, gp, last, incoming, dgate_raw, dbeta, w_query, w_key, w_value, w_gate_out, wb, layer_input],
        smem=(0,),
        vmem=12,
    )
    beside = swap(send, 1)
    piece = model // blocks
    fold_rows = piece * width // model
    split = dict(folds=model // width)
    plans_c = [
        Plan(0, ways[2][0], i * fold_rows, piece, lane=i * width, **split) for i in range(3)
    ]
    keep_c, send_c = run(
        lambda *r: grads_c_kernel(plans_c, *r),
        "grads_c",
        sum_shapes(blocks, 3 * fold_rows, model),
        [place, hidden, gp],
        smem=(0,),
        scratch=[pltpu.VMEM((model, 3 * width), f32)],
        vmem=16,
    )
    f3 = begin(keep_c, send_c, *ways[2], "f3")
    kept, cross = fold(order, keep, beside, "fold_tp")
    got = swap(cross, 2)
    row8 = ((8, model), f32)
    small, gains = run(
        small_kernel, "small", [row8, row8], [dtaps, dbeta, hidden, in_part, mid_part, head_part]
    )
    gains = plus(order, gains, swap(gains, 1))
    far_gains = swap(gains, 2)
    (grad_in_own,) = run(
        in_kernel,
        "inp",
        [((share, model), bf16)],
        [kept[0], got[0], x_own, norm_in, grad_residual],
    )
    grad_in_all = gather_rel(grad_in_own)
    gains = plus(order, gains, far_gains)
    wo_rows = width // blocks
    out_parts = [Plan(0, ways[3][0], 0, wo_rows)]
    gate_out_parts = [Plan(0, ways[3][0], wo_rows, piece, **split)]
    line_base = wo_rows + fold_rows
    keep_d, send_d = run(
        lambda *r: grads_d_kernel(out_parts + gate_out_parts, ways[3][0], line_base, *r),
        "grads_d",
        sum_shapes(blocks, line_base + 8, model),
        [place, attended, branch, hidden, dgate_raw, small, gains],
        smem=(0,),
        scratch=[
            pltpu.VMEM((width, model), f32),
            pltpu.VMEM((model, width), f32),
            pltpu.VMEM((8, model), f32),
        ],
        vmem=12,
    )
    f4 = begin(keep_d, send_d, *ways[3], "f4")
    f1.step()
    f2.step()
    f3.step()
    (grad_input,) = run(
        place_kernel,
        "place_in",
        [((total, model), f32)],
        [tp, *grad_in_all],
        smem=(0,),
    )
    out_all = gather_rel(out_own)
    f4.step()
    (block_out,) = run(
        place_kernel,
        "place_out",
        [((total, model), bf16)],
        [tp, *out_all],
        smem=(0,),
    )
    f1.step()
    f3.step()
    f4.step()
    f2.step()
    f2.step()
    f4.step()
    f3.step()
    f1.step()
    f4.step()
    f3.step()
    f4.step()
    f3.step()

    def settle(name, jobs, flows, outs, line_at=None):
        return run(
            lambda *r: settle_kernel(jobs, line_at, *r),
            name,
            [(o, f32) for o in outs],
            [place, *[a for flow in flows for a in (flow.own, flow.got)]],
            smem=(0,),
        )

    wayed = lambda parts, ways_of: [(part, ways_of[part.index][1]) for part in parts]
    (grad_down_w,) = settle("settle_1", [wayed(down_parts, ways)], [f1], [(ffw, model)])
    grad_gate_w, grad_up_w = settle(
        "settle_2",
        [wayed(gate_parts, ways), wayed(up_parts, ways)],
        [f1, f2],
        [(ffw, model)] * 2,
    )
    grad_out_w, grad_gate_out_w, small = settle(
        "settle_4",
        [wayed(out_parts, ways[3:]), wayed(gate_out_parts, ways[3:])],
        [f4],
        [(width, model), (model, width), (8, model)],
        line_at=(0, ways[3][1], line_base),
    )
    hidden_sums = settle(
        "settle_3", [wayed([part], ways[2:]) for part in plans_c], [f3], [(model, width)] * 3
    )
    cut = model // 4
    head_cut = DH // 4
    gain_of = lambda row, size, lane=0: lax.dynamic_slice(
        small, (row, lane + tp_rank * size), (1, size)
    ).reshape(size)
    tap_of = lambda i: small[:KW, i * width : (i + 1) * width]
    return (
        block_out,
        grad_input,
        gain_of(KW + 2, cut),
        hidden_sums[0],
        hidden_sums[1],
        hidden_sums[2],
        tap_of(0),
        tap_of(1),
        tap_of(2),
        small[KW : KW + heads].T,
        grad_gate_out_w,
        gain_of(0, head_cut, 3 * width),
        grad_out_w,
        gain_of(KW + 3, cut),
        grad_gate_w.T,
        grad_up_w.T,
        grad_down_w,
    )


def solution(mesh):
    rows = P("seq", None)
    cols = P(None, "tp")
    return jax.shard_map(
        shards,
        mesh=mesh,
        in_specs=(rows, P(), P(), P(), cols, cols, cols, cols, cols, cols, cols, cols, P(), P("tp", None), P(), cols, cols, P("tp", None), rows),
        out_specs=(rows, rows, P("tp"), cols, cols, cols, cols, cols, cols, cols, cols, P("tp"), P("tp", None), P("tp"), cols, cols, P("tp", None)),
        check_vma=False,
    )
```

```python
import jax
import jax.numpy as jnp
from jax import lax
from jax.experimental import pallas as pl
from jax.experimental.pallas import tpu as pltpu
from jax.sharding import PartitionSpec as P

DH = 128
KW = 4
GROUP = 64
TAIL = 16
LANES = 128

row_epsilon = 1e-06
head_epsilon = 1e-05
unit_epsilon = 1e-06
f32 = jnp.float32
bf16 = jnp.bfloat16


def dot(a, b, ca=1, cb=0):
    return lax.dot_general(a, b, (((ca,), (cb,)), ((), ())), preferred_element_type=f32)


def halves(a):
    high = a.astype(bf16)
    return high, (a - high.astype(f32)).astype(bf16)


def fdot(a, b, ca=1, cb=0):
    ah, al = halves(a)
    bh, bl = halves(b)
    return dot(
        jnp.concatenate([ah, al, ah], axis=ca), jnp.concatenate([bh, bh, bl], axis=cb), ca, cb
    )


def gdot(a, b, ca=1, cb=0):
    return dot(a.astype(bf16), b.astype(bf16), ca, cb)


def iota(shape, axis):
    return lax.broadcasted_iota(jnp.int32, shape, axis)


def rows_of(block, size):
    return pl.ds(pl.multiple_of(block * size, size), size)


COST = 1153500
STEPS = {'hops': ['f2', 'f1'], 'back': [], 'taps': ['f1', 'f2'], 'hid': [], 'x': [], 'tail': ['f3', 'f1', 'f2', 'in', 'f4', 'out', 'f1', 'f3', 'f4', 'f2', 'f2', 'f3', 'f1', 'f4', 'f4', 'f3', 'f3', 'f4', 's1', 's2', 's4', 's3']}
WAYS = {'f1': ((0, 1, 2), (2, 1, 0)), 'f2': ((1, 0, 2), (2, 0, 1)), 'f3': ((0, 1, 2), (1, 2, 0)), 'f4': ((1, 0, 2), (2, 0, 1))}


class Order:
    def __init__(self):
        self.last = None
        self.also = ()

    def wait(self, *values):
        self.also = values

    def run(self, kernel, name, outs, args, smem=(), smem_out=(), hbm=(), pin=(), scratch=(), flops=COST, vmem=8):
        held = {"far": pltpu.HBM, "near": pltpu.VMEM}
        shapes = [
            held[o[2]](o[0], o[1]) if len(o) > 2 else jax.ShapeDtypeStruct(*o) for o in outs
        ]
        hbm_out = [i for i, o in enumerate(outs) if o[2:] == ("far",)]
        args = list(args)
        if self.last is not None:
            free = [i for i in range(len(args)) if i not in smem]
            at = min(free, key=lambda i: (i in pin, i))
            args[at] = lax.optimization_barrier((args[at], self.last, *self.also))[0]
            self.also = ()
        for i in pin:
            args[i] = pltpu.with_memory_space_constraint(args[i], pltpu.HBM)
        space = lambda i, low, far: pltpu.SMEM if i in low else pltpu.HBM if i in far else pltpu.VMEM
        made = pl.pallas_call(
            kernel,
            name=name,
            out_shape=shapes,
            in_specs=[pl.BlockSpec(memory_space=space(i, smem, hbm)) for i in range(len(args))],
            out_specs=[
                pl.BlockSpec(memory_space=space(i, smem_out, hbm_out)) for i in range(len(outs))
            ],
            scratch_shapes=list(scratch),
            compiler_params=pltpu.CompilerParams(vmem_limit_bytes=vmem << 20),
            cost_estimate=pl.CostEstimate(flops=flops, bytes_accessed=1, transcendentals=0),
        )(*args)
        self.last = next(o for i, o in enumerate(made) if i not in smem_out and i not in hbm_out)
        return made


def wide_gain(ref):
    return ref[...].astype(f32).reshape(1, ref.shape[0])


def live_mask(meta, block, size):
    parts = size // GROUP
    row = iota((size, 1), 0)
    limit = jnp.full((size, 1), 0, jnp.int32) + meta[1, block * parts]
    for part in range(1, parts):
        limit = jnp.where(row >= part * GROUP, meta[1, block * parts + part] + part * GROUP, limit)
    return row < limit


def rms_rows(values, gain):
    factor = lax.rsqrt(jnp.mean(values * values, axis=-1, keepdims=True) + row_epsilon)
    return values * factor * gain


def beta_col(beta, meta, n, h):
    raw = beta[pl.ds(pl.multiple_of(n * GROUP, GROUP), GROUP), h : h + 1]
    sig = jax.nn.sigmoid(raw)
    live = iota((GROUP, 1), 0) < meta[1, n]
    return jnp.where(live, sig, 0.0), sig, live


def unit(rows):
    return rows * lax.rsqrt(jnp.sum(rows * rows, axis=-1, keepdims=True) + unit_epsilon)


def tri_inverse(systems, block=16):
    size = systems[0].shape[0]
    row = iota((size, size), 0)
    col = iota((size, size), 1)
    eye = (row == col).astype(f32)
    tiles = [[eye[r : r + 8] for r in range(0, size, 8)] for _ in systems]
    lower = [[system[r : r + 8] for r in range(0, size, 8)] for system in systems]
    for step in range(block - 1):
        for low, part in zip(lower, tiles):
            for start in range(0, size, block):
                j = start + step
                line = part[j // 8][j % 8 : j % 8 + 1]
                for r in range((j + 1) // 8, (start + block) // 8):
                    part[r] = part[r] - low[r][:, j : j + 1] * line
    inverses = [jnp.concatenate(part, axis=0) for part in tiles]
    while block < size:
        pick = ((row // block) % 2 == 1) & (col // block == row // block - 1)
        mids = [
            fdot(inverse, jnp.where(pick, system, 0.0))
            for inverse, system in zip(inverses, systems)
        ]
        inverses = [inverse - fdot(mid, inverse) for mid, inverse in zip(mids, inverses)]
        block *= 2
    return inverses


def tap_table(*tables):
    values = [table[...].astype(f32) for table in tables]
    parts = values[0].shape[1] // DH
    return lambda j, c: values[c // parts][j : j + 1, (c % parts) * DH : (c % parts + 1) * DH]


def front_kernel(first, tp, seq_groups, seq_pads, xh, coth, gain, wqh, wkh, wvh, wgh, wb, tail, cq, ck, cv, gate, beta, meta, qkv, wmix, umix, score, zst, dev, last, hidden_h, gd_h, x_own, gd_own, ext_h, conv_h, inv_h, amap_h, x, cot, wq, wk, wv, wg, hidden, gd, ext, conv, inv, amap, badd, sems, out_sems):
    loads = [
        pltpu.make_async_copy(src, dst, sems.at[i])
        for i, (src, dst) in enumerate(
            ((xh, x), (wqh, wq), (wkh, wk), (wvh, wv), (wgh, wg), (coth, cot))
        )
    ]
    for load in loads:
        load.start()
    groups = x.shape[0] // GROUP
    for n in range(groups):
        meta[0, n] = 0
        meta[1, n] = 0

    def one(s, start):
        count = seq_groups[s]
        length = count * GROUP - seq_pads[s]
        for n in range(groups):
            gid = first[0] * groups + n
            inside = (gid >= start) & (gid < start + count)
            here = jnp.clip(length - (gid - start) * GROUP, 0, GROUP)
            meta[0, n] = jnp.where(gid == start, 1, meta[0, n])
            meta[1, n] = jnp.where(inside, here, meta[1, n])
        return start + count

    lax.fori_loop(0, seq_groups.shape[0], one, jnp.int32(0))
    width = wq.shape[1]
    heads = width // DH
    tile = 256
    share = x_own.shape[0]
    scale = wide_gain(gain)
    own = rows_of(tp[0], share)
    stores = []

    def store(src, dst):
        copy = pltpu.make_async_copy(src, dst, out_sems.at[len(stores)])
        copy.start()
        stores.append(copy)

    loads[0].wait()
    store(x.at[own], x_own)
    tiles = [slice(t * tile, (t + 1) * tile) for t in range(x.shape[0] // tile)]
    for rows in tiles:
        hidden[rows] = rms_rows(x[rows].astype(f32), scale).astype(bf16)
    store(hidden, hidden_h)
    low = rms_rows(tail[...].astype(f32), scale).astype(bf16)
    for rows in tiles:
        beta[rows] = dot(hidden[rows], wb[...], 1, 1)
    for i, w in enumerate((wq, wk, wv, wg)):
        loads[1 + i].wait()
        lanes = slice(i * width, (i + 1) * width)
        for rows in tiles:
            got = dot(hidden[rows], w[...])
            if i < 3:
                ext[TAIL + rows.start : TAIL + rows.stop, lanes] = got
            else:
                gate[rows] = got
        if i < 3:
            ext[0:TAIL, lanes] = dot(low, w[...])
    store(ext, ext_h)
    loads[5].wait()
    for t, rows in enumerate(tiles):
        live = live_mask(meta, t, tile)
        gd[rows] = jnp.where(live, cot[rows].astype(f32), 0.0).astype(bf16)
    store(gd, gd_h)
    store(gd.at[own], gd_own)
    row = iota((GROUP, 1), 0)
    taps = tap_table(cq, ck, cv)

    def front(n):
        base = pl.multiple_of(n * GROUP, GROUP)
        for c in range(3 * heads):
            lanes = slice(c * DH, (c + 1) * DH)
            win = ext[pl.ds(pl.multiple_of(base + TAIL - 8, 8), GROUP + 8), lanes]
            acc = taps(KW - 1, c) * win[8:]
            for d in range(1, KW):
                part = jnp.where(row < meta[0, n] * d, 0.0, win[8 - d : 8 - d + GROUP])
                acc = acc + taps(KW - 1 - d, c) * part
            conv[pl.ds(base, GROUP), lanes] = acc
            acted = acc * jax.nn.sigmoid(acc)
            qkv[pl.ds(base, GROUP), lanes] = unit(acted) if c < 2 * heads else acted

    pl.loop(0, groups)(front)
    store(conv, conv_h)
    r64 = iota((GROUP, GROUP), 0)
    c64 = iota((GROUP, GROUP), 1)
    eye = (iota((DH, DH), 0) == iota((DH, DH), 1)).astype(f32)

    def load(n, h):
        rows = pl.ds(pl.multiple_of(n * GROUP, GROUP), GROUP)
        return [qkv[rows, (i * heads + h) * DH : (i * heads + h + 1) * DH] for i in range(3)]

    def local(i, _):
        chains = [(j, h) for j in range(groups) for h in range(heads)]
        systems = []
        kept = []
        for n, h in chains:
            q, k, v = load(n, h)
            b = beta_col(beta, meta, n, h)[0]
            both = fdot(jnp.concatenate([k * b, q], axis=0), k, 1, 1)
            systems.append(jnp.where(r64 > c64, both[:GROUP], 0.0))
            score[n * heads + h] = jnp.where(r64 >= c64, both[GROUP:], 0.0)
            kept.append((k, b, v))
        inverses = tri_inverse(systems)
        for (n, h), inverse, (k, b, v) in zip(chains, inverses, kept):
            rows = pl.ds(pl.multiple_of(n * GROUP, GROUP), GROUP)
            inv[n * heads + h] = inverse
            wu = fdot(inverse, jnp.concatenate([k * b, v * b], axis=1))
            wmix[rows, h * DH : (h + 1) * DH] = wu[:, :DH]
            umix[rows, h * DH : (h + 1) * DH] = wu[:, DH:]
            kwu = fdot(k, wu, 0, 0)
            amap[n * heads + h] = eye - kwu[:, :DH]
            badd[n * heads + h] = kwu[:, DH:]
        return 0

    local(0, 0)
    store(inv, inv_h)
    store(amap, amap_h)
    for h in range(heads):
        dev[h, :, :DH] = eye
        dev[h, :, DH:] = jnp.zeros((DH, DH), f32)

    def chain(n, _):
        keep = 1.0 - meta[0, n].astype(f32)
        for h in range(heads):
            start = dev[h] * keep
            zst[n * heads + h] = start
            moved = fdot(amap[n * heads + h], start)
            dev[h, :, :DH] = moved[:, :DH]
            dev[h, :, DH:] = moved[:, DH:] + badd[n * heads + h]
        return 0

    lax.fori_loop(0, groups, chain, 0)
    last[...] = dev[:, :, DH:]

    for copy in stores:
        copy.wait()


def local_kernel(qkv, wmix, umix, score, zst, mout, oloc):
    groups = qkv.shape[0] // GROUP
    heads = wmix.shape[1] // DH

    def one(i, _):
        for n, h in [(2 * i + j, h) for j in range(2) for h in range(heads)]:
            rows = pl.ds(pl.multiple_of(n * GROUP, GROUP), GROUP)
            lanes = slice(h * DH, (h + 1) * DH)
            q = qkv[rows, lanes]
            both = fdot(jnp.concatenate([q, wmix[rows, lanes]], axis=0), zst[n * heads + h])
            lower = jnp.concatenate(
                [-both[GROUP:, :DH], umix[rows, lanes] - both[GROUP:, DH:]], axis=1
            )
            made = both[:GROUP] + fdot(score[n * heads + h], lower)
            mout[rows, lanes] = made[:, :DH]
            oloc[rows, lanes] = made[:, DH:]
        return 0

    lax.fori_loop(0, groups // 2, one, 0)


def fold_hops(hops, h):
    state = hops[-1][h]
    for hop in hops[-2::-1]:
        state = hop[h, :, DH:] + fdot(hop[h, :, :DH], state)
    return state


def out_kernel(hop_count, tp, *refs):
    hops, refs = refs[:hop_count], refs[hop_count:]
    mout, oloc, gate, nh, wo, heads_out, att, send, keep, entry = refs
    heads = gate.shape[1] // DH
    states = [fold_hops(hops, h) for h in range(heads)]
    for h in range(heads):
        entry[h] = states[h]
    share = mout.shape[0] // 4
    for rel in range(4):
        rows = rows_of(tp[0] ^ rel, share)
        lows = []
        for h in range(heads):
            lanes = slice(h * DH, (h + 1) * DH)
            o = oloc[rows, lanes] + fdot(mout[rows, lanes], states[h])
            heads_out[rows, lanes] = o
            factor = lax.rsqrt(jnp.mean(o * o, axis=-1, keepdims=True) + head_epsilon)
            g = gate[rows, lanes]
            lows.append((o * factor * wide_gain(nh) * (g * jax.nn.sigmoid(g))).astype(bf16))
        low = jnp.concatenate(lows, axis=1)
        att[rows] = low
        part = dot(low, wo[...])
        if rel % 2:
            send[rel // 2] = part.astype(bf16)
        else:
            keep[rel // 2] = part


def states_kernel(entry, zst, qkv, wmix, umix, score, states, vnew, qeff):
    groups = qkv.shape[0] // GROUP
    heads = wmix.shape[1] // DH

    def one(i, _):
        for n, h in [(2 * i + j, h) for j in range(2) for h in range(heads)]:
            rows = pl.ds(pl.multiple_of(n * GROUP, GROUP), GROUP)
            lanes = slice(h * DH, (h + 1) * DH)
            at = n * heads + h
            s = zst[at, :, DH:] + fdot(zst[at, :, :DH], entry[h])
            states[at] = s
            w = wmix[rows, lanes]
            vnew[rows, lanes] = umix[rows, lanes] - fdot(w, s)
            qeff[rows, lanes] = qkv[rows, lanes] - fdot(score[at], w)
        return 0

    lax.fori_loop(0, groups // 2, one, 0)


def mid_kernel(x, kept, got, gain, residual, second):
    total = x[...].astype(f32) + kept[...] + got[...].astype(f32)
    residual[...] = total
    second[...] = rms_rows(total, wide_gain(gain)).astype(bf16)


def warm_kernel(wgh, wuh, wdh, gdh, wg, wu, wd, gd, grad_inner, sems):
    loads = [
        pltpu.make_async_copy(src, dst, sems.at[i])
        for i, (src, dst) in enumerate(((wdh, wd), (gdh, gd), (wgh, wg), (wuh, wu)))
    ]
    for load in loads:
        load.start()
    loads[0].wait()
    loads[1].wait()
    tile = 256
    for t in range(gd.shape[0] // tile):
        rows = slice(t * tile, (t + 1) * tile)
        grad_inner[rows] = dot(gd[rows], wd[...], 1, 1)
    loads[2].wait()
    loads[3].wait()


def ffn_half(tp, half, sa, sb, wg, wu, wd, grad_inner, sec, inner, dgate, dup, down_keep, down_send, keep, send):
    share = sa.shape[0]
    sec[:share] = sa[...]
    sec[share:] = sb[...]
    gv = dot(sec[...], wg[...], 1, 1)
    uv = dot(sec[...], wu[...], 1, 1)
    sig = jax.nn.sigmoid(gv)
    act = gv * sig
    inn = (act * uv).astype(bf16)
    gi = jnp.concatenate(
        [grad_inner[rows_of(tp[0] ^ (2 * half + j), share)] for j in range(2)], axis=0
    )
    dg = (gi * uv * (sig * (1.0 + gv * (1.0 - sig)))).astype(bf16)
    du = (gi * act).astype(bf16)
    inner[...] = inn
    dgate[...] = dg
    dup[...] = du
    grad = dot(dg, wg[...]) + dot(du, wu[...])
    keep[0] = grad[:share]
    send[0] = grad[share:].astype(bf16)
    down = dot(inn, wd[...])
    down_keep[0] = down[:share]
    down_send[0] = down[share:].astype(bf16)


def ffn_a_kernel(tp, sa, sb, wg, wu, wd, grad_inner, *outs):
    ffn_half(tp, 0, sa, sb, wg, wu, wd, grad_inner, *outs)


def ffn_b_kernel(plans, tp, place, sa, sb, wg, wu, wd, grad_inner, gd, sec_a, inner_a, dgate_a, dup_a, down_keep, down_send, keep, send, *refs):
    sums, (sec, inner, dgate, dup, acc) = refs[:-5], refs[-5:]
    share = sa.shape[0]
    ffn_half(tp, 1, sa, sb, wg, wu, wd, grad_inner, sec, inner, dgate, dup, down_keep, down_send, keep, send)
    near = [jnp.concatenate([gd[rows_of(tp[0] ^ (2 * i + j), share)] for j in range(2)], axis=0) for i in range(2)]
    for pair, plan in (
        (((inner_a[...], near[0]), (inner[...], near[1])), 0),
        (((dgate_a[...], sec_a[...]), (dgate[...], sec[...])), 1),
        (((dup_a[...], sec_a[...]), (dup[...], sec[...])), 2),
    ):
        acc[...] = dot(*pair[0], 0, 0) + dot(*pair[1], 0, 0)
        put(acc, acc.shape[1], (place[0] & 7), plans[plan], sums)


def turn_kernel(kept, got, residual, gain, grad_y, grad_residual, branch, gain_part):
    gs = kept[...] + got[...].astype(f32)
    v = residual[...]
    g = wide_gain(gain)
    r = lax.rsqrt(jnp.mean(v * v, axis=-1, keepdims=True) + row_epsilon)
    gain_part[...] = jnp.sum(gs * v * r, axis=0, keepdims=True)
    e = gs * g
    back = r * e - v * (r * r * r) * jnp.mean(e * v, axis=-1, keepdims=True)
    total = grad_y[...].astype(f32) + back
    grad_residual[...] = total
    branch[...] = total.astype(bf16)


def flow_kernel(tp, meta, b0, b1, b2, b3, wo, heads_out, gate, nh, qeff, amap, branch, dgate, dout, rst, dev, last, nh_part, flows):
    share = b0.shape[0]
    heads = gate.shape[1] // DH
    groups = gate.shape[0] // GROUP
    gains = jnp.zeros((1, DH), f32)
    for half, pair in enumerate(((b0, b1), (b2, b3))):
        both = jnp.concatenate([pair[0][...], pair[1][...]], axis=0)
        ga = dot(both, wo[...], 1, 1)
        for j in range(2):
            rows = rows_of(tp[0] ^ (2 * half + j), share)
            branch[rows] = pair[j][...]
            for h in range(heads):
                lanes = slice(h * DH, (h + 1) * DH)
                gz = ga[j * share : (j + 1) * share, lanes]
                o = heads_out[rows, lanes]
                g = gate[rows, lanes]
                gain = wide_gain(nh)
                r = lax.rsqrt(jnp.mean(o * o, axis=-1, keepdims=True) + head_epsilon)
                sig = jax.nn.sigmoid(g)
                act = g * sig
                e = gz * gain * act
                base = gz * o * r
                gains = gains + jnp.sum(base * act, axis=0, keepdims=True)
                dgate[rows, lanes] = (base * gain * (sig * (1.0 + g * (1.0 - sig)))).astype(bf16)
                dout[rows, lanes] = r * e - o * (r * r * r) * jnp.mean(e * o, axis=-1, keepdims=True)
    nh_part[...] = gains

    def local(i, _):
        for n, h in [(2 * i + j, h) for j in range(2) for h in range(heads)]:
            rows = pl.ds(pl.multiple_of(n * GROUP, GROUP), GROUP)
            lanes = slice(h * DH, (h + 1) * DH)
            flows[n * heads + h] = fdot(qeff[rows, lanes], dout[rows, lanes], 0, 0)
        return 0

    lax.fori_loop(0, groups // 2, local, 0)
    eye = (iota((DH, DH), 0) == iota((DH, DH), 1)).astype(f32)
    for h in range(heads):
        dev[h, :, :DH] = eye
        dev[h, :, DH:] = jnp.zeros((DH, DH), f32)

    def chain(i, _):
        n = groups - 1 - i
        keep = 1.0 - meta[0, n].astype(f32)
        for h in range(heads):
            at = n * heads + h
            later = dev[h]
            rst[at] = later
            moved = fdot(amap[at], later, 0, 0)
            dev[h, :, :DH] = moved[:, :DH] * keep
            dev[h, :, DH:] = (moved[:, DH:] + flows[at]) * keep
        return 0

    lax.fori_loop(0, groups, chain, 0)
    last[...] = dev[:, :, DH:]


def side_kernel(qkv, dout, vnew, states, score, ndo, dq, dk):
    heads = dout.shape[1] // DH
    groups = dout.shape[0] // GROUP
    lower = iota((GROUP, GROUP), 0) >= iota((GROUP, GROUP), 1)

    def one(i, _):
        for n, h in [(2 * i + j, h) for j in range(2) for h in range(heads)]:
            rows = pl.ds(pl.multiple_of(n * GROUP, GROUP), GROUP)
            lanes = slice(h * DH, (h + 1) * DH)
            at = n * heads + h
            q = qkv[rows, lanes]
            k = qkv[rows, (heads + h) * DH : (heads + h + 1) * DH]
            do = dout[rows, lanes]
            ndo[rows, lanes] = fdot(score[at], do, 0, 0)
            dn = jnp.where(lower, fdot(do, vnew[rows, lanes], 1, 1), 0.0)
            dq[rows, lanes] = fdot(do, states[at], 1, 1) + fdot(dn, k)
            dk[rows, lanes] = fdot(dn, q, 0, 0)
        return 0

    lax.fori_loop(0, groups // 2, one, 0)


def unit_back(a, grad):
    r = lax.rsqrt(jnp.sum(a * a, axis=-1, keepdims=True) + unit_epsilon)
    return r * grad - a * (r * r * r) * jnp.sum(a * grad, axis=-1, keepdims=True)


def back_kernel(hop_count, meta, *refs):
    hops, refs = refs[:hop_count], refs[hop_count:]
    rst, qkv, conv, cq, ck, cv, beta, inv, states, vnew, ndo, dq, dk1, dc, halo, dbeta = refs
    taps = tap_table(cq, ck, cv)
    heads = ndo.shape[1] // DH
    groups = ndo.shape[0] // GROUP
    total = ndo.shape[0]
    exits = [fold_hops(hops, h) for h in range(heads)]
    strict = iota((GROUP, GROUP), 0) > iota((GROUP, GROUP), 1)
    lane = iota((GROUP, LANES), 1)
    dc[total:] = jnp.zeros((8, dc.shape[1]), f32)

    def one(i, _):
        for j in range(2):
            n = 2 * i + j
            rows = pl.ds(pl.multiple_of(n * GROUP, GROUP), GROUP)
            raws = jnp.zeros((GROUP, LANES), f32)
            for h in range(heads):
                at = n * heads + h
                lanes = [slice((p * heads + h) * DH, (p * heads + h + 1) * DH) for p in range(3)]
                k = qkv[rows, lanes[1]]
                v = qkv[rows, lanes[2]]
                b, sig, live = beta_col(beta, meta, n, h)
                ds = rst[at, :, DH:] + gdot(rst[at, :, :DH], exits[h])
                dvn = ndo[rows, lanes[0]] + gdot(k, ds)
                d = gdot(inv[at], dvn, 0, 0)
                vn = vnew[rows, lanes[0]]
                both = gdot(d, jnp.concatenate([states[at], vn], axis=0), 1, 1)
                dstate = both[:, :DH]
                vds = gdot(vn, ds, 1, 1)
                da = jnp.where(strict, -both[:, DH:], 0.0)
                dak = gdot(da, k)
                datk = gdot(da, k * b, 0, 0)
                dk = dk1[rows, lanes[0]] + vds + b * (dak - dstate) + datk
                db = jnp.sum(d * v + (dak - dstate) * k, axis=-1, keepdims=True)
                db = jnp.where(live, db * sig * (1.0 - sig), 0.0)
                raws = jnp.where(lane == h, db, raws)
                grads = (dq[rows, lanes[0]], dk, d * b)
                for p in range(3):
                    c = conv[rows, lanes[p]]
                    s = jax.nn.sigmoid(c)
                    grad = unit_back(c * s, grads[p]) if p < 2 else grads[p]
                    dc[rows, lanes[p]] = grad * (s * (1.0 + c * (1.0 - s)))
            dbeta[rows] = raws.astype(bf16)
        return 0

    lax.fori_loop(0, groups // 2, one, 0)
    zero = jnp.zeros((8, DH), f32)
    for c in range(3 * heads):
        lanes = slice(c * DH, (c + 1) * DH)
        win = dc[0:8, lanes]
        acc = zero
        for d in range(1, KW):
            part = jnp.where(iota((8, 1), 0) < meta[0, 0] * d, 0.0, win)
            j = KW - 1 - d
            acc = acc + taps(j, c) * jnp.concatenate([zero, part], axis=0)[d : d + 8]
        halo[:, lanes] = acc


def taps_kernel(meta, dc, ext, cq, ck, cv, gp, last, dtaps):
    heads = cq.shape[1] // DH
    groups = gp.shape[0] // GROUP
    taps = tap_table(cq, ck, cv)
    dtaps[...] = jnp.zeros(dtaps.shape, f32)

    def masked(win, d, here, after):
        front = jnp.where(iota((GROUP, 1), 0) < here * d, 0.0, win[:GROUP])
        if after is None:
            return front
        back = jnp.where(iota((8, 1), 0) < after * d, 0.0, win[GROUP:])
        return jnp.concatenate([front, back], axis=0)

    def taps_back(n, _):
        base = pl.multiple_of(n * GROUP, GROUP)
        here = meta[0, n]
        after = meta[0, jnp.minimum(n + 1, groups - 1)]
        for c in range(3 * heads):
            lanes = slice(c * DH, (c + 1) * DH)
            win = dc[pl.ds(base, GROUP + 8), lanes]
            old = ext[pl.ds(pl.multiple_of(base + TAIL - 8, 8), GROUP + 8), lanes]
            acc = taps(KW - 1, c) * win[:GROUP]
            dtaps[KW - 1 : KW, lanes] += jnp.sum(win[:GROUP] * old[8:], axis=0, keepdims=True)
            for d in range(1, KW):
                part = masked(win, d, here, after)
                j = KW - 1 - d
                acc = acc + taps(j, c) * part[d : d + GROUP]
                dtaps[j : j + 1, lanes] += jnp.sum(
                    part[:GROUP] * old[8 - d : 8 - d + GROUP], axis=0, keepdims=True
                )
            gp[pl.ds(base, GROUP), lanes] = acc.astype(bf16)

            @pl.when(n == groups - 1)
            def _():
                last[:, lanes] = acc[GROUP - TAIL :]

        return 0

    lax.fori_loop(0, groups, taps_back, 0)


def hid_kernel(tp, gp_in, last, incoming, dgate, dbeta, wq, wk, wv, wg, wb, x, gp, send, keep, gain_part):
    total = gp.shape[0]
    width = wq.shape[1]
    gp[: total - TAIL] = gp_in[: total - TAIL]
    fixed = jnp.concatenate([last[: TAIL - 8], last[TAIL - 8 :] + incoming[...]], axis=0)
    gp[total - TAIL :] = fixed.astype(bf16)
    share = total // 4
    for half in range(2):
        blocks = [rows_of(tp[0] ^ (2 * half + j), share) for j in range(2)]
        cat = lambda ref: jnp.concatenate([ref[b] for b in blocks], axis=0)
        grads = cat(gp)
        acc = dot(cat(dgate), wg[...], 1, 1)
        small = cat(dbeta).astype(f32)
        for h in range(wb.shape[0]):
            acc = acc + small[:, h : h + 1] * wb[h : h + 1].astype(f32)
        for i, w in enumerate((wq, wk, wv)):
            acc = acc + dot(grads[:, i * width : (i + 1) * width], w[...], 1, 1)
        v = cat(x).astype(f32)
        r = lax.rsqrt(jnp.mean(v * v, axis=-1, keepdims=True) + row_epsilon)
        part = jnp.sum(acc * (v * r), axis=0, keepdims=True)
        gain_part[...] = part if half == 0 else gain_part[...] + part
        keep[half] = acc[:share]
        send[half] = acc[share:].astype(bf16)


def in_kernel(kept, got, x, gain, grad_residual, grad_in):
    gh = kept[...] + got[...].astype(f32)
    v = x[...].astype(f32)
    g = wide_gain(gain)
    r = lax.rsqrt(jnp.mean(v * v, axis=-1, keepdims=True) + row_epsilon)
    e = gh * g
    back = r * e - v * (r * r * r) * jnp.mean(e * v, axis=-1, keepdims=True)
    grad_in[...] = (grad_residual[...] + back).astype(bf16)


def outblock_kernel(tp, meta, kept, got, residual, out):
    total = residual[...] + kept[...] + got[...].astype(f32)
    live = live_mask(meta, tp[0], total.shape[0])
    out[...] = jnp.where(live, total, 0.0).astype(bf16)


def place_kernel(tp, a0, a1, a2, a3, out):
    for rel, part in enumerate((a0, a1, a2, a3)):
        out[rows_of(tp[0] ^ rel, part.shape[0])] = part[...].astype(out.dtype)


def swap(value, bit, axis="tp"):
    count = lax.axis_size(axis)
    return lax.ppermute(value, axis, [(i, i ^ bit) for i in range(count)])


def add_kernel(keep, got, kept, send):
    half = kept.shape[0]
    kept[...] = keep[:half] + got[:half].astype(f32)
    send[...] = (keep[half:] + got[half:].astype(f32)).astype(bf16)


def last_kernel(keep, got, own):
    own[...] = (keep[...] + got[...].astype(f32)).astype(bf16)


def pack_kernel(a, b, out):
    half = a.shape[0]
    out[:half] = a[...]
    out[half:] = b[...]


def fold(order, keep, got, name):
    half = (keep.shape[0] // 2, *keep.shape[1:])
    return order.run(add_kernel, name, [(half, f32), (half, bf16)], [keep, got])


def rank_of(m, bits):
    at = 0
    for bit in bits:
        at = 2 * at + ((m >> bit) & 1)
    return at


class Plan:
    def __init__(self, index, bits, base, size, start=0, folds=1, lane=0):
        self.index, self.bits, self.base, self.size = index, bits, base, size
        self.start, self.folds, self.lane = start, folds, lane

    def rest(self):
        return self.bits, self.base, self.size, self.start, self.folds, self.lane


def put(acc, wide, place, plans, sums):
    for part in plans:
        keep, send = sums[2 * part.index : 2 * part.index + 2]
        height = part.size // part.folds
        for m in range(1 << len(part.bits)):
            at = rank_of(m, part.bits[1:])
            low = (m >> part.bits[0]) & 1
            for i in range(part.folds):
                begin = part.start + (m ^ place) * part.size + i * height
                block = acc[pl.ds(pl.multiple_of(begin, 8), height), part.lane : part.lane + wide]
                rows = slice(part.base, part.base + height)
                lanes = slice(i * wide, (i + 1) * wide)
                if low:
                    send[at, rows, lanes] = block.astype(bf16)
                else:
                    keep[at, rows, lanes] = block


def take(out, place, part, bits, near, far):
    height = part.size // part.folds
    wide = out.shape[1]
    for m in range(1 << len(bits)):
        source = far if (m >> bits[-1]) & 1 else near
        at = rank_of(m, bits[-2::-1])
        for i in range(part.folds):
            begin = part.start + (m ^ place) * part.size + i * height
            out[pl.ds(pl.multiple_of(begin, 8), height)] = source[
                at, part.base : part.base + height, i * wide : (i + 1) * wide
            ].astype(f32)


class Sum:
    def __init__(self, order, keep, send, scatter, gather, tag):
        self.order, self.tag, self.gather = order, tag, gather
        self.keep, self.left = keep, list(scatter)
        self.swap(send)
        self.own = self.near = None

    def swap(self, send):
        self.got = swap(send, 1 << self.left.pop(0), "seq")

    def step(self):
        order, tag = self.order, self.tag
        if self.own is None and self.left:
            self.keep, send = fold(order, self.keep, self.got, tag + "_fold")
            self.swap(send)
            return
        if self.own is None:
            (self.own,) = order.run(
                last_kernel, tag + "_last", [(self.keep.shape, bf16)], [self.keep, self.got]
            )
            more = 1 << len(self.gather)
            while more < lax.axis_size("seq"):
                other = swap(self.own, more, "seq")
                self.own = (self.own.astype(f32) + other.astype(f32)).astype(bf16)
                more *= 2
            self.left = list(self.gather)
        else:
            twice = (2 * self.own.shape[0], *self.own.shape[1:])
            (self.own,) = order.run(
                pack_kernel, tag + "_pack", [(twice, bf16)], [self.own, self.got]
            )
        self.swap(self.own)


def pair_kernel(keep_a, got_a, keep_b, got_b, kept, send):
    kept[...] = keep_a[...] + got_a[...].astype(f32)
    send[...] = (keep_b[...] + got_b[...].astype(f32)).astype(bf16)


def fold_pair(order, keep_a, got_a, keep_b, got_b):
    shape = keep_a.shape
    return order.run(
        pair_kernel, "fold_tp", [(shape, f32), (shape, bf16)], [keep_a, got_a, keep_b, got_b]
    )


def scatter_first(order, keep, send):
    return fold(order, keep, swap(send, 1), "fold_tp")


def grads_c_kernel(plans, place, hidden, gp, *refs):
    sums, acc = refs[:-1], refs[-1]
    acc[...] = dot(hidden[...], gp[...], 0, 0)
    put(acc, acc.shape[1] // 3, (place[0] & 7), plans, sums)


def grads_d_kernel(plans, way, base, place, attended, branch, hidden, dgate, small, gains, keep, send, acc, acc2, both):
    sums = (keep, send)
    acc[...] = dot(attended[...], branch[...], 0, 0)
    put(acc, acc.shape[1], (place[0] & 7), plans[:1], sums)
    acc2[...] = dot(hidden[...], dgate[...], 0, 0)
    put(acc2, acc2.shape[1], (place[0] & 7), plans[1:], sums)
    both[...] = small[...] + gains[...]
    for m in range(1 << len(way)):
        line = both[pl.ds(m ^ (place[0] & 7), 1)] + jnp.zeros((8, both.shape[1]), f32)
        at = rank_of(m, way[1:])
        if (m >> way[0]) & 1:
            send[at, base : base + 8] = line.astype(bf16)
        else:
            keep[at, base : base + 8] = line


def settle_kernel(count, jobs, line_at, place, *refs):
    pairs, outs = refs[: 2 * count], refs[2 * count :]
    for parts, out in zip(jobs, outs):
        for part, way in parts:
            take(out, (place[0] & 7), part, way, *pairs[2 * part.index : 2 * part.index + 2])
    if line_at is not None:
        index, way, base = line_at
        near, far = pairs[2 * index : 2 * index + 2]
        for m in range(1 << len(way)):
            source = far if (m >> way[-1]) & 1 else near
            at = rank_of(m, way[-2::-1])
            outs[-1][pl.ds(m ^ (place[0] & 7), 1)] = source[at, base : base + 8].astype(f32)[:1]


def sum_shapes(blocks, rows, cols):
    return [((blocks // 2, rows, cols), f32), ((blocks // 2, rows, cols), bf16)]


def gather_rel(own):
    near = swap(own, 1)
    far = swap(own, 2)
    return own, near, far, swap(far, 1)


def shift(value, steps):
    count = lax.axis_size("seq")
    pairs = [(i, i + steps) for i in range(count) if 0 <= i + steps < count]
    return lax.ppermute(value, "seq", pairs)


def hops_of(dev, last, sign, reach):
    return [shift(dev, sign * k) for k in range(1, reach)] + [shift(last, sign * reach)]


def small_kernel(dtaps, dbeta, hidden, in_part, mid_part, head_part, local, gains):
    wide = dtaps.shape[1]
    local[...] = jnp.zeros(local.shape, f32)
    local[0:KW, :wide] = dtaps[...]
    local[KW : KW + 2] = dot(dbeta[...], hidden[...], 0, 0)[:2]
    gains[...] = jnp.zeros(gains.shape, f32)
    gains[KW + 2 : KW + 3] = in_part[...]
    gains[KW + 3 : KW + 4] = mid_part[...]
    gains[0:1, wide : wide + head_part.shape[1]] = head_part[...]


def plus_kernel(a, b, out):
    out[...] = a[...] + b[...]


def plus(order, a, b):
    return order.run(plus_kernel, "plus", [(a.shape, f32)], [a, b])[0]


def shards(
    layer_input,
    seq_groups,
    seq_pads,
    norm_in,
    w_query,
    w_key,
    w_value,
    conv_query,
    conv_key,
    conv_value,
    w_beta,
    w_gate_out,
    norm_head,
    w_out,
    norm_mid,
    w_gate,
    w_up,
    w_down,
    cotangent,
):
    total, model = layer_input.shape
    width = w_query.shape[1]
    heads = width // DH
    groups = total // GROUP
    share = total // 4
    ffw = w_gate.shape[1]
    seq_count = lax.axis_size("seq")
    reach = max(1, seq_count // 4)
    tp_rank = lax.axis_index("tp")
    tp = tp_rank.astype(jnp.int32).reshape(1)
    blocks = 8
    place = lax.axis_index("seq").astype(jnp.int32).reshape(1)
    taps = (conv_query, conv_key, conv_value)
    wb = w_beta.T
    tail = shift(layer_input[total - TAIL :], 1)
    chains = groups * heads
    wide = (total, width)
    mats = 2 * total * model
    order = Order()
    run = order.run

    def begin(keep, send, scatter, gather, tag):
        made = Sum(order, keep, send, scatter, gather, tag)
        made.place = place
        return made

    weight = pltpu.VMEM((model, width), bf16)
    rows = pltpu.VMEM((total, model), bf16)
    ext_shape = (total + TAIL, 3 * width)
    conv_shape = (total, 3 * width)
    inv_shape = (chains, GROUP, GROUP)
    map_shape = (chains, DH, DH)
    zst_shape = (chains, DH, 2 * DH)
    dev_shapes = [((heads, DH, 2 * DH), f32), ((heads, DH, DH), f32)]
    near = "near"
    far = "far"
    tp_sums = [((2, share, model), bf16), ((2, share, model), f32)]
    (
        gate_raw, beta_raw, meta, qkv, wmix, umix, score, zst, dev, last,
        hidden, grad_down, x_own, gd_own, ext, conv, inv, amap,
    ) = run(
        front_kernel,
        "front",
        [
            (wide, f32, near),
            ((total, heads), f32, near),
            ((2, groups), jnp.int32),
            (conv_shape, f32, near),
            (wide, f32, near),
            (wide, f32, near),
            (inv_shape, f32, near),
            (zst_shape, f32, near),
            *dev_shapes,
            ((total, model), bf16, far),
            ((total, model), bf16, far),
            ((share, model), bf16, far),
            ((share, model), bf16, far),
            (ext_shape, f32, far),
            (conv_shape, f32, far),
            (inv_shape, f32, far),
            (map_shape, f32, far),
        ],
        [place, tp, seq_groups, seq_pads, layer_input, cotangent, norm_in, w_query, w_key, w_value, w_gate_out, wb, tail, *taps],
        smem=(0, 1, 2, 3),
        smem_out=(2,),
        hbm=(4, 5, 7, 8, 9, 10),
        pin=(2, 3, 4, 5, 6, 7, 8, 9, 10, 11, 13, 14, 15),
        scratch=[
            rows, rows, weight, weight, weight, weight, rows, rows,
            pltpu.VMEM(ext_shape, f32),
            pltpu.VMEM(conv_shape, f32),
            pltpu.VMEM(inv_shape, f32),
            pltpu.VMEM(map_shape, f32),
            pltpu.VMEM(map_shape, f32),
            pltpu.SemaphoreType.DMA((6,)),
            pltpu.SemaphoreType.DMA((8,)),
        ],
        vmem=22,
    )
    hops = hops_of(dev, last, 1, reach)
    mout, oloc = run(
        local_kernel, "local", [(wide, f32, near)] * 2, [qkv, wmix, umix, score, zst]
    )
    heads_out, attended, send, keep, entry = run(
        lambda *r: out_kernel(reach, *r),
        "out",
        [(wide, f32, near), (wide, bf16, near), *tp_sums, ((heads, DH, DH), f32)],
        [tp, *hops, mout, oloc, gate_raw, norm_head, w_out],
        smem=(0,),
    )
    kept, cross = scatter_first(order, keep, send)
    got = swap(cross, 2)
    states, vnew, qeff = run(
        states_kernel,
        "states",
        [(map_shape, f32, near), (wide, f32, near), (wide, f32, near)],
        [entry, zst, qkv, wmix, umix, score],
    )
    residual, second_own = run(
        mid_kernel,
        "mid",
        [((share, model), f32, near), ((share, model), bf16)],
        [x_own, kept[0], got[0], norm_mid],
    )
    size = ffw // blocks
    ways = [WAYS[name] for name in ("f1", "f2", "f3", "f4")]
    flows = {}

    def go(slot):
        for name in STEPS[slot]:
            flows[name].step()

    near_up = size // 16 * 8
    far_up = size - near_up
    down_parts = [Plan(0, ways[0][0], 0, size)]
    gate_parts = [Plan(1, ways[1][0], 0, size)]
    up_parts = [
        Plan(0, ways[0][0], size, near_up),
        Plan(1, ways[1][0], size, far_up, start=near_up * blocks),
    ]
    plans_a = (down_parts, gate_parts, up_parts)
    f1_rows, f2_rows = size + near_up, size + far_up
    own_rows, beside_rows = second_own, swap(second_own, 1)
    far_rows = swap(second_own, 2)
    w_shape = (ffw, model)
    wg, wu, wd, gd, grad_inner = run(
        warm_kernel,
        "warm",
        [
            (w_shape, bf16, near),
            (w_shape, bf16, near),
            (w_shape, bf16, near),
            ((total, model), bf16, near),
            ((total, ffw), f32, near),
        ],
        [w_gate.T, w_up.T, w_down, grad_down],
        hbm=(0, 1, 2, 3),
        pin=(0, 1, 2, 3),
        scratch=[pltpu.SemaphoreType.DMA((4,))],
    )
    part = (1, share, model)
    half_ffn = ((2 * share, ffw), bf16)
    half_outs = [(part, f32), (part, bf16)] * 2
    sec_a, inner_a, dgate_a, dup_a, down_keep_a, down_send_a, keep_a, send_a = run(
        ffn_a_kernel,
        "ffn_a",
        [((2 * share, model), bf16), half_ffn, half_ffn, half_ffn, *half_outs],
        [tp, own_rows, beside_rows, wg, wu, wd, grad_inner],
        smem=(0,),
        vmem=12,
    )
    far_rows, sec_a = lax.optimization_barrier((far_rows, sec_a))
    near_a = swap(send_a, 1)
    down_near_a = swap(down_send_a, 1)
    down_keep_b, down_send_b, keep_b, send_b, *sums = run(
        lambda *r: ffn_b_kernel(plans_a, *r),
        "ffn_b",
        [*half_outs, *sum_shapes(blocks, f1_rows, model), *sum_shapes(blocks, f2_rows, model)],
        [tp, place, far_rows, swap(far_rows, 1), wg, wu, wd, grad_inner, gd, sec_a, inner_a, dgate_a, dup_a],
        smem=(0, 1),
        scratch=[
            pltpu.VMEM((2 * share, model), bf16),
            *[pltpu.VMEM((2 * share, ffw), bf16)] * 3,
            pltpu.VMEM((ffw, model), f32),
        ],
        vmem=16,
    )
    near_b = swap(send_b, 1)
    flows["f1"] = begin(sums[0], sums[1], *ways[0], "f1")
    flows["f2"] = begin(sums[2], sums[3], *ways[1], "f2")
    kept, cross = fold_pair(order, keep_a, near_a, keep_b, near_b)
    got = swap(cross, 2)
    grad_residual, branch_own, mid_part = run(
        turn_kernel,
        "turn",
        [((share, model), f32), ((share, model), bf16), ((1, model), f32)],
        [kept[0], got[0], residual, norm_mid, gd_own],
    )
    branch_all = gather_rel(branch_own)
    branch, dgate_raw, dout, rst, dev, last, head_part = run(
        flow_kernel,
        "flow",
        [
            ((total, model), bf16),
            (wide, bf16),
            (wide, f32),
            (zst_shape, f32),
            *dev_shapes,
            ((1, DH), f32),
        ],
        [tp, meta, *branch_all, w_out, heads_out, gate_raw, norm_head, qeff, amap],
        smem=(0, 1),
        scratch=[pltpu.VMEM(map_shape, f32)],
    )
    hops = hops_of(dev, last, -1, reach)
    down_near_b = swap(down_send_b, 1)
    ndo, dq, dk = run(
        side_kernel,
        "side",
        [(wide, f32)] * 3,
        [qkv, dout, vnew, states, score],
    )
    down_kept, cross = fold_pair(order, down_keep_a, down_near_a, down_keep_b, down_near_b)
    down_got = swap(cross, 2)
    order.wait(*hops)
    go("hops")
    dc, halo, dbeta = run(
        lambda *r: back_kernel(reach, *r),
        "back",
        [((total + 8, 3 * width), f32), ((8, 3 * width), f32), ((total, LANES), bf16)],
        [meta, *hops, rst, qkv, conv, *taps, beta_raw, inv, states, vnew, ndo, dq, dk],
        smem=(0,),
    )
    incoming = shift(halo, -1)
    go("back")
    gp, last, dtaps = run(
        taps_kernel,
        "taps",
        [(conv_shape, bf16), ((TAIL, 3 * width), f32), ((KW, 3 * width), f32)],
        [meta, dc, ext, *taps],
        smem=(0,),
    )
    (out_own,) = run(
        outblock_kernel,
        "outblk",
        [((share, model), bf16)],
        [tp, meta, down_kept[0], down_got[0], residual],
        smem=(0, 1),
    )
    go("taps")
    gp, send, keep, in_part = run(
        hid_kernel,
        "hid",
        [(conv_shape, bf16), *tp_sums, ((1, model), f32)],
        [tp, gp, last, incoming, dgate_raw, dbeta, w_query, w_key, w_value, w_gate_out, wb, layer_input],
        smem=(0,),
        vmem=12,
    )
    beside = swap(send, 1)
    piece = model // blocks
    fold_rows = piece * width // model
    split = dict(folds=model // width)
    plans_c = [
        Plan(0, ways[2][0], i * fold_rows, piece, lane=i * width, **split) for i in range(3)
    ]
    keep_c, send_c = run(
        lambda *r: grads_c_kernel(plans_c, *r),
        "grads_c",
        sum_shapes(blocks, 3 * fold_rows, model),
        [place, hidden, gp],
        smem=(0,),
        scratch=[pltpu.VMEM((model, 3 * width), f32)],
        vmem=16,
    )
    flows["f3"] = begin(keep_c, send_c, *ways[2], "f3")
    go("hid")
    kept, cross = fold(order, keep, beside, "fold_tp")
    got = swap(cross, 2)
    row8 = ((8, model), f32)
    small, gains = run(
        small_kernel, "small", [row8, row8], [dtaps, dbeta, hidden, in_part, mid_part, head_part]
    )
    gains = plus(order, gains, swap(gains, 1))
    far_gains = swap(gains, 2)
    go("x")
    (grad_in_own,) = run(
        in_kernel,
        "inp",
        [((share, model), bf16)],
        [kept[0], got[0], x_own, norm_in, grad_residual],
    )
    grad_in_all = gather_rel(grad_in_own)
    gains = plus(order, gains, far_gains)
    wo_rows = width // blocks
    out_parts = [Plan(0, ways[3][0], 0, wo_rows)]
    gate_out_parts = [Plan(0, ways[3][0], wo_rows, piece, **split)]
    line_base = wo_rows + fold_rows
    keep_d, send_d = run(
        lambda *r: grads_d_kernel(out_parts + gate_out_parts, ways[3][0], line_base, *r),
        "grads_d",
        sum_shapes(blocks, line_base + 8, model),
        [place, attended, branch, hidden, dgate_raw, small, gains],
        smem=(0,),
        scratch=[
            pltpu.VMEM((width, model), f32),
            pltpu.VMEM((model, width), f32),
            pltpu.VMEM((8, model), f32),
        ],
        vmem=12,
    )
    flows["f4"] = begin(keep_d, send_d, *ways[3], "f4")
    out_all = gather_rel(out_own)
    results = {}

    def settle(name, jobs, used, outs, line_at=None):
        return run(
            lambda *r: settle_kernel(len(used), jobs, line_at, *r),
            name,
            [(o, f32) for o in outs],
            [place, *[a for flow in used for a in (flows[flow].own, flows[flow].got)]],
            smem=(0,),
        )

    def wayed(parts, first_flow=0):
        moved = [Plan(p.index - first_flow, *p.rest()) for p in parts]
        return [(m, ways[p.index][1]) for m, p in zip(moved, parts)]

    def late(parts, flow):
        return [(part, ways[flow][1]) for part in parts]

    for name in STEPS["tail"]:
        if name in flows:
            flows[name].step()
        elif name in ("in", "out"):
            results[name] = run(
                place_kernel,
                "place_" + name,
                [((total, model), f32 if name == "in" else bf16)],
                [tp, *(grad_in_all if name == "in" else out_all)],
                smem=(0,),
            )
        elif name == "s1":
            results[name] = settle(
                "settle_1",
                [wayed(down_parts), wayed(up_parts)],
                ["f1", "f2"],
                [(ffw, model)] * 2,
            )
        elif name == "s2":
            results[name] = settle("settle_2", [wayed(gate_parts, 1)], ["f2"], [(ffw, model)])
        elif name == "s3":
            results[name] = settle(
                "settle_3", [late([part], 2) for part in plans_c], ["f3"], [(model, width)] * 3
            )
        else:
            results[name] = settle(
                "settle_4",
                [late(out_parts, 3), late(gate_out_parts, 3)],
                ["f4"],
                [(width, model), (model, width), (8, model)],
                line_at=(0, ways[3][1], line_base),
            )
    (grad_input,) = results["in"]
    (block_out,) = results["out"]
    grad_down_w, grad_up_w = results["s1"]
    (grad_gate_w,) = results["s2"]
    hidden_sums = results["s3"]
    grad_out_w, grad_gate_out_w, small = results["s4"]
    cut = model // 4
    head_cut = DH // 4
    gain_of = lambda row, size, lane=0: lax.dynamic_slice(
        small, (row, lane + tp_rank * size), (1, size)
    ).reshape(size)
    tap_of = lambda i: small[:KW, i * width : (i + 1) * width]
    return (
        block_out,
        grad_input,
        gain_of(KW + 2, cut),
        hidden_sums[0],
        hidden_sums[1],
        hidden_sums[2],
        tap_of(0),
        tap_of(1),
        tap_of(2),
        small[KW : KW + heads].T,
        grad_gate_out_w,
        gain_of(0, head_cut, 3 * width),
        grad_out_w,
        gain_of(KW + 3, cut),
        grad_gate_w.T,
        grad_up_w.T,
        grad_down_w,
    )


def solution(mesh):
    rows = P("seq", None)
    cols = P(None, "tp")
    return jax.shard_map(
        shards,
        mesh=mesh,
        in_specs=(rows, P(), P(), P(), cols, cols, cols, cols, cols, cols, cols, cols, P(), P("tp", None), P(), cols, cols, P("tp", None), rows),
        out_specs=(rows, rows, P("tp"), cols, cols, cols, cols, cols, cols, cols, cols, P("tp"), P("tp", None), P("tp"), cols, cols, P("tp", None)),
        check_vma=False,
    )
```

```python
import jax
import jax.numpy as jnp
from jax import lax
from jax.experimental import pallas as pl
from jax.experimental.pallas import tpu as pltpu
from jax.sharding import PartitionSpec as P

DH = 128
KW = 4
GROUP = 64
TAIL = 16
LANES = 128

row_epsilon = 1e-06
head_epsilon = 1e-05
unit_epsilon = 1e-06
f32 = jnp.float32
bf16 = jnp.bfloat16


def dot(a, b, ca=1, cb=0):
    return lax.dot_general(a, b, (((ca,), (cb,)), ((), ())), preferred_element_type=f32)


def halves(a):
    high = a.astype(bf16)
    return high, (a - high.astype(f32)).astype(bf16)


def fdot(a, b, ca=1, cb=0):
    ah, al = halves(a)
    bh, bl = halves(b)
    return dot(
        jnp.concatenate([ah, al, ah], axis=ca), jnp.concatenate([bh, bh, bl], axis=cb), ca, cb
    )


def gdot(a, b, ca=1, cb=0):
    return dot(a.astype(bf16), b.astype(bf16), ca, cb)


def iota(shape, axis):
    return lax.broadcasted_iota(jnp.int32, shape, axis)


def rows_of(block, size):
    return pl.ds(pl.multiple_of(block * size, size), size)


COST = 1153500
STEPS = {'hops': ['f2', 'f1'], 'back': ['f1', 'f2'], 'taps': ['f2'], 'hid': [], 'x': ['f1'], 'tail': ['f3', 'in', 'f4', 'out', 'f1', 'f3', 'f4', 'f2', 'f2', 'f3', 'f1', 'f4', 'f4', 'f3', 'f3', 'f4', 's1', 's2', 's4', 's3']}
WAYS = {'f1': ((0, 1, 2), (2, 1, 0)), 'f2': ((1, 0, 2), (2, 0, 1)), 'f3': ((0, 1, 2), (1, 2, 0)), 'f4': ((1, 0, 2), (2, 0, 1))}


class Order:
    def __init__(self):
        self.last = None
        self.also = ()

    def wait(self, *values):
        self.also = values

    def run(self, kernel, name, outs, args, smem=(), smem_out=(), hbm=(), pin=(), scratch=(), flops=COST, vmem=8):
        held = {"far": pltpu.HBM, "near": pltpu.VMEM}
        shapes = [
            held[o[2]](o[0], o[1]) if len(o) > 2 else jax.ShapeDtypeStruct(*o) for o in outs
        ]
        hbm_out = [i for i, o in enumerate(outs) if o[2:] == ("far",)]
        args = list(args)
        if self.last is not None:
            free = [i for i in range(len(args)) if i not in smem]
            at = min(free, key=lambda i: (i in pin, i))
            args[at] = lax.optimization_barrier((args[at], self.last, *self.also))[0]
            self.also = ()
        for i in pin:
            args[i] = pltpu.with_memory_space_constraint(args[i], pltpu.HBM)
        space = lambda i, low, far: pltpu.SMEM if i in low else pltpu.HBM if i in far else pltpu.VMEM
        made = pl.pallas_call(
            kernel,
            name=name,
            out_shape=shapes,
            in_specs=[pl.BlockSpec(memory_space=space(i, smem, hbm)) for i in range(len(args))],
            out_specs=[
                pl.BlockSpec(memory_space=space(i, smem_out, hbm_out)) for i in range(len(outs))
            ],
            scratch_shapes=list(scratch),
            compiler_params=pltpu.CompilerParams(vmem_limit_bytes=vmem << 20),
            cost_estimate=pl.CostEstimate(flops=flops, bytes_accessed=1, transcendentals=0),
        )(*args)
        kept = [i for i in range(len(made)) if i not in smem_out]
        self.last = made[min(kept, key=lambda i: (i in hbm_out, i))]
        return made


def wide_gain(ref):
    return ref[...].astype(f32).reshape(1, ref.shape[0])


def live_mask(meta, block, size):
    parts = size // GROUP
    row = iota((size, 1), 0)
    limit = jnp.full((size, 1), 0, jnp.int32) + meta[1, block * parts]
    for part in range(1, parts):
        limit = jnp.where(row >= part * GROUP, meta[1, block * parts + part] + part * GROUP, limit)
    return row < limit


def rms_rows(values, gain):
    factor = lax.rsqrt(jnp.mean(values * values, axis=-1, keepdims=True) + row_epsilon)
    return values * factor * gain


def beta_col(beta, meta, n, h):
    raw = beta[pl.ds(pl.multiple_of(n * GROUP, GROUP), GROUP), h : h + 1]
    sig = jax.nn.sigmoid(raw)
    live = iota((GROUP, 1), 0) < meta[1, n]
    return jnp.where(live, sig, 0.0), sig, live


def unit(rows):
    return rows * lax.rsqrt(jnp.sum(rows * rows, axis=-1, keepdims=True) + unit_epsilon)


def tri_inverse(systems, block=16):
    size = systems[0].shape[0]
    row = iota((size, size), 0)
    col = iota((size, size), 1)
    eye = (row == col).astype(f32)
    tiles = [[eye[r : r + 8] for r in range(0, size, 8)] for _ in systems]
    lower = [[system[r : r + 8] for r in range(0, size, 8)] for system in systems]
    for step in range(block - 1):
        for low, part in zip(lower, tiles):
            for start in range(0, size, block):
                j = start + step
                line = part[j // 8][j % 8 : j % 8 + 1]
                for r in range((j + 1) // 8, (start + block) // 8):
                    part[r] = part[r] - low[r][:, j : j + 1] * line
    inverses = [jnp.concatenate(part, axis=0) for part in tiles]
    while block < size:
        pick = ((row // block) % 2 == 1) & (col // block == row // block - 1)
        mids = [
            fdot(inverse, jnp.where(pick, system, 0.0))
            for inverse, system in zip(inverses, systems)
        ]
        inverses = [inverse - fdot(mid, inverse) for mid, inverse in zip(mids, inverses)]
        block *= 2
    return inverses


def tap_table(*tables):
    values = [table[...].astype(f32) for table in tables]
    parts = values[0].shape[1] // DH
    return lambda j, c: values[c // parts][j : j + 1, (c % parts) * DH : (c % parts + 1) * DH]


def front_kernel(first, tp, seq_groups, seq_pads, xh, coth, gain, wqh, wkh, wvh, wgh, wb, tail, cq, ck, cv, gate, beta, meta, qkv, wmix, umix, score, zst, dev, last, hidden_h, gd_h, x_own, gd_own, ext_h, conv_h, inv_h, amap_h, x, cot, wq, wk, wv, wg, hidden, gd, ext, conv, inv, amap, badd, sems, out_sems):
    loads = [
        pltpu.make_async_copy(src, dst, sems.at[i])
        for i, (src, dst) in enumerate(
            ((xh, x), (wqh, wq), (wkh, wk), (wvh, wv), (wgh, wg), (coth, cot))
        )
    ]
    for load in loads:
        load.start()
    groups = x.shape[0] // GROUP
    for n in range(groups):
        meta[0, n] = 0
        meta[1, n] = 0

    def one(s, start):
        count = seq_groups[s]
        length = count * GROUP - seq_pads[s]
        for n in range(groups):
            gid = first[0] * groups + n
            inside = (gid >= start) & (gid < start + count)
            here = jnp.clip(length - (gid - start) * GROUP, 0, GROUP)
            meta[0, n] = jnp.where(gid == start, 1, meta[0, n])
            meta[1, n] = jnp.where(inside, here, meta[1, n])
        return start + count

    lax.fori_loop(0, seq_groups.shape[0], one, jnp.int32(0))
    width = wq.shape[1]
    heads = width // DH
    tile = 256
    share = x_own.shape[0]
    scale = wide_gain(gain)
    own = rows_of(tp[0], share)
    stores = []

    def store(src, dst):
        copy = pltpu.make_async_copy(src, dst, out_sems.at[len(stores)])
        copy.start()
        stores.append(copy)

    loads[0].wait()
    store(x.at[own], x_own)
    tiles = [slice(t * tile, (t + 1) * tile) for t in range(x.shape[0] // tile)]
    for rows in tiles:
        hidden[rows] = rms_rows(x[rows].astype(f32), scale).astype(bf16)
    store(hidden, hidden_h)
    low = rms_rows(tail[...].astype(f32), scale).astype(bf16)
    for rows in tiles:
        beta[rows] = dot(hidden[rows], wb[...], 1, 1)
    for i, w in enumerate((wq, wk, wv, wg)):
        loads[1 + i].wait()
        lanes = slice(i * width, (i + 1) * width)
        for rows in tiles:
            got = dot(hidden[rows], w[...])
            if i < 3:
                ext[TAIL + rows.start : TAIL + rows.stop, lanes] = got
            else:
                gate[rows] = got
        if i < 3:
            ext[0:TAIL, lanes] = dot(low, w[...])
    store(ext, ext_h)
    loads[5].wait()
    for t, rows in enumerate(tiles):
        live = live_mask(meta, t, tile)
        gd[rows] = jnp.where(live, cot[rows].astype(f32), 0.0).astype(bf16)
    store(gd, gd_h)
    store(gd.at[own], gd_own)
    row = iota((GROUP, 1), 0)
    taps = tap_table(cq, ck, cv)

    def front(n):
        base = pl.multiple_of(n * GROUP, GROUP)
        for c in range(3 * heads):
            lanes = slice(c * DH, (c + 1) * DH)
            win = ext[pl.ds(pl.multiple_of(base + TAIL - 8, 8), GROUP + 8), lanes]
            acc = taps(KW - 1, c) * win[8:]
            for d in range(1, KW):
                part = jnp.where(row < meta[0, n] * d, 0.0, win[8 - d : 8 - d + GROUP])
                acc = acc + taps(KW - 1 - d, c) * part
            conv[pl.ds(base, GROUP), lanes] = acc
            acted = acc * jax.nn.sigmoid(acc)
            qkv[pl.ds(base, GROUP), lanes] = unit(acted) if c < 2 * heads else acted

    pl.loop(0, groups)(front)
    store(conv, conv_h)
    r64 = iota((GROUP, GROUP), 0)
    c64 = iota((GROUP, GROUP), 1)
    eye = (iota((DH, DH), 0) == iota((DH, DH), 1)).astype(f32)

    def load(n, h):
        rows = pl.ds(pl.multiple_of(n * GROUP, GROUP), GROUP)
        return [qkv[rows, (i * heads + h) * DH : (i * heads + h + 1) * DH] for i in range(3)]

    def local(i, _):
        chains = [(j, h) for j in range(groups) for h in range(heads)]
        systems = []
        kept = []
        for n, h in chains:
            q, k, v = load(n, h)
            b = beta_col(beta, meta, n, h)[0]
            both = fdot(jnp.concatenate([k * b, q], axis=0), k, 1, 1)
            systems.append(jnp.where(r64 > c64, both[:GROUP], 0.0))
            score[n * heads + h] = jnp.where(r64 >= c64, both[GROUP:], 0.0)
            kept.append((k, b, v))
        inverses = tri_inverse(systems)
        for (n, h), inverse, (k, b, v) in zip(chains, inverses, kept):
            rows = pl.ds(pl.multiple_of(n * GROUP, GROUP), GROUP)
            inv[n * heads + h] = inverse
            wu = fdot(inverse, jnp.concatenate([k * b, v * b], axis=1))
            wmix[rows, h * DH : (h + 1) * DH] = wu[:, :DH]
            umix[rows, h * DH : (h + 1) * DH] = wu[:, DH:]
            kwu = fdot(k, wu, 0, 0)
            amap[n * heads + h] = eye - kwu[:, :DH]
            badd[n * heads + h] = kwu[:, DH:]
        return 0

    local(0, 0)
    store(inv, inv_h)
    store(amap, amap_h)
    for h in range(heads):
        dev[h, :, :DH] = eye
        dev[h, :, DH:] = jnp.zeros((DH, DH), f32)

    def chain(n, _):
        keep = 1.0 - meta[0, n].astype(f32)
        for h in range(heads):
            start = dev[h] * keep
            zst[n * heads + h] = start
            moved = fdot(amap[n * heads + h], start)
            dev[h, :, :DH] = moved[:, :DH]
            dev[h, :, DH:] = moved[:, DH:] + badd[n * heads + h]
        return 0

    lax.fori_loop(0, groups, chain, 0)
    last[...] = dev[:, :, DH:]

    for copy in stores:
        copy.wait()


def local_kernel(qkv, wmix, umix, score, zst, mout, oloc):
    groups = qkv.shape[0] // GROUP
    heads = wmix.shape[1] // DH

    def one(i, _):
        for n, h in [(2 * i + j, h) for j in range(2) for h in range(heads)]:
            rows = pl.ds(pl.multiple_of(n * GROUP, GROUP), GROUP)
            lanes = slice(h * DH, (h + 1) * DH)
            q = qkv[rows, lanes]
            both = fdot(jnp.concatenate([q, wmix[rows, lanes]], axis=0), zst[n * heads + h])
            lower = jnp.concatenate(
                [-both[GROUP:, :DH], umix[rows, lanes] - both[GROUP:, DH:]], axis=1
            )
            made = both[:GROUP] + fdot(score[n * heads + h], lower)
            mout[rows, lanes] = made[:, :DH]
            oloc[rows, lanes] = made[:, DH:]
        return 0

    lax.fori_loop(0, groups // 2, one, 0)


def fold_hops(hops, h):
    state = hops[-1][h].astype(f32)
    for hop in hops[-2::-1]:
        state = hop[h, :, DH:].astype(f32) + fdot(hop[h, :, :DH].astype(f32), state)
    return state


def out_kernel(hop_count, tp, *refs):
    hops, refs = refs[:hop_count], refs[hop_count:]
    mout, oloc, gate, nh, wo, heads_out, att, send, keep, entry = refs
    heads = gate.shape[1] // DH
    states = [fold_hops(hops, h) for h in range(heads)]
    for h in range(heads):
        entry[h] = states[h]
    share = mout.shape[0] // 4
    for rel in range(4):
        rows = rows_of(tp[0] ^ rel, share)
        lows = []
        for h in range(heads):
            lanes = slice(h * DH, (h + 1) * DH)
            o = oloc[rows, lanes] + fdot(mout[rows, lanes], states[h])
            heads_out[rows, lanes] = o
            factor = lax.rsqrt(jnp.mean(o * o, axis=-1, keepdims=True) + head_epsilon)
            g = gate[rows, lanes]
            lows.append((o * factor * wide_gain(nh) * (g * jax.nn.sigmoid(g))).astype(bf16))
        low = jnp.concatenate(lows, axis=1)
        att[rows] = low
        part = dot(low, wo[...])
        if rel % 2:
            send[rel // 2] = part.astype(bf16)
        else:
            keep[rel // 2] = part


def states_kernel(entry, zst, qkv, wmix, umix, score, states, vnew, qeff):
    groups = qkv.shape[0] // GROUP
    heads = wmix.shape[1] // DH

    def one(i, _):
        for n, h in [(2 * i + j, h) for j in range(2) for h in range(heads)]:
            rows = pl.ds(pl.multiple_of(n * GROUP, GROUP), GROUP)
            lanes = slice(h * DH, (h + 1) * DH)
            at = n * heads + h
            s = zst[at, :, DH:] + fdot(zst[at, :, :DH], entry[h])
            states[at] = s
            w = wmix[rows, lanes]
            vnew[rows, lanes] = umix[rows, lanes] - fdot(w, s)
            qeff[rows, lanes] = qkv[rows, lanes] - fdot(score[at], w)
        return 0

    lax.fori_loop(0, groups // 2, one, 0)


def mid_kernel(x, kept, got, gain, residual, second):
    total = x[...].astype(f32) + kept[...] + got[...].astype(f32)
    residual[...] = total
    second[...] = rms_rows(total, wide_gain(gain)).astype(bf16)


def warm_kernel(wgh, wuh, wdh, gdh, wg, wu, wd, gd, grad_inner, sems):
    loads = [
        pltpu.make_async_copy(src, dst, sems.at[i])
        for i, (src, dst) in enumerate(((wdh, wd), (gdh, gd), (wgh, wg), (wuh, wu)))
    ]
    for load in loads:
        load.start()
    loads[0].wait()
    loads[1].wait()
    tile = 256
    for t in range(gd.shape[0] // tile):
        rows = slice(t * tile, (t + 1) * tile)
        grad_inner[rows] = dot(gd[rows], wd[...], 1, 1)
    loads[2].wait()
    loads[3].wait()


def ffn_half(tp, half, sa, sb, wg, wu, wd, grad_inner, sec, inner, dgate, dup, down_keep, down_send, keep, send):
    share = sa.shape[0]
    sec[:share] = sa[...]
    sec[share:] = sb[...]
    gv = dot(sec[...], wg[...], 1, 1)
    uv = dot(sec[...], wu[...], 1, 1)
    sig = jax.nn.sigmoid(gv)
    act = gv * sig
    inn = (act * uv).astype(bf16)
    gi = jnp.concatenate(
        [grad_inner[rows_of(tp[0] ^ (2 * half + j), share)] for j in range(2)], axis=0
    )
    dg = (gi * uv * (sig * (1.0 + gv * (1.0 - sig)))).astype(bf16)
    du = (gi * act).astype(bf16)
    inner[...] = inn
    dgate[...] = dg
    dup[...] = du
    grad = dot(dg, wg[...]) + dot(du, wu[...])
    keep[0] = grad[:share]
    send[0] = grad[share:].astype(bf16)
    down = dot(inn, wd[...])
    down_keep[0] = down[:share]
    down_send[0] = down[share:].astype(bf16)


def ffn_a_kernel(tp, sa, sb, wg, wu, wd, grad_inner, *outs):
    ffn_half(tp, 0, sa, sb, wg, wu, wd, grad_inner, *outs)


def ffn_b_kernel(plans, tp, place, sa, sb, wg, wu, wd, grad_inner, gd, sec_a, inner_a, dgate_a, dup_a, down_keep, down_send, keep, send, *refs):
    sums, (sec, inner, dgate, dup, acc) = refs[:-5], refs[-5:]
    share = sa.shape[0]
    ffn_half(tp, 1, sa, sb, wg, wu, wd, grad_inner, sec, inner, dgate, dup, down_keep, down_send, keep, send)
    near = [jnp.concatenate([gd[rows_of(tp[0] ^ (2 * i + j), share)] for j in range(2)], axis=0) for i in range(2)]
    for pair, plan in (
        (((inner_a[...], near[0]), (inner[...], near[1])), 0),
        (((dgate_a[...], sec_a[...]), (dgate[...], sec[...])), 1),
        (((dup_a[...], sec_a[...]), (dup[...], sec[...])), 2),
    ):
        acc[...] = dot(*pair[0], 0, 0) + dot(*pair[1], 0, 0)
        put(acc, acc.shape[1], (place[0] & 7), plans[plan], sums)


def turn_kernel(kept, got, residual, gain, grad_y, grad_residual, branch, gain_part):
    gs = kept[...] + got[...].astype(f32)
    v = residual[...]
    g = wide_gain(gain)
    r = lax.rsqrt(jnp.mean(v * v, axis=-1, keepdims=True) + row_epsilon)
    gain_part[...] = jnp.sum(gs * v * r, axis=0, keepdims=True)
    e = gs * g
    back = r * e - v * (r * r * r) * jnp.mean(e * v, axis=-1, keepdims=True)
    total = grad_y[...].astype(f32) + back
    grad_residual[...] = total
    branch[...] = total.astype(bf16)


def flow_kernel(tp, meta, b0, b1, b2, b3, wo, heads_out, gate, nh, qeff, amap, branch, dgate, dout, rst, dev_low, last, nh_part, flows, dev):
    share = b0.shape[0]
    heads = gate.shape[1] // DH
    groups = gate.shape[0] // GROUP
    gains = jnp.zeros((1, DH), f32)
    for half, pair in enumerate(((b0, b1), (b2, b3))):
        both = jnp.concatenate([pair[0][...], pair[1][...]], axis=0)
        ga = dot(both, wo[...], 1, 1)
        for j in range(2):
            rows = rows_of(tp[0] ^ (2 * half + j), share)
            branch[rows] = pair[j][...]
            for h in range(heads):
                lanes = slice(h * DH, (h + 1) * DH)
                gz = ga[j * share : (j + 1) * share, lanes]
                o = heads_out[rows, lanes]
                g = gate[rows, lanes]
                gain = wide_gain(nh)
                r = lax.rsqrt(jnp.mean(o * o, axis=-1, keepdims=True) + head_epsilon)
                sig = jax.nn.sigmoid(g)
                act = g * sig
                e = gz * gain * act
                base = gz * o * r
                gains = gains + jnp.sum(base * act, axis=0, keepdims=True)
                dgate[rows, lanes] = (base * gain * (sig * (1.0 + g * (1.0 - sig)))).astype(bf16)
                dout[rows, lanes] = r * e - o * (r * r * r) * jnp.mean(e * o, axis=-1, keepdims=True)
    nh_part[...] = gains

    def local(i, _):
        for n, h in [(2 * i + j, h) for j in range(2) for h in range(heads)]:
            rows = pl.ds(pl.multiple_of(n * GROUP, GROUP), GROUP)
            lanes = slice(h * DH, (h + 1) * DH)
            flows[n * heads + h] = fdot(qeff[rows, lanes], dout[rows, lanes], 0, 0)
        return 0

    lax.fori_loop(0, groups // 2, local, 0)
    eye = (iota((DH, DH), 0) == iota((DH, DH), 1)).astype(f32)
    for h in range(heads):
        dev[h, :, :DH] = eye
        dev[h, :, DH:] = jnp.zeros((DH, DH), f32)

    def chain(i, _):
        n = groups - 1 - i
        keep = 1.0 - meta[0, n].astype(f32)
        for h in range(heads):
            at = n * heads + h
            later = dev[h]
            rst[at] = later
            moved = fdot(amap[at], later, 0, 0)
            dev[h, :, :DH] = moved[:, :DH] * keep
            dev[h, :, DH:] = (moved[:, DH:] + flows[at]) * keep
        return 0

    lax.fori_loop(0, groups, chain, 0)
    dev_low[...] = dev[...].astype(bf16)
    last[...] = dev[:, :, DH:].astype(bf16)


def side_kernel(qkv, dout, vnew, states, score, ndo, dq, dk):
    heads = dout.shape[1] // DH
    groups = dout.shape[0] // GROUP
    lower = iota((GROUP, GROUP), 0) >= iota((GROUP, GROUP), 1)

    def one(i, _):
        for n, h in [(2 * i + j, h) for j in range(2) for h in range(heads)]:
            rows = pl.ds(pl.multiple_of(n * GROUP, GROUP), GROUP)
            lanes = slice(h * DH, (h + 1) * DH)
            at = n * heads + h
            q = qkv[rows, lanes]
            k = qkv[rows, (heads + h) * DH : (heads + h + 1) * DH]
            do = dout[rows, lanes]
            ndo[rows, lanes] = fdot(score[at], do, 0, 0)
            dn = jnp.where(lower, fdot(do, vnew[rows, lanes], 1, 1), 0.0)
            dq[rows, lanes] = fdot(do, states[at], 1, 1) + fdot(dn, k)
            dk[rows, lanes] = fdot(dn, q, 0, 0)
        return 0

    lax.fori_loop(0, groups // 2, one, 0)


def unit_back(a, grad):
    r = lax.rsqrt(jnp.sum(a * a, axis=-1, keepdims=True) + unit_epsilon)
    return r * grad - a * (r * r * r) * jnp.sum(a * grad, axis=-1, keepdims=True)


def back_kernel(hop_count, meta, *refs):
    hops, refs = refs[:hop_count], refs[hop_count:]
    rst, qkv, conv, cq, ck, cv, beta, inv, states, vnew, ndo, dq, dk1, dc, halo, dbeta = refs
    taps = tap_table(cq, ck, cv)
    heads = ndo.shape[1] // DH
    groups = ndo.shape[0] // GROUP
    total = ndo.shape[0]
    exits = [fold_hops(hops, h) for h in range(heads)]
    strict = iota((GROUP, GROUP), 0) > iota((GROUP, GROUP), 1)
    lane = iota((GROUP, LANES), 1)
    dc[total:] = jnp.zeros((8, dc.shape[1]), f32)

    def one(i, _):
        for j in range(2):
            n = 2 * i + j
            rows = pl.ds(pl.multiple_of(n * GROUP, GROUP), GROUP)
            raws = jnp.zeros((GROUP, LANES), f32)
            for h in range(heads):
                at = n * heads + h
                lanes = [slice((p * heads + h) * DH, (p * heads + h + 1) * DH) for p in range(3)]
                k = qkv[rows, lanes[1]]
                v = qkv[rows, lanes[2]]
                b, sig, live = beta_col(beta, meta, n, h)
                ds = rst[at, :, DH:] + gdot(rst[at, :, :DH], exits[h])
                dvn = ndo[rows, lanes[0]] + gdot(k, ds)
                d = gdot(inv[at], dvn, 0, 0)
                vn = vnew[rows, lanes[0]]
                both = gdot(d, jnp.concatenate([states[at], vn], axis=0), 1, 1)
                dstate = both[:, :DH]
                vds = gdot(vn, ds, 1, 1)
                da = jnp.where(strict, -both[:, DH:], 0.0)
                dak = gdot(da, k)
                datk = gdot(da, k * b, 0, 0)
                dk = dk1[rows, lanes[0]] + vds + b * (dak - dstate) + datk
                db = jnp.sum(d * v + (dak - dstate) * k, axis=-1, keepdims=True)
                db = jnp.where(live, db * sig * (1.0 - sig), 0.0)
                raws = jnp.where(lane == h, db, raws)
                grads = (dq[rows, lanes[0]], dk, d * b)
                for p in range(3):
                    c = conv[rows, lanes[p]]
                    s = jax.nn.sigmoid(c)
                    grad = unit_back(c * s, grads[p]) if p < 2 else grads[p]
                    dc[rows, lanes[p]] = grad * (s * (1.0 + c * (1.0 - s)))
            dbeta[rows] = raws.astype(bf16)
        return 0

    lax.fori_loop(0, groups // 2, one, 0)
    zero = jnp.zeros((8, DH), f32)
    for c in range(3 * heads):
        lanes = slice(c * DH, (c + 1) * DH)
        win = dc[0:8, lanes]
        acc = zero
        for d in range(1, KW):
            part = jnp.where(iota((8, 1), 0) < meta[0, 0] * d, 0.0, win)
            j = KW - 1 - d
            acc = acc + taps(j, c) * jnp.concatenate([zero, part], axis=0)[d : d + 8]
        halo[:, lanes] = acc


def taps_kernel(meta, dc, ext, cq, ck, cv, gp, last, dtaps):
    heads = cq.shape[1] // DH
    groups = gp.shape[0] // GROUP
    taps = tap_table(cq, ck, cv)
    dtaps[...] = jnp.zeros(dtaps.shape, f32)

    def masked(win, d, here, after):
        front = jnp.where(iota((GROUP, 1), 0) < here * d, 0.0, win[:GROUP])
        if after is None:
            return front
        back = jnp.where(iota((8, 1), 0) < after * d, 0.0, win[GROUP:])
        return jnp.concatenate([front, back], axis=0)

    def taps_back(n, _):
        base = pl.multiple_of(n * GROUP, GROUP)
        here = meta[0, n]
        after = meta[0, jnp.minimum(n + 1, groups - 1)]
        for c in range(3 * heads):
            lanes = slice(c * DH, (c + 1) * DH)
            win = dc[pl.ds(base, GROUP + 8), lanes]
            old = ext[pl.ds(pl.multiple_of(base + TAIL - 8, 8), GROUP + 8), lanes]
            acc = taps(KW - 1, c) * win[:GROUP]
            dtaps[KW - 1 : KW, lanes] += jnp.sum(win[:GROUP] * old[8:], axis=0, keepdims=True)
            for d in range(1, KW):
                part = masked(win, d, here, after)
                j = KW - 1 - d
                acc = acc + taps(j, c) * part[d : d + GROUP]
                dtaps[j : j + 1, lanes] += jnp.sum(
                    part[:GROUP] * old[8 - d : 8 - d + GROUP], axis=0, keepdims=True
                )
            gp[pl.ds(base, GROUP), lanes] = acc.astype(bf16)

            @pl.when(n == groups - 1)
            def _():
                last[:, lanes] = acc[GROUP - TAIL :]

        return 0

    lax.fori_loop(0, groups, taps_back, 0)


def hid_kernel(tp, gp_in, last, incoming, dgate, dbeta, wq, wk, wv, wg, wb, x, gp, send, keep, gain_part):
    total = gp.shape[0]
    width = wq.shape[1]
    gp[: total - TAIL] = gp_in[: total - TAIL]
    fixed = jnp.concatenate([last[: TAIL - 8], last[TAIL - 8 :] + incoming[...]], axis=0)
    gp[total - TAIL :] = fixed.astype(bf16)
    share = total // 4
    for half in range(2):
        blocks = [rows_of(tp[0] ^ (2 * half + j), share) for j in range(2)]
        cat = lambda ref: jnp.concatenate([ref[b] for b in blocks], axis=0)
        grads = cat(gp)
        acc = dot(cat(dgate), wg[...], 1, 1)
        small = cat(dbeta).astype(f32)
        for h in range(wb.shape[0]):
            acc = acc + small[:, h : h + 1] * wb[h : h + 1].astype(f32)
        for i, w in enumerate((wq, wk, wv)):
            acc = acc + dot(grads[:, i * width : (i + 1) * width], w[...], 1, 1)
        v = cat(x).astype(f32)
        r = lax.rsqrt(jnp.mean(v * v, axis=-1, keepdims=True) + row_epsilon)
        part = jnp.sum(acc * (v * r), axis=0, keepdims=True)
        gain_part[...] = part if half == 0 else gain_part[...] + part
        keep[half] = acc[:share]
        send[half] = acc[share:].astype(bf16)


def in_kernel(kept, got, x, gain, grad_residual, grad_in):
    gh = kept[...] + got[...].astype(f32)
    v = x[...].astype(f32)
    g = wide_gain(gain)
    r = lax.rsqrt(jnp.mean(v * v, axis=-1, keepdims=True) + row_epsilon)
    e = gh * g
    back = r * e - v * (r * r * r) * jnp.mean(e * v, axis=-1, keepdims=True)
    grad_in[...] = (grad_residual[...] + back).astype(bf16)


def outblock_kernel(tp, meta, kept, got, residual, out):
    total = residual[...] + kept[...] + got[...].astype(f32)
    live = live_mask(meta, tp[0], total.shape[0])
    out[...] = jnp.where(live, total, 0.0).astype(bf16)


def place_kernel(tp, a0, a1, a2, a3, out):
    for rel, part in enumerate((a0, a1, a2, a3)):
        out[rows_of(tp[0] ^ rel, part.shape[0])] = part[...].astype(out.dtype)


def swap(value, bit, axis="tp"):
    count = lax.axis_size(axis)
    return lax.ppermute(value, axis, [(i, i ^ bit) for i in range(count)])


def add_kernel(keep, got, kept, send):
    half = kept.shape[0]
    kept[...] = keep[:half] + got[:half].astype(f32)
    send[...] = (keep[half:] + got[half:].astype(f32)).astype(bf16)


def last_kernel(keep, got, own):
    own[...] = (keep[...] + got[...].astype(f32)).astype(bf16)


def pack_kernel(a, b, out):
    half = a.shape[0]
    out[:half] = a[...]
    out[half:] = b[...]


def fold(order, keep, got, name):
    half = (keep.shape[0] // 2, *keep.shape[1:])
    return order.run(add_kernel, name, [(half, f32), (half, bf16)], [keep, got])


def rank_of(m, bits):
    at = 0
    for bit in bits:
        at = 2 * at + ((m >> bit) & 1)
    return at


class Plan:
    def __init__(self, index, bits, base, size, start=0, folds=1, lane=0):
        self.index, self.bits, self.base, self.size = index, bits, base, size
        self.start, self.folds, self.lane = start, folds, lane

    def rest(self):
        return self.bits, self.base, self.size, self.start, self.folds, self.lane


def put(acc, wide, place, plans, sums):
    for part in plans:
        keep, send = sums[2 * part.index : 2 * part.index + 2]
        height = part.size // part.folds
        for m in range(1 << len(part.bits)):
            at = rank_of(m, part.bits[1:])
            low = (m >> part.bits[0]) & 1
            for i in range(part.folds):
                begin = part.start + (m ^ place) * part.size + i * height
                block = acc[pl.ds(pl.multiple_of(begin, 8), height), part.lane : part.lane + wide]
                rows = slice(part.base, part.base + height)
                lanes = slice(i * wide, (i + 1) * wide)
                if low:
                    send[at, rows, lanes] = block.astype(bf16)
                else:
                    keep[at, rows, lanes] = block


def take(out, place, part, bits, near, far, send=None):
    height = part.size // part.folds
    wide = out.shape[1]
    for m in range(1 << len(bits)):
        source = far if (m >> bits[-1]) & 1 else near
        at = rank_of(m, bits[-2::-1])
        start = part.start + (m ^ place) * part.size
        for i in range(part.folds):
            out[pl.ds(pl.multiple_of(start + i * height, 8), height)] = source[
                at, part.base : part.base + height, i * wide : (i + 1) * wide
            ].astype(f32)
        if send is not None:
            send(pl.ds(pl.multiple_of(start, 8), part.size))


class Sum:
    def __init__(self, order, keep, send, scatter, gather, tag):
        self.order, self.tag, self.gather = order, tag, gather
        self.keep, self.left = keep, list(scatter)
        self.swap(send)
        self.own = self.near = None

    def swap(self, send):
        self.got = swap(send, 1 << self.left.pop(0), "seq")

    def step(self):
        order, tag = self.order, self.tag
        if self.own is None and self.left:
            self.keep, send = fold(order, self.keep, self.got, tag + "_fold")
            self.swap(send)
            return
        if self.own is None:
            (self.own,) = order.run(
                last_kernel, tag + "_last", [(self.keep.shape, bf16)], [self.keep, self.got]
            )
            more = 1 << len(self.gather)
            while more < lax.axis_size("seq"):
                other = swap(self.own, more, "seq")
                self.own = (self.own.astype(f32) + other.astype(f32)).astype(bf16)
                more *= 2
            self.left = list(self.gather)
        else:
            twice = (2 * self.own.shape[0], *self.own.shape[1:])
            (self.own,) = order.run(
                pack_kernel, tag + "_pack", [(twice, bf16)], [self.own, self.got]
            )
        self.swap(self.own)


def pair_kernel(keep_a, got_a, keep_b, got_b, kept, send):
    kept[...] = keep_a[...] + got_a[...].astype(f32)
    send[...] = (keep_b[...] + got_b[...].astype(f32)).astype(bf16)


def fold_pair(order, keep_a, got_a, keep_b, got_b):
    shape = keep_a.shape
    return order.run(
        pair_kernel, "fold_tp", [(shape, f32), (shape, bf16)], [keep_a, got_a, keep_b, got_b]
    )


def scatter_first(order, keep, send):
    return fold(order, keep, swap(send, 1), "fold_tp")


def grads_c_kernel(plans, place, hidden, gp, *refs):
    sums, acc = refs[:-1], refs[-1]
    acc[...] = dot(hidden[...], gp[...], 0, 0)
    put(acc, acc.shape[1] // 3, (place[0] & 7), plans, sums)


def grads_d_kernel(plans, way, base, place, attended, branch, hidden, dgate, small, gains, keep, send, acc, acc2, both):
    sums = (keep, send)
    acc[...] = dot(attended[...], branch[...], 0, 0)
    put(acc, acc.shape[1], (place[0] & 7), plans[:1], sums)
    acc2[...] = dot(hidden[...], dgate[...], 0, 0)
    put(acc2, acc2.shape[1], (place[0] & 7), plans[1:], sums)
    both[...] = small[...] + gains[...]
    for m in range(1 << len(way)):
        line = both[pl.ds(m ^ (place[0] & 7), 1)] + jnp.zeros((8, both.shape[1]), f32)
        at = rank_of(m, way[1:])
        if (m >> way[0]) & 1:
            send[at, base : base + 8] = line.astype(bf16)
        else:
            keep[at, base : base + 8] = line


def settle_kernel(count, jobs, line_at, place, *refs):
    pairs, refs = refs[: 2 * count], refs[2 * count :]
    size = len(jobs)
    outs, (staged, sem) = refs[: len(refs) - size - 1], (refs[len(refs) - size - 1 : -1], refs[-1])
    copies = []
    for parts, out, stage in zip(jobs, outs, staged):

        def send(rows):
            copy = pltpu.make_async_copy(stage.at[rows], out.at[rows], sem.at[len(copies)])
            copy.start()
            copies.append(copy)

        for part, way in parts:
            take(
                stage,
                (place[0] & 7),
                part,
                way,
                *pairs[2 * part.index : 2 * part.index + 2],
                send,
            )
    if line_at is not None:
        index, way, base = line_at
        near, far = pairs[2 * index : 2 * index + 2]
        for m in range(1 << len(way)):
            source = far if (m >> way[-1]) & 1 else near
            at = rank_of(m, way[-2::-1])
            outs[-1][pl.ds(m ^ (place[0] & 7), 1)] = source[at, base : base + 8].astype(f32)[:1]
    for copy in copies:
        copy.wait()


def sum_shapes(blocks, rows, cols):
    return [((blocks // 2, rows, cols), f32), ((blocks // 2, rows, cols), bf16)]


def gather_rel(own):
    near = swap(own, 1)
    far = swap(own, 2)
    return own, near, far, swap(far, 1)


def shift(value, steps):
    count = lax.axis_size("seq")
    pairs = [(i, i + steps) for i in range(count) if 0 <= i + steps < count]
    return lax.ppermute(value, "seq", pairs)


def hops_of(dev, last, sign, reach):
    return [shift(dev, sign * k) for k in range(1, reach)] + [shift(last, sign * reach)]


def small_kernel(dtaps, dbeta, hidden, in_part, mid_part, head_part, local, gains):
    wide = dtaps.shape[1]
    local[...] = jnp.zeros(local.shape, f32)
    local[0:KW, :wide] = dtaps[...]
    local[KW : KW + 2] = dot(dbeta[...], hidden[...], 0, 0)[:2]
    gains[...] = jnp.zeros(gains.shape, f32)
    gains[KW + 2 : KW + 3] = in_part[...]
    gains[KW + 3 : KW + 4] = mid_part[...]
    gains[0:1, wide : wide + head_part.shape[1]] = head_part[...]


def plus_kernel(a, b, out):
    out[...] = a[...] + b[...]


def plus(order, a, b):
    return order.run(plus_kernel, "plus", [(a.shape, f32)], [a, b])[0]


def shards(
    layer_input,
    seq_groups,
    seq_pads,
    norm_in,
    w_query,
    w_key,
    w_value,
    conv_query,
    conv_key,
    conv_value,
    w_beta,
    w_gate_out,
    norm_head,
    w_out,
    norm_mid,
    w_gate,
    w_up,
    w_down,
    cotangent,
):
    total, model = layer_input.shape
    width = w_query.shape[1]
    heads = width // DH
    groups = total // GROUP
    share = total // 4
    ffw = w_gate.shape[1]
    seq_count = lax.axis_size("seq")
    reach = max(1, seq_count // 4)
    tp_rank = lax.axis_index("tp")
    tp = tp_rank.astype(jnp.int32).reshape(1)
    blocks = 8
    place = lax.axis_index("seq").astype(jnp.int32).reshape(1)
    taps = (conv_query, conv_key, conv_value)
    wb = w_beta.T
    tail = shift(layer_input[total - TAIL :], 1)
    chains = groups * heads
    wide = (total, width)
    mats = 2 * total * model
    order = Order()
    run = order.run

    def begin(keep, send, scatter, gather, tag):
        made = Sum(order, keep, send, scatter, gather, tag)
        made.place = place
        return made

    weight = pltpu.VMEM((model, width), bf16)
    rows = pltpu.VMEM((total, model), bf16)
    ext_shape = (total + TAIL, 3 * width)
    conv_shape = (total, 3 * width)
    inv_shape = (chains, GROUP, GROUP)
    map_shape = (chains, DH, DH)
    zst_shape = (chains, DH, 2 * DH)
    dev_shapes = [((heads, DH, 2 * DH), f32), ((heads, DH, DH), f32)]
    near = "near"
    far = "far"
    tp_sums = [((2, share, model), bf16), ((2, share, model), f32)]
    (
        gate_raw, beta_raw, meta, qkv, wmix, umix, score, zst, dev, last,
        hidden, grad_down, x_own, gd_own, ext, conv, inv, amap,
    ) = run(
        front_kernel,
        "front",
        [
            (wide, f32, near),
            ((total, heads), f32, near),
            ((2, groups), jnp.int32),
            (conv_shape, f32, near),
            (wide, f32, near),
            (wide, f32, near),
            (inv_shape, f32, near),
            (zst_shape, f32, near),
            *dev_shapes,
            ((total, model), bf16, far),
            ((total, model), bf16, far),
            ((share, model), bf16, far),
            ((share, model), bf16, far),
            (ext_shape, f32, far),
            (conv_shape, f32, far),
            (inv_shape, f32, far),
            (map_shape, f32, far),
        ],
        [place, tp, seq_groups, seq_pads, layer_input, cotangent, norm_in, w_query, w_key, w_value, w_gate_out, wb, tail, *taps],
        smem=(0, 1, 2, 3),
        smem_out=(2,),
        hbm=(4, 5, 7, 8, 9, 10),
        pin=(2, 3, 4, 5, 6, 7, 8, 9, 10, 11, 13, 14, 15),
        scratch=[
            rows, rows, weight, weight, weight, weight, rows, rows,
            pltpu.VMEM(ext_shape, f32),
            pltpu.VMEM(conv_shape, f32),
            pltpu.VMEM(inv_shape, f32),
            pltpu.VMEM(map_shape, f32),
            pltpu.VMEM(map_shape, f32),
            pltpu.SemaphoreType.DMA((6,)),
            pltpu.SemaphoreType.DMA((8,)),
        ],
        vmem=22,
    )
    hops = hops_of(dev, last, 1, reach)
    mout, oloc = run(
        local_kernel, "local", [(wide, f32, near)] * 2, [qkv, wmix, umix, score, zst]
    )
    heads_out, attended, send, keep, entry = run(
        lambda *r: out_kernel(reach, *r),
        "out",
        [(wide, f32, near), (wide, bf16, near), *tp_sums, ((heads, DH, DH), f32)],
        [tp, *hops, mout, oloc, gate_raw, norm_head, w_out],
        smem=(0,),
    )
    kept, cross = scatter_first(order, keep, send)
    got = swap(cross, 2)
    states, vnew, qeff = run(
        states_kernel,
        "states",
        [(map_shape, f32, near), (wide, f32, near), (wide, f32, near)],
        [entry, zst, qkv, wmix, umix, score],
    )
    residual, second_own = run(
        mid_kernel,
        "mid",
        [((share, model), f32, near), ((share, model), bf16)],
        [x_own, kept[0], got[0], norm_mid],
    )
    size = ffw // blocks
    ways = [WAYS[name] for name in ("f1", "f2", "f3", "f4")]
    flows = {}

    def go(slot):
        for name in STEPS[slot]:
            flows[name].step()

    near_up = size // 16 * 8
    far_up = size - near_up
    down_parts = [Plan(0, ways[0][0], 0, size)]
    gate_parts = [Plan(1, ways[1][0], 0, size)]
    up_parts = [
        Plan(0, ways[0][0], size, near_up),
        Plan(1, ways[1][0], size, far_up, start=near_up * blocks),
    ]
    plans_a = (down_parts, gate_parts, up_parts)
    f1_rows, f2_rows = size + near_up, size + far_up
    own_rows, beside_rows = second_own, swap(second_own, 1)
    far_rows = swap(second_own, 2)
    w_shape = (ffw, model)
    wg, wu, wd, gd, grad_inner = run(
        warm_kernel,
        "warm",
        [
            (w_shape, bf16, near),
            (w_shape, bf16, near),
            (w_shape, bf16, near),
            ((total, model), bf16, near),
            ((total, ffw), f32, near),
        ],
        [w_gate.T, w_up.T, w_down, grad_down],
        hbm=(0, 1, 2, 3),
        pin=(0, 1, 2, 3),
        scratch=[pltpu.SemaphoreType.DMA((4,))],
    )
    part = (1, share, model)
    half_ffn = ((2 * share, ffw), bf16)
    half_outs = [(part, f32), (part, bf16)] * 2
    sec_a, inner_a, dgate_a, dup_a, down_keep_a, down_send_a, keep_a, send_a = run(
        ffn_a_kernel,
        "ffn_a",
        [((2 * share, model), bf16), half_ffn, half_ffn, half_ffn, *half_outs],
        [tp, own_rows, beside_rows, wg, wu, wd, grad_inner],
        smem=(0,),
        vmem=12,
    )
    far_rows, sec_a = lax.optimization_barrier((far_rows, sec_a))
    near_a = swap(send_a, 1)
    down_near_a = swap(down_send_a, 1)
    down_keep_b, down_send_b, keep_b, send_b, *sums = run(
        lambda *r: ffn_b_kernel(plans_a, *r),
        "ffn_b",
        [*half_outs, *sum_shapes(blocks, f1_rows, model), *sum_shapes(blocks, f2_rows, model)],
        [tp, place, far_rows, swap(far_rows, 1), wg, wu, wd, grad_inner, gd, sec_a, inner_a, dgate_a, dup_a],
        smem=(0, 1),
        scratch=[
            pltpu.VMEM((2 * share, model), bf16),
            *[pltpu.VMEM((2 * share, ffw), bf16)] * 3,
            pltpu.VMEM((ffw, model), f32),
        ],
        vmem=16,
    )
    near_b = swap(send_b, 1)
    flows["f1"] = begin(sums[0], sums[1], *ways[0], "f1")
    flows["f2"] = begin(sums[2], sums[3], *ways[1], "f2")
    kept, cross = fold_pair(order, keep_a, near_a, keep_b, near_b)
    got = swap(cross, 2)
    grad_residual, branch_own, mid_part = run(
        turn_kernel,
        "turn",
        [((share, model), f32), ((share, model), bf16), ((1, model), f32)],
        [kept[0], got[0], residual, norm_mid, gd_own],
    )
    branch_all = gather_rel(branch_own)
    branch, dgate_raw, dout, rst, dev, last, head_part = run(
        flow_kernel,
        "flow",
        [
            ((total, model), bf16),
            (wide, bf16),
            (wide, f32),
            (zst_shape, f32),
            *[(shape, bf16) for shape, _ in dev_shapes],
            ((1, DH), f32),
        ],
        [tp, meta, *branch_all, w_out, heads_out, gate_raw, norm_head, qeff, amap],
        smem=(0, 1),
        scratch=[pltpu.VMEM(map_shape, f32), pltpu.VMEM(dev_shapes[0][0], f32)],
    )
    hops = hops_of(dev, last, -1, reach)
    down_near_b = swap(down_send_b, 1)
    ndo, dq, dk = run(
        side_kernel,
        "side",
        [(wide, f32)] * 3,
        [qkv, dout, vnew, states, score],
    )
    down_kept, cross = fold_pair(order, down_keep_a, down_near_a, down_keep_b, down_near_b)
    down_got = swap(cross, 2)
    order.wait(*hops)
    go("hops")
    dc, halo, dbeta = run(
        lambda *r: back_kernel(reach, *r),
        "back",
        [((total + 8, 3 * width), f32), ((8, 3 * width), f32), ((total, LANES), bf16)],
        [meta, *hops, rst, qkv, conv, *taps, beta_raw, inv, states, vnew, ndo, dq, dk],
        smem=(0,),
    )
    incoming = shift(halo, -1)
    go("back")
    gp, last, dtaps = run(
        taps_kernel,
        "taps",
        [(conv_shape, bf16), ((TAIL, 3 * width), f32), ((KW, 3 * width), f32)],
        [meta, dc, ext, *taps],
        smem=(0,),
    )
    (out_own,) = run(
        outblock_kernel,
        "outblk",
        [((share, model), bf16)],
        [tp, meta, down_kept[0], down_got[0], residual],
        smem=(0, 1),
    )
    go("taps")
    gp, send, keep, in_part = run(
        hid_kernel,
        "hid",
        [(conv_shape, bf16), *tp_sums, ((1, model), f32)],
        [tp, gp, last, incoming, dgate_raw, dbeta, w_query, w_key, w_value, w_gate_out, wb, layer_input],
        smem=(0,),
        vmem=12,
    )
    beside = swap(send, 1)
    piece = model // blocks
    fold_rows = piece * width // model
    split = dict(folds=model // width)
    plans_c = [
        Plan(0, ways[2][0], i * fold_rows, piece, lane=i * width, **split) for i in range(3)
    ]
    keep_c, send_c = run(
        lambda *r: grads_c_kernel(plans_c, *r),
        "grads_c",
        sum_shapes(blocks, 3 * fold_rows, model),
        [place, hidden, gp],
        smem=(0,),
        scratch=[pltpu.VMEM((model, 3 * width), f32)],
        vmem=16,
    )
    flows["f3"] = begin(keep_c, send_c, *ways[2], "f3")
    go("hid")
    kept, cross = fold(order, keep, beside, "fold_tp")
    got = swap(cross, 2)
    row8 = ((8, model), f32)
    small, gains = run(
        small_kernel, "small", [row8, row8], [dtaps, dbeta, hidden, in_part, mid_part, head_part]
    )
    gains = plus(order, gains, swap(gains, 1))
    far_gains = swap(gains, 2)
    go("x")
    (grad_in_own,) = run(
        in_kernel,
        "inp",
        [((share, model), bf16)],
        [kept[0], got[0], x_own, norm_in, grad_residual],
    )
    grad_in_all = gather_rel(grad_in_own)
    gains = plus(order, gains, far_gains)
    wo_rows = width // blocks
    out_parts = [Plan(0, ways[3][0], 0, wo_rows)]
    gate_out_parts = [Plan(0, ways[3][0], wo_rows, piece, **split)]
    line_base = wo_rows + fold_rows
    keep_d, send_d = run(
        lambda *r: grads_d_kernel(out_parts + gate_out_parts, ways[3][0], line_base, *r),
        "grads_d",
        sum_shapes(blocks, line_base + 8, model),
        [place, attended, branch, hidden, dgate_raw, small, gains],
        smem=(0,),
        scratch=[
            pltpu.VMEM((width, model), f32),
            pltpu.VMEM((model, width), f32),
            pltpu.VMEM((8, model), f32),
        ],
        vmem=12,
    )
    flows["f4"] = begin(keep_d, send_d, *ways[3], "f4")
    out_all = gather_rel(out_own)
    results = {}

    def settle(name, jobs, used, outs, line_at=None):
        return run(
            lambda *r: settle_kernel(len(used), jobs, line_at, *r),
            name,
            [(o, f32, far) for o in outs[: len(jobs)]] + [(o, f32) for o in outs[len(jobs) :]],
            [place, *[a for flow in used for a in (flows[flow].own, flows[flow].got)]],
            smem=(0,),
            scratch=[
                *[pltpu.VMEM(o, f32) for o in outs[: len(jobs)]],
                pltpu.SemaphoreType.DMA((blocks * sum(len(parts) for parts in jobs),)),
            ],
        )

    def wayed(parts, first_flow=0):
        moved = [Plan(p.index - first_flow, *p.rest()) for p in parts]
        return [(m, ways[p.index][1]) for m, p in zip(moved, parts)]

    def late(parts, flow):
        return [(part, ways[flow][1]) for part in parts]

    for name in STEPS["tail"]:
        if name in flows:
            flows[name].step()
        elif name in ("in", "out"):
            results[name] = run(
                place_kernel,
                "place_" + name,
                [((total, model), f32 if name == "in" else bf16)],
                [tp, *(grad_in_all if name == "in" else out_all)],
                smem=(0,),
            )
        elif name == "s1":
            results[name] = settle(
                "settle_1",
                [wayed(down_parts), wayed(up_parts)],
                ["f1", "f2"],
                [(ffw, model)] * 2,
            )
        elif name == "s2":
            results[name] = settle("settle_2", [wayed(gate_parts, 1)], ["f2"], [(ffw, model)])
        elif name == "s3":
            results[name] = settle(
                "settle_3", [late([part], 2) for part in plans_c], ["f3"], [(model, width)] * 3
            )
        else:
            results[name] = settle(
                "settle_4",
                [late(out_parts, 3), late(gate_out_parts, 3)],
                ["f4"],
                [(width, model), (model, width), (8, model)],
                line_at=(0, ways[3][1], line_base),
            )
    (grad_input,) = results["in"]
    (block_out,) = results["out"]
    grad_down_w, grad_up_w = results["s1"]
    (grad_gate_w,) = results["s2"]
    hidden_sums = results["s3"]
    grad_out_w, grad_gate_out_w, small = results["s4"]
    cut = model // 4
    head_cut = DH // 4
    gain_of = lambda row, size, lane=0: lax.dynamic_slice(
        small, (row, lane + tp_rank * size), (1, size)
    ).reshape(size)
    tap_of = lambda i: small[:KW, i * width : (i + 1) * width]
    return (
        block_out,
        grad_input,
        gain_of(KW + 2, cut),
        hidden_sums[0],
        hidden_sums[1],
        hidden_sums[2],
        tap_of(0),
        tap_of(1),
        tap_of(2),
        small[KW : KW + heads].T,
        grad_gate_out_w,
        gain_of(0, head_cut, 3 * width),
        grad_out_w,
        gain_of(KW + 3, cut),
        grad_gate_w.T,
        grad_up_w.T,
        grad_down_w,
    )


def solution(mesh):
    rows = P("seq", None)
    cols = P(None, "tp")
    return jax.shard_map(
        shards,
        mesh=mesh,
        in_specs=(rows, P(), P(), P(), cols, cols, cols, cols, cols, cols, cols, cols, P(), P("tp", None), P(), cols, cols, P("tp", None), rows),
        out_specs=(rows, rows, P("tp"), cols, cols, cols, cols, cols, cols, cols, cols, P("tp"), P("tp", None), P("tp"), cols, cols, P("tp", None)),
        check_vma=False,
    )
```

```python
import jax
import jax.numpy as jnp
from jax import lax
from jax.experimental import pallas as pl
from jax.experimental.pallas import tpu as pltpu
from jax.sharding import PartitionSpec as P

DH = 128
KW = 4
GROUP = 64
TAIL = 16
LANES = 128

row_epsilon = 1e-06
head_epsilon = 1e-05
unit_epsilon = 1e-06
f32 = jnp.float32
bf16 = jnp.bfloat16


def dot(a, b, ca=1, cb=0):
    return lax.dot_general(a, b, (((ca,), (cb,)), ((), ())), preferred_element_type=f32)


def halves(a):
    high = a.astype(bf16)
    return high, (a - high.astype(f32)).astype(bf16)


def fdot(a, b, ca=1, cb=0):
    ah, al = halves(a)
    bh, bl = halves(b)
    return dot(
        jnp.concatenate([ah, al, ah], axis=ca), jnp.concatenate([bh, bh, bl], axis=cb), ca, cb
    )


def gdot(a, b, ca=1, cb=0):
    return dot(a.astype(bf16), b.astype(bf16), ca, cb)


def iota(shape, axis):
    return lax.broadcasted_iota(jnp.int32, shape, axis)


def rows_of(block, size):
    return pl.ds(pl.multiple_of(block * size, size), size)


COST = 1153500
STEPS = {'hops': ['f2', 'f1'], 'back': ['f1', 'f2'], 'taps': ['f1'], 'hid': [], 'x': ['f2'], 'tail': ['f3', 'in', 'f4', 'out', 'f1', 'f4', 'f3', 'f2', 'f2', 'f4', 'f3', 'f1', 'f4', 'f3', 'f3', 'f4', 's1', 's2', 's4', 's3']}
WAYS = {'f1': ((0, 1, 2), (2, 1, 0)), 'f2': ((1, 0, 2), (2, 0, 1)), 'f3': ((0, 1, 2), (1, 2, 0)), 'f4': ((1, 0, 2), (2, 0, 1))}


class Order:
    def __init__(self):
        self.last = None
        self.also = ()

    def wait(self, *values):
        self.also = values

    def run(self, kernel, name, outs, args, smem=(), smem_out=(), hbm=(), pin=(), scratch=(), flops=COST, vmem=8):
        held = {"far": pltpu.HBM, "near": pltpu.VMEM}
        shapes = [
            held[o[2]](o[0], o[1]) if len(o) > 2 else jax.ShapeDtypeStruct(*o) for o in outs
        ]
        hbm_out = [i for i, o in enumerate(outs) if o[2:] == ("far",)]
        args = list(args)
        if self.last is not None:
            free = [i for i in range(len(args)) if i not in smem]
            at = min(free, key=lambda i: (i in pin, i))
            args[at] = lax.optimization_barrier((args[at], self.last, *self.also))[0]
            self.also = ()
        for i in pin:
            args[i] = pltpu.with_memory_space_constraint(args[i], pltpu.HBM)
        space = lambda i, low, far: pltpu.SMEM if i in low else pltpu.HBM if i in far else pltpu.VMEM
        made = pl.pallas_call(
            kernel,
            name=name,
            out_shape=shapes,
            in_specs=[pl.BlockSpec(memory_space=space(i, smem, hbm)) for i in range(len(args))],
            out_specs=[
                pl.BlockSpec(memory_space=space(i, smem_out, hbm_out)) for i in range(len(outs))
            ],
            scratch_shapes=list(scratch),
            compiler_params=pltpu.CompilerParams(vmem_limit_bytes=vmem << 20),
            cost_estimate=pl.CostEstimate(flops=flops, bytes_accessed=1, transcendentals=0),
        )(*args)
        kept = [i for i in range(len(made)) if i not in smem_out]
        self.last = made[min(kept, key=lambda i: (i in hbm_out, i))]
        return made


def wide_gain(ref):
    return ref[...].astype(f32).reshape(1, ref.shape[0])


def live_mask(meta, block, size):
    parts = size // GROUP
    row = iota((size, 1), 0)
    limit = jnp.full((size, 1), 0, jnp.int32) + meta[1, block * parts]
    for part in range(1, parts):
        limit = jnp.where(row >= part * GROUP, meta[1, block * parts + part] + part * GROUP, limit)
    return row < limit


def rms_rows(values, gain):
    factor = lax.rsqrt(jnp.mean(values * values, axis=-1, keepdims=True) + row_epsilon)
    return values * factor * gain


def beta_col(beta, meta, n, h):
    raw = beta[pl.ds(pl.multiple_of(n * GROUP, GROUP), GROUP), h : h + 1]
    sig = jax.nn.sigmoid(raw)
    live = iota((GROUP, 1), 0) < meta[1, n]
    return jnp.where(live, sig, 0.0), sig, live


def unit(rows):
    return rows * lax.rsqrt(jnp.sum(rows * rows, axis=-1, keepdims=True) + unit_epsilon)


def tri_inverse(systems, block=16):
    size = systems[0].shape[0]
    row = iota((size, size), 0)
    col = iota((size, size), 1)
    eye = (row == col).astype(f32)
    tiles = [[eye[r : r + 8] for r in range(0, size, 8)] for _ in systems]
    lower = [[system[r : r + 8] for r in range(0, size, 8)] for system in systems]
    for step in range(block - 1):
        for low, part in zip(lower, tiles):
            for start in range(0, size, block):
                j = start + step
                line = part[j // 8][j % 8 : j % 8 + 1]
                for r in range((j + 1) // 8, (start + block) // 8):
                    part[r] = part[r] - low[r][:, j : j + 1] * line
    inverses = [jnp.concatenate(part, axis=0) for part in tiles]
    while block < size:
        pick = ((row // block) % 2 == 1) & (col // block == row // block - 1)
        mids = [
            fdot(inverse, jnp.where(pick, system, 0.0))
            for inverse, system in zip(inverses, systems)
        ]
        inverses = [inverse - fdot(mid, inverse) for mid, inverse in zip(mids, inverses)]
        block *= 2
    return inverses


def tap_table(*tables):
    values = [table[...].astype(f32) for table in tables]
    parts = values[0].shape[1] // DH
    return lambda j, c: values[c // parts][j : j + 1, (c % parts) * DH : (c % parts + 1) * DH]


def front_kernel(first, tp, seq_groups, seq_pads, xh, coth, gain, wqh, wkh, wvh, wgh, wb, tail, cq, ck, cv, gate, beta, meta, qkv, wmix, umix, score, zst, dev_low, last, hidden_h, gd_h, x_own, gd_own, ext_h, conv_h, inv_h, amap_h, x, cot, wq, wk, wv, wg, hidden, gd, ext, conv, inv, amap, badd, dev, sems, out_sems):
    loads = [
        pltpu.make_async_copy(src, dst, sems.at[i])
        for i, (src, dst) in enumerate(
            ((xh, x), (wqh, wq), (wkh, wk), (wvh, wv), (wgh, wg), (coth, cot))
        )
    ]
    for load in loads:
        load.start()
    groups = x.shape[0] // GROUP
    for n in range(groups):
        meta[0, n] = 0
        meta[1, n] = 0

    def one(s, start):
        count = seq_groups[s]
        length = count * GROUP - seq_pads[s]
        for n in range(groups):
            gid = first[0] * groups + n
            inside = (gid >= start) & (gid < start + count)
            here = jnp.clip(length - (gid - start) * GROUP, 0, GROUP)
            meta[0, n] = jnp.where(gid == start, 1, meta[0, n])
            meta[1, n] = jnp.where(inside, here, meta[1, n])
        return start + count

    lax.fori_loop(0, seq_groups.shape[0], one, jnp.int32(0))
    width = wq.shape[1]
    heads = width // DH
    tile = 256
    share = x_own.shape[0]
    scale = wide_gain(gain)
    own = rows_of(tp[0], share)
    stores = []

    def store(src, dst):
        copy = pltpu.make_async_copy(src, dst, out_sems.at[len(stores)])
        copy.start()
        stores.append(copy)

    loads[0].wait()
    store(x.at[own], x_own)
    tiles = [slice(t * tile, (t + 1) * tile) for t in range(x.shape[0] // tile)]
    for rows in tiles:
        hidden[rows] = rms_rows(x[rows].astype(f32), scale).astype(bf16)
    store(hidden, hidden_h)
    low = rms_rows(tail[...].astype(f32), scale).astype(bf16)
    for rows in tiles:
        beta[rows] = dot(hidden[rows], wb[...], 1, 1)
    for i, w in enumerate((wq, wk, wv, wg)):
        loads[1 + i].wait()
        lanes = slice(i * width, (i + 1) * width)
        for rows in tiles:
            got = dot(hidden[rows], w[...])
            if i < 3:
                ext[TAIL + rows.start : TAIL + rows.stop, lanes] = got
            else:
                gate[rows] = got
        if i < 3:
            ext[0:TAIL, lanes] = dot(low, w[...])
    store(ext, ext_h)
    loads[5].wait()
    for t, rows in enumerate(tiles):
        live = live_mask(meta, t, tile)
        gd[rows] = jnp.where(live, cot[rows].astype(f32), 0.0).astype(bf16)
    store(gd, gd_h)
    store(gd.at[own], gd_own)
    row = iota((GROUP, 1), 0)
    taps = tap_table(cq, ck, cv)

    def front(n):
        base = pl.multiple_of(n * GROUP, GROUP)
        for c in range(3 * heads):
            lanes = slice(c * DH, (c + 1) * DH)
            win = ext[pl.ds(pl.multiple_of(base + TAIL - 8, 8), GROUP + 8), lanes]
            acc = taps(KW - 1, c) * win[8:]
            for d in range(1, KW):
                part = jnp.where(row < meta[0, n] * d, 0.0, win[8 - d : 8 - d + GROUP])
                acc = acc + taps(KW - 1 - d, c) * part
            conv[pl.ds(base, GROUP), lanes] = acc
            acted = acc * jax.nn.sigmoid(acc)
            qkv[pl.ds(base, GROUP), lanes] = unit(acted) if c < 2 * heads else acted

    pl.loop(0, groups)(front)
    store(conv, conv_h)
    r64 = iota((GROUP, GROUP), 0)
    c64 = iota((GROUP, GROUP), 1)
    eye = (iota((DH, DH), 0) == iota((DH, DH), 1)).astype(f32)

    def load(n, h):
        rows = pl.ds(pl.multiple_of(n * GROUP, GROUP), GROUP)
        return [qkv[rows, (i * heads + h) * DH : (i * heads + h + 1) * DH] for i in range(3)]

    def local(i, _):
        chains = [(j, h) for j in range(groups) for h in range(heads)]
        systems = []
        kept = []
        for n, h in chains:
            q, k, v = load(n, h)
            b = beta_col(beta, meta, n, h)[0]
            both = fdot(jnp.concatenate([k * b, q], axis=0), k, 1, 1)
            systems.append(jnp.where(r64 > c64, both[:GROUP], 0.0))
            score[n * heads + h] = jnp.where(r64 >= c64, both[GROUP:], 0.0)
            kept.append((k, b, v))
        inverses = tri_inverse(systems)
        for (n, h), inverse, (k, b, v) in zip(chains, inverses, kept):
            rows = pl.ds(pl.multiple_of(n * GROUP, GROUP), GROUP)
            inv[n * heads + h] = inverse
            wu = fdot(inverse, jnp.concatenate([k * b, v * b], axis=1))
            wmix[rows, h * DH : (h + 1) * DH] = wu[:, :DH]
            umix[rows, h * DH : (h + 1) * DH] = wu[:, DH:]
            kwu = fdot(k, wu, 0, 0)
            amap[n * heads + h] = eye - kwu[:, :DH]
            badd[n * heads + h] = kwu[:, DH:]
        return 0

    local(0, 0)
    store(inv, inv_h)
    store(amap, amap_h)
    for h in range(heads):
        dev[h, :, :DH] = eye
        dev[h, :, DH:] = jnp.zeros((DH, DH), f32)

    def chain(n, _):
        keep = 1.0 - meta[0, n].astype(f32)
        for h in range(heads):
            start = dev[h] * keep
            zst[n * heads + h] = start
            moved = fdot(amap[n * heads + h], start)
            dev[h, :, :DH] = moved[:, :DH]
            dev[h, :, DH:] = moved[:, DH:] + badd[n * heads + h]
        return 0

    lax.fori_loop(0, groups, chain, 0)
    dev_low[...] = dev[...].astype(bf16)
    last[...] = dev[:, :, DH:].astype(bf16)

    for copy in stores:
        copy.wait()


def local_kernel(qkv, wmix, umix, score, zst, mout, oloc):
    groups = qkv.shape[0] // GROUP
    heads = wmix.shape[1] // DH

    def one(i, _):
        for n, h in [(2 * i + j, h) for j in range(2) for h in range(heads)]:
            rows = pl.ds(pl.multiple_of(n * GROUP, GROUP), GROUP)
            lanes = slice(h * DH, (h + 1) * DH)
            q = qkv[rows, lanes]
            both = fdot(jnp.concatenate([q, wmix[rows, lanes]], axis=0), zst[n * heads + h])
            lower = jnp.concatenate(
                [-both[GROUP:, :DH], umix[rows, lanes] - both[GROUP:, DH:]], axis=1
            )
            made = both[:GROUP] + fdot(score[n * heads + h], lower)
            mout[rows, lanes] = made[:, :DH]
            oloc[rows, lanes] = made[:, DH:]
        return 0

    lax.fori_loop(0, groups // 2, one, 0)


def fold_hops(hops, h):
    state = hops[-1][h].astype(f32)
    for hop in hops[-2::-1]:
        state = hop[h, :, DH:].astype(f32) + fdot(hop[h, :, :DH].astype(f32), state)
    return state


def out_kernel(hop_count, tp, *refs):
    hops, refs = refs[:hop_count], refs[hop_count:]
    mout, oloc, gate, nh, wo, heads_out, att, send, keep, entry = refs
    heads = gate.shape[1] // DH
    states = [fold_hops(hops, h) for h in range(heads)]
    for h in range(heads):
        entry[h] = states[h]
    share = mout.shape[0] // 4
    for rel in range(4):
        rows = rows_of(tp[0] ^ rel, share)
        lows = []
        for h in range(heads):
            lanes = slice(h * DH, (h + 1) * DH)
            o = oloc[rows, lanes] + fdot(mout[rows, lanes], states[h])
            heads_out[rows, lanes] = o
            factor = lax.rsqrt(jnp.mean(o * o, axis=-1, keepdims=True) + head_epsilon)
            g = gate[rows, lanes]
            lows.append((o * factor * wide_gain(nh) * (g * jax.nn.sigmoid(g))).astype(bf16))
        low = jnp.concatenate(lows, axis=1)
        att[rows] = low
        part = dot(low, wo[...])
        if rel % 2:
            send[rel // 2] = part.astype(bf16)
        else:
            keep[rel // 2] = part


def states_kernel(entry, zst, qkv, wmix, umix, score, states, vnew, qeff):
    groups = qkv.shape[0] // GROUP
    heads = wmix.shape[1] // DH

    def one(i, _):
        for n, h in [(2 * i + j, h) for j in range(2) for h in range(heads)]:
            rows = pl.ds(pl.multiple_of(n * GROUP, GROUP), GROUP)
            lanes = slice(h * DH, (h + 1) * DH)
            at = n * heads + h
            s = zst[at, :, DH:] + fdot(zst[at, :, :DH], entry[h])
            states[at] = s
            w = wmix[rows, lanes]
            vnew[rows, lanes] = umix[rows, lanes] - fdot(w, s)
            qeff[rows, lanes] = qkv[rows, lanes] - fdot(score[at], w)
        return 0

    lax.fori_loop(0, groups // 2, one, 0)


def mid_kernel(x, kept, got, gain, residual, second):
    total = x[...].astype(f32) + kept[...] + got[...].astype(f32)
    residual[...] = total
    second[...] = rms_rows(total, wide_gain(gain)).astype(bf16)


def warm_kernel(wgh, wuh, wdh, gdh, wg, wu, wd, gd, grad_inner, sems):
    loads = [
        pltpu.make_async_copy(src, dst, sems.at[i])
        for i, (src, dst) in enumerate(((wdh, wd), (gdh, gd), (wgh, wg), (wuh, wu)))
    ]
    for load in loads:
        load.start()
    loads[0].wait()
    loads[1].wait()
    tile = 256
    for t in range(gd.shape[0] // tile):
        rows = slice(t * tile, (t + 1) * tile)
        grad_inner[rows] = dot(gd[rows], wd[...], 1, 1)
    loads[2].wait()
    loads[3].wait()


def ffn_half(tp, half, sa, sb, wg, wu, wd, grad_inner, sec, inner, dgate, dup, down_keep, down_send, keep, send):
    share = sa.shape[0]
    sec[:share] = sa[...]
    sec[share:] = sb[...]
    gv = dot(sec[...], wg[...], 1, 1)
    uv = dot(sec[...], wu[...], 1, 1)
    sig = jax.nn.sigmoid(gv)
    act = gv * sig
    inn = (act * uv).astype(bf16)
    gi = jnp.concatenate(
        [grad_inner[rows_of(tp[0] ^ (2 * half + j), share)] for j in range(2)], axis=0
    )
    dg = (gi * uv * (sig * (1.0 + gv * (1.0 - sig)))).astype(bf16)
    du = (gi * act).astype(bf16)
    inner[...] = inn
    dgate[...] = dg
    dup[...] = du
    grad = dot(dg, wg[...]) + dot(du, wu[...])
    keep[0] = grad[:share]
    send[0] = grad[share:].astype(bf16)
    down = dot(inn, wd[...])
    down_keep[0] = down[:share]
    down_send[0] = down[share:].astype(bf16)


def ffn_a_kernel(tp, sa, sb, wg, wu, wd, grad_inner, *outs):
    ffn_half(tp, 0, sa, sb, wg, wu, wd, grad_inner, *outs)


def ffn_b_kernel(plans, tp, place, sa, sb, wg, wu, wd, grad_inner, gd, sec_a, inner_a, dgate_a, dup_a, down_keep, down_send, keep, send, *refs):
    sums, (sec, inner, dgate, dup, acc) = refs[:-5], refs[-5:]
    share = sa.shape[0]
    ffn_half(tp, 1, sa, sb, wg, wu, wd, grad_inner, sec, inner, dgate, dup, down_keep, down_send, keep, send)
    near = [jnp.concatenate([gd[rows_of(tp[0] ^ (2 * i + j), share)] for j in range(2)], axis=0) for i in range(2)]
    for pair, plan in (
        (((inner_a[...], near[0]), (inner[...], near[1])), 0),
        (((dgate_a[...], sec_a[...]), (dgate[...], sec[...])), 1),
        (((dup_a[...], sec_a[...]), (dup[...], sec[...])), 2),
    ):
        acc[...] = dot(*pair[0], 0, 0) + dot(*pair[1], 0, 0)
        put(acc, acc.shape[1], (place[0] & 7), plans[plan], sums)


def turn_kernel(kept, got, residual, gain, grad_y, grad_residual, branch, gain_part):
    gs = kept[...] + got[...].astype(f32)
    v = residual[...]
    g = wide_gain(gain)
    r = lax.rsqrt(jnp.mean(v * v, axis=-1, keepdims=True) + row_epsilon)
    gain_part[...] = jnp.sum(gs * v * r, axis=0, keepdims=True)
    e = gs * g
    back = r * e - v * (r * r * r) * jnp.mean(e * v, axis=-1, keepdims=True)
    total = grad_y[...].astype(f32) + back
    grad_residual[...] = total
    branch[...] = total.astype(bf16)


def flow_kernel(tp, meta, b0, b1, b2, b3, wo, heads_out, gate, nh, qeff, amap, branch, dgate, dout, rst, dev_low, last, nh_part, flows, dev):
    share = b0.shape[0]
    heads = gate.shape[1] // DH
    groups = gate.shape[0] // GROUP
    gains = jnp.zeros((1, DH), f32)
    for half, pair in enumerate(((b0, b1), (b2, b3))):
        both = jnp.concatenate([pair[0][...], pair[1][...]], axis=0)
        ga = dot(both, wo[...], 1, 1)
        for j in range(2):
            rows = rows_of(tp[0] ^ (2 * half + j), share)
            branch[rows] = pair[j][...]
            for h in range(heads):
                lanes = slice(h * DH, (h + 1) * DH)
                gz = ga[j * share : (j + 1) * share, lanes]
                o = heads_out[rows, lanes]
                g = gate[rows, lanes]
                gain = wide_gain(nh)
                r = lax.rsqrt(jnp.mean(o * o, axis=-1, keepdims=True) + head_epsilon)
                sig = jax.nn.sigmoid(g)
                act = g * sig
                e = gz * gain * act
                base = gz * o * r
                gains = gains + jnp.sum(base * act, axis=0, keepdims=True)
                dgate[rows, lanes] = (base * gain * (sig * (1.0 + g * (1.0 - sig)))).astype(bf16)
                dout[rows, lanes] = r * e - o * (r * r * r) * jnp.mean(e * o, axis=-1, keepdims=True)
    nh_part[...] = gains

    def local(i, _):
        for n, h in [(2 * i + j, h) for j in range(2) for h in range(heads)]:
            rows = pl.ds(pl.multiple_of(n * GROUP, GROUP), GROUP)
            lanes = slice(h * DH, (h + 1) * DH)
            flows[n * heads + h] = fdot(qeff[rows, lanes], dout[rows, lanes], 0, 0)
        return 0

    lax.fori_loop(0, groups // 2, local, 0)
    eye = (iota((DH, DH), 0) == iota((DH, DH), 1)).astype(f32)
    for h in range(heads):
        dev[h, :, :DH] = eye
        dev[h, :, DH:] = jnp.zeros((DH, DH), f32)

    def chain(i, _):
        n = groups - 1 - i
        keep = 1.0 - meta[0, n].astype(f32)
        for h in range(heads):
            at = n * heads + h
            later = dev[h]
            rst[at] = later
            moved = fdot(amap[at], later, 0, 0)
            dev[h, :, :DH] = moved[:, :DH] * keep
            dev[h, :, DH:] = (moved[:, DH:] + flows[at]) * keep
        return 0

    lax.fori_loop(0, groups, chain, 0)
    dev_low[...] = dev[...].astype(bf16)
    last[...] = dev[:, :, DH:].astype(bf16)


def side_kernel(qkv, dout, vnew, states, score, ndo, dq, dk):
    heads = dout.shape[1] // DH
    groups = dout.shape[0] // GROUP
    lower = iota((GROUP, GROUP), 0) >= iota((GROUP, GROUP), 1)

    def one(i, _):
        for n, h in [(2 * i + j, h) for j in range(2) for h in range(heads)]:
            rows = pl.ds(pl.multiple_of(n * GROUP, GROUP), GROUP)
            lanes = slice(h * DH, (h + 1) * DH)
            at = n * heads + h
            q = qkv[rows, lanes]
            k = qkv[rows, (heads + h) * DH : (heads + h + 1) * DH]
            do = dout[rows, lanes]
            ndo[rows, lanes] = fdot(score[at], do, 0, 0)
            dn = jnp.where(lower, fdot(do, vnew[rows, lanes], 1, 1), 0.0)
            dq[rows, lanes] = fdot(do, states[at], 1, 1) + fdot(dn, k)
            dk[rows, lanes] = fdot(dn, q, 0, 0)
        return 0

    lax.fori_loop(0, groups // 2, one, 0)


def unit_back(a, grad):
    r = lax.rsqrt(jnp.sum(a * a, axis=-1, keepdims=True) + unit_epsilon)
    return r * grad - a * (r * r * r) * jnp.sum(a * grad, axis=-1, keepdims=True)


def back_kernel(hop_count, meta, *refs):
    hops, refs = refs[:hop_count], refs[hop_count:]
    rst, qkv, conv, cq, ck, cv, beta, inv, states, vnew, ndo, dq, dk1, dc, halo, dbeta = refs
    taps = tap_table(cq, ck, cv)
    heads = ndo.shape[1] // DH
    groups = ndo.shape[0] // GROUP
    total = ndo.shape[0]
    exits = [fold_hops(hops, h) for h in range(heads)]
    strict = iota((GROUP, GROUP), 0) > iota((GROUP, GROUP), 1)
    lane = iota((GROUP, LANES), 1)
    dc[total:] = jnp.zeros((8, dc.shape[1]), f32)

    def one(i, _):
        for j in range(2):
            n = 2 * i + j
            rows = pl.ds(pl.multiple_of(n * GROUP, GROUP), GROUP)
            raws = jnp.zeros((GROUP, LANES), f32)
            for h in range(heads):
                at = n * heads + h
                lanes = [slice((p * heads + h) * DH, (p * heads + h + 1) * DH) for p in range(3)]
                k = qkv[rows, lanes[1]]
                v = qkv[rows, lanes[2]]
                b, sig, live = beta_col(beta, meta, n, h)
                ds = rst[at, :, DH:] + gdot(rst[at, :, :DH], exits[h])
                dvn = ndo[rows, lanes[0]] + gdot(k, ds)
                d = gdot(inv[at], dvn, 0, 0)
                vn = vnew[rows, lanes[0]]
                both = gdot(d, jnp.concatenate([states[at], vn], axis=0), 1, 1)
                dstate = both[:, :DH]
                vds = gdot(vn, ds, 1, 1)
                da = jnp.where(strict, -both[:, DH:], 0.0)
                dak = gdot(da, k)
                datk = gdot(da, k * b, 0, 0)
                dk = dk1[rows, lanes[0]] + vds + b * (dak - dstate) + datk
                db = jnp.sum(d * v + (dak - dstate) * k, axis=-1, keepdims=True)
                db = jnp.where(live, db * sig * (1.0 - sig), 0.0)
                raws = jnp.where(lane == h, db, raws)
                grads = (dq[rows, lanes[0]], dk, d * b)
                for p in range(3):
                    c = conv[rows, lanes[p]]
                    s = jax.nn.sigmoid(c)
                    grad = unit_back(c * s, grads[p]) if p < 2 else grads[p]
                    dc[rows, lanes[p]] = grad * (s * (1.0 + c * (1.0 - s)))
            dbeta[rows] = raws.astype(bf16)
        return 0

    lax.fori_loop(0, groups // 2, one, 0)
    zero = jnp.zeros((8, DH), f32)
    for c in range(3 * heads):
        lanes = slice(c * DH, (c + 1) * DH)
        win = dc[0:8, lanes]
        acc = zero
        for d in range(1, KW):
            part = jnp.where(iota((8, 1), 0) < meta[0, 0] * d, 0.0, win)
            j = KW - 1 - d
            acc = acc + taps(j, c) * jnp.concatenate([zero, part], axis=0)[d : d + 8]
        halo[:, lanes] = acc


def taps_kernel(meta, dc, ext, cq, ck, cv, gp, last, dtaps):
    heads = cq.shape[1] // DH
    groups = gp.shape[0] // GROUP
    taps = tap_table(cq, ck, cv)
    dtaps[...] = jnp.zeros(dtaps.shape, f32)

    def masked(win, d, here, after):
        front = jnp.where(iota((GROUP, 1), 0) < here * d, 0.0, win[:GROUP])
        if after is None:
            return front
        back = jnp.where(iota((8, 1), 0) < after * d, 0.0, win[GROUP:])
        return jnp.concatenate([front, back], axis=0)

    def taps_back(n, _):
        base = pl.multiple_of(n * GROUP, GROUP)
        here = meta[0, n]
        after = meta[0, jnp.minimum(n + 1, groups - 1)]
        for c in range(3 * heads):
            lanes = slice(c * DH, (c + 1) * DH)
            win = dc[pl.ds(base, GROUP + 8), lanes]
            old = ext[pl.ds(pl.multiple_of(base + TAIL - 8, 8), GROUP + 8), lanes]
            acc = taps(KW - 1, c) * win[:GROUP]
            dtaps[KW - 1 : KW, lanes] += jnp.sum(win[:GROUP] * old[8:], axis=0, keepdims=True)
            for d in range(1, KW):
                part = masked(win, d, here, after)
                j = KW - 1 - d
                acc = acc + taps(j, c) * part[d : d + GROUP]
                dtaps[j : j + 1, lanes] += jnp.sum(
                    part[:GROUP] * old[8 - d : 8 - d + GROUP], axis=0, keepdims=True
                )
            gp[pl.ds(base, GROUP), lanes] = acc.astype(bf16)

            @pl.when(n == groups - 1)
            def _():
                last[:, lanes] = acc[GROUP - TAIL :]

        return 0

    lax.fori_loop(0, groups, taps_back, 0)


def hid_kernel(tp, gp_in, last, incoming, dgate, dbeta, wq, wk, wv, wg, wb, x, gp, send, keep, gain_part):
    total = gp.shape[0]
    width = wq.shape[1]
    gp[: total - TAIL] = gp_in[: total - TAIL]
    fixed = jnp.concatenate([last[: TAIL - 8], last[TAIL - 8 :] + incoming[...]], axis=0)
    gp[total - TAIL :] = fixed.astype(bf16)
    share = total // 4
    for half in range(2):
        blocks = [rows_of(tp[0] ^ (2 * half + j), share) for j in range(2)]
        cat = lambda ref: jnp.concatenate([ref[b] for b in blocks], axis=0)
        grads = cat(gp)
        acc = dot(cat(dgate), wg[...], 1, 1)
        small = cat(dbeta).astype(f32)
        for h in range(wb.shape[0]):
            acc = acc + small[:, h : h + 1] * wb[h : h + 1].astype(f32)
        for i, w in enumerate((wq, wk, wv)):
            acc = acc + dot(grads[:, i * width : (i + 1) * width], w[...], 1, 1)
        v = cat(x).astype(f32)
        r = lax.rsqrt(jnp.mean(v * v, axis=-1, keepdims=True) + row_epsilon)
        part = jnp.sum(acc * (v * r), axis=0, keepdims=True)
        gain_part[...] = part if half == 0 else gain_part[...] + part
        keep[half] = acc[:share]
        send[half] = acc[share:].astype(bf16)


def in_kernel(kept, got, x, gain, grad_residual, grad_in):
    gh = kept[...] + got[...].astype(f32)
    v = x[...].astype(f32)
    g = wide_gain(gain)
    r = lax.rsqrt(jnp.mean(v * v, axis=-1, keepdims=True) + row_epsilon)
    e = gh * g
    back = r * e - v * (r * r * r) * jnp.mean(e * v, axis=-1, keepdims=True)
    grad_in[...] = (grad_residual[...] + back).astype(bf16)


def outblock_kernel(tp, meta, kept, got, residual, out):
    total = residual[...] + kept[...] + got[...].astype(f32)
    live = live_mask(meta, tp[0], total.shape[0])
    out[...] = jnp.where(live, total, 0.0).astype(bf16)


def place_kernel(tp, a0, a1, a2, a3, out):
    for rel, part in enumerate((a0, a1, a2, a3)):
        out[rows_of(tp[0] ^ rel, part.shape[0])] = part[...].astype(out.dtype)


def swap(value, bit, axis="tp"):
    count = lax.axis_size(axis)
    return lax.ppermute(value, axis, [(i, i ^ bit) for i in range(count)])


def add_kernel(keep, got, kept, send):
    half = kept.shape[0]
    kept[...] = keep[:half] + got[:half].astype(f32)
    send[...] = (keep[half:] + got[half:].astype(f32)).astype(bf16)


def last_kernel(keep, got, own):
    own[...] = (keep[...] + got[...].astype(f32)).astype(bf16)


def pack_kernel(a, b, out):
    half = a.shape[0]
    out[:half] = a[...]
    out[half:] = b[...]


def fold(order, keep, got, name):
    half = (keep.shape[0] // 2, *keep.shape[1:])
    return order.run(add_kernel, name, [(half, f32), (half, bf16)], [keep, got])


def rank_of(m, bits):
    at = 0
    for bit in bits:
        at = 2 * at + ((m >> bit) & 1)
    return at


class Plan:
    def __init__(self, index, bits, base, size, start=0, folds=1, lane=0):
        self.index, self.bits, self.base, self.size = index, bits, base, size
        self.start, self.folds, self.lane = start, folds, lane

    def rest(self):
        return self.bits, self.base, self.size, self.start, self.folds, self.lane


def put(acc, wide, place, plans, sums):
    for part in plans:
        keep, send = sums[2 * part.index : 2 * part.index + 2]
        height = part.size // part.folds
        for m in range(1 << len(part.bits)):
            at = rank_of(m, part.bits[1:])
            low = (m >> part.bits[0]) & 1
            for i in range(part.folds):
                begin = part.start + (m ^ place) * part.size + i * height
                block = acc[pl.ds(pl.multiple_of(begin, 8), height), part.lane : part.lane + wide]
                rows = slice(part.base, part.base + height)
                lanes = slice(i * wide, (i + 1) * wide)
                if low:
                    send[at, rows, lanes] = block.astype(bf16)
                else:
                    keep[at, rows, lanes] = block


def take(out, place, part, bits, near, far, send=None):
    height = part.size // part.folds
    wide = out.shape[1]
    for m in range(1 << len(bits)):
        source = far if (m >> bits[-1]) & 1 else near
        at = rank_of(m, bits[-2::-1])
        start = part.start + (m ^ place) * part.size
        for i in range(part.folds):
            out[pl.ds(pl.multiple_of(start + i * height, 8), height)] = source[
                at, part.base : part.base + height, i * wide : (i + 1) * wide
            ].astype(f32)
        if send is not None:
            send(pl.ds(pl.multiple_of(start, 8), part.size))


class Sum:
    def __init__(self, order, keep, send, scatter, gather, tag):
        self.order, self.tag, self.gather = order, tag, gather
        self.keep, self.left = keep, list(scatter)
        self.swap(send)
        self.own = self.near = None

    def swap(self, send):
        self.got = swap(send, 1 << self.left.pop(0), "seq")

    def step(self):
        order, tag = self.order, self.tag
        if self.own is None and self.left:
            self.keep, send = fold(order, self.keep, self.got, tag + "_fold")
            self.swap(send)
            return
        if self.own is None:
            (self.own,) = order.run(
                last_kernel, tag + "_last", [(self.keep.shape, bf16)], [self.keep, self.got]
            )
            more = 1 << len(self.gather)
            while more < lax.axis_size("seq"):
                other = swap(self.own, more, "seq")
                self.own = (self.own.astype(f32) + other.astype(f32)).astype(bf16)
                more *= 2
            self.left = list(self.gather)
        else:
            twice = (2 * self.own.shape[0], *self.own.shape[1:])
            (self.own,) = order.run(
                pack_kernel, tag + "_pack", [(twice, bf16)], [self.own, self.got]
            )
        self.swap(self.own)


def pair_kernel(keep_a, got_a, keep_b, got_b, kept, send):
    kept[...] = keep_a[...] + got_a[...].astype(f32)
    send[...] = (keep_b[...] + got_b[...].astype(f32)).astype(bf16)


def fold_pair(order, keep_a, got_a, keep_b, got_b):
    shape = keep_a.shape
    return order.run(
        pair_kernel, "fold_tp", [(shape, f32), (shape, bf16)], [keep_a, got_a, keep_b, got_b]
    )


def scatter_first(order, keep, send):
    return fold(order, keep, swap(send, 1), "fold_tp")


def grads_c_kernel(plans, place, hidden, gp, *refs):
    sums, acc = refs[:-1], refs[-1]
    acc[...] = dot(hidden[...], gp[...], 0, 0)
    put(acc, acc.shape[1] // 3, (place[0] & 7), plans, sums)


def grads_d_kernel(plans, way, base, place, attended, branch, hidden, dgate, small, gains, keep, send, acc, acc2, both):
    sums = (keep, send)
    acc[...] = dot(attended[...], branch[...], 0, 0)
    put(acc, acc.shape[1], (place[0] & 7), plans[:1], sums)
    acc2[...] = dot(hidden[...], dgate[...], 0, 0)
    put(acc2, acc2.shape[1], (place[0] & 7), plans[1:], sums)
    both[...] = small[...] + gains[...]
    for m in range(1 << len(way)):
        line = both[pl.ds(m ^ (place[0] & 7), 1)] + jnp.zeros((8, both.shape[1]), f32)
        at = rank_of(m, way[1:])
        if (m >> way[0]) & 1:
            send[at, base : base + 8] = line.astype(bf16)
        else:
            keep[at, base : base + 8] = line


def settle_kernel(count, jobs, line_at, place, *refs):
    pairs, refs = refs[: 2 * count], refs[2 * count :]
    size = len(jobs)
    outs, (staged, sem) = refs[: len(refs) - size - 1], (refs[len(refs) - size - 1 : -1], refs[-1])
    copies = []
    for parts, out, stage in zip(jobs, outs, staged):

        def send(rows):
            copy = pltpu.make_async_copy(stage.at[rows], out.at[rows], sem.at[len(copies)])
            copy.start()
            copies.append(copy)

        for part, way in parts:
            take(
                stage,
                (place[0] & 7),
                part,
                way,
                *pairs[2 * part.index : 2 * part.index + 2],
                send,
            )
    if line_at is not None:
        index, way, base = line_at
        near, far = pairs[2 * index : 2 * index + 2]
        for m in range(1 << len(way)):
            source = far if (m >> way[-1]) & 1 else near
            at = rank_of(m, way[-2::-1])
            outs[-1][pl.ds(m ^ (place[0] & 7), 1)] = source[at, base : base + 8].astype(f32)[:1]
    for copy in copies:
        copy.wait()


def sum_shapes(blocks, rows, cols):
    return [((blocks // 2, rows, cols), f32), ((blocks // 2, rows, cols), bf16)]


def gather_rel(own):
    near = swap(own, 1)
    far = swap(own, 2)
    return own, near, far, swap(far, 1)


def shift(value, steps):
    count = lax.axis_size("seq")
    pairs = [(i, i + steps) for i in range(count) if 0 <= i + steps < count]
    return lax.ppermute(value, "seq", pairs)


def hops_of(dev, last, sign, reach):
    return [shift(dev, sign * k) for k in range(1, reach)] + [shift(last, sign * reach)]


def small_kernel(dtaps, dbeta, hidden, in_part, mid_part, head_part, local, gains):
    wide = dtaps.shape[1]
    local[...] = jnp.zeros(local.shape, f32)
    local[0:KW, :wide] = dtaps[...]
    local[KW : KW + 2] = dot(dbeta[...], hidden[...], 0, 0)[:2]
    gains[...] = jnp.zeros(gains.shape, f32)
    gains[KW + 2 : KW + 3] = in_part[...]
    gains[KW + 3 : KW + 4] = mid_part[...]
    gains[0:1, wide : wide + head_part.shape[1]] = head_part[...]


def plus_kernel(a, b, out):
    out[...] = a[...] + b[...]


def plus(order, a, b):
    return order.run(plus_kernel, "plus", [(a.shape, f32)], [a, b])[0]


def shards(
    layer_input,
    seq_groups,
    seq_pads,
    norm_in,
    w_query,
    w_key,
    w_value,
    conv_query,
    conv_key,
    conv_value,
    w_beta,
    w_gate_out,
    norm_head,
    w_out,
    norm_mid,
    w_gate,
    w_up,
    w_down,
    cotangent,
):
    total, model = layer_input.shape
    width = w_query.shape[1]
    heads = width // DH
    groups = total // GROUP
    share = total // 4
    ffw = w_gate.shape[1]
    seq_count = lax.axis_size("seq")
    reach = max(1, seq_count // 4)
    tp_rank = lax.axis_index("tp")
    tp = tp_rank.astype(jnp.int32).reshape(1)
    blocks = 8
    place = lax.axis_index("seq").astype(jnp.int32).reshape(1)
    taps = (conv_query, conv_key, conv_value)
    wb = w_beta.T
    tail = shift(layer_input[total - TAIL :], 1)
    chains = groups * heads
    wide = (total, width)
    mats = 2 * total * model
    order = Order()
    run = order.run

    def begin(keep, send, scatter, gather, tag):
        made = Sum(order, keep, send, scatter, gather, tag)
        made.place = place
        return made

    weight = pltpu.VMEM((model, width), bf16)
    rows = pltpu.VMEM((total, model), bf16)
    ext_shape = (total + TAIL, 3 * width)
    conv_shape = (total, 3 * width)
    inv_shape = (chains, GROUP, GROUP)
    map_shape = (chains, DH, DH)
    zst_shape = (chains, DH, 2 * DH)
    dev_shapes = [((heads, DH, 2 * DH), f32), ((heads, DH, DH), f32)]
    near = "near"
    far = "far"
    tp_sums = [((2, share, model), bf16), ((2, share, model), f32)]
    (
        gate_raw, beta_raw, meta, qkv, wmix, umix, score, zst, dev, last,
        hidden, grad_down, x_own, gd_own, ext, conv, inv, amap,
    ) = run(
        front_kernel,
        "front",
        [
            (wide, f32, near),
            ((total, heads), f32, near),
            ((2, groups), jnp.int32),
            (conv_shape, f32, near),
            (wide, f32, near),
            (wide, f32, near),
            (inv_shape, f32, near),
            (zst_shape, f32, near),
            *[(shape, bf16) for shape, _ in dev_shapes],
            ((total, model), bf16, far),
            ((total, model), bf16, far),
            ((share, model), bf16, far),
            ((share, model), bf16, far),
            (ext_shape, f32, far),
            (conv_shape, f32, far),
            (inv_shape, f32, far),
            (map_shape, f32, far),
        ],
        [place, tp, seq_groups, seq_pads, layer_input, cotangent, norm_in, w_query, w_key, w_value, w_gate_out, wb, tail, *taps],
        smem=(0, 1, 2, 3),
        smem_out=(2,),
        hbm=(4, 5, 7, 8, 9, 10),
        pin=(2, 3, 4, 5, 6, 7, 8, 9, 10, 11, 13, 14, 15),
        scratch=[
            rows, rows, weight, weight, weight, weight, rows, rows,
            pltpu.VMEM(ext_shape, f32),
            pltpu.VMEM(conv_shape, f32),
            pltpu.VMEM(inv_shape, f32),
            pltpu.VMEM(map_shape, f32),
            pltpu.VMEM(map_shape, f32),
            pltpu.VMEM(dev_shapes[0][0], f32),
            pltpu.SemaphoreType.DMA((6,)),
            pltpu.SemaphoreType.DMA((8,)),
        ],
        vmem=22,
    )
    hops = hops_of(dev, last, 1, reach)
    mout, oloc = run(
        local_kernel, "local", [(wide, f32, near)] * 2, [qkv, wmix, umix, score, zst]
    )
    heads_out, attended, send, keep, entry = run(
        lambda *r: out_kernel(reach, *r),
        "out",
        [(wide, f32, near), (wide, bf16, near), *tp_sums, ((heads, DH, DH), f32)],
        [tp, *hops, mout, oloc, gate_raw, norm_head, w_out],
        smem=(0,),
    )
    kept, cross = scatter_first(order, keep, send)
    got = swap(cross, 2)
    states, vnew, qeff = run(
        states_kernel,
        "states",
        [(map_shape, f32, near), (wide, f32, near), (wide, f32, near)],
        [entry, zst, qkv, wmix, umix, score],
    )
    residual, second_own = run(
        mid_kernel,
        "mid",
        [((share, model), f32, near), ((share, model), bf16)],
        [x_own, kept[0], got[0], norm_mid],
    )
    size = ffw // blocks
    ways = [WAYS[name] for name in ("f1", "f2", "f3", "f4")]
    flows = {}

    def go(slot):
        for name in STEPS[slot]:
            flows[name].step()

    near_up = size // 16 * 8
    far_up = size - near_up
    down_parts = [Plan(0, ways[0][0], 0, size)]
    gate_parts = [Plan(1, ways[1][0], 0, size)]
    up_parts = [
        Plan(0, ways[0][0], size, near_up),
        Plan(1, ways[1][0], size, far_up, start=near_up * blocks),
    ]
    plans_a = (down_parts, gate_parts, up_parts)
    f1_rows, f2_rows = size + near_up, size + far_up
    own_rows, beside_rows = second_own, swap(second_own, 1)
    far_rows = swap(second_own, 2)
    w_shape = (ffw, model)
    wg, wu, wd, gd, grad_inner = run(
        warm_kernel,
        "warm",
        [
            (w_shape, bf16, near),
            (w_shape, bf16, near),
            (w_shape, bf16, near),
            ((total, model), bf16, near),
            ((total, ffw), f32, near),
        ],
        [w_gate.T, w_up.T, w_down, grad_down],
        hbm=(0, 1, 2, 3),
        pin=(0, 1, 2, 3),
        scratch=[pltpu.SemaphoreType.DMA((4,))],
    )
    part = (1, share, model)
    half_ffn = ((2 * share, ffw), bf16)
    half_outs = [(part, f32), (part, bf16)] * 2
    sec_a, inner_a, dgate_a, dup_a, down_keep_a, down_send_a, keep_a, send_a = run(
        ffn_a_kernel,
        "ffn_a",
        [((2 * share, model), bf16), half_ffn, half_ffn, half_ffn, *half_outs],
        [tp, own_rows, beside_rows, wg, wu, wd, grad_inner],
        smem=(0,),
        vmem=12,
    )
    far_rows, sec_a = lax.optimization_barrier((far_rows, sec_a))
    near_a = swap(send_a, 1)
    down_near_a = swap(down_send_a, 1)
    down_keep_b, down_send_b, keep_b, send_b, *sums = run(
        lambda *r: ffn_b_kernel(plans_a, *r),
        "ffn_b",
        [*half_outs, *sum_shapes(blocks, f1_rows, model), *sum_shapes(blocks, f2_rows, model)],
        [tp, place, far_rows, swap(far_rows, 1), wg, wu, wd, grad_inner, gd, sec_a, inner_a, dgate_a, dup_a],
        smem=(0, 1),
        scratch=[
            pltpu.VMEM((2 * share, model), bf16),
            *[pltpu.VMEM((2 * share, ffw), bf16)] * 3,
            pltpu.VMEM((ffw, model), f32),
        ],
        vmem=16,
    )
    near_b = swap(send_b, 1)
    flows["f1"] = begin(sums[0], sums[1], *ways[0], "f1")
    flows["f2"] = begin(sums[2], sums[3], *ways[1], "f2")
    kept, cross = fold_pair(order, keep_a, near_a, keep_b, near_b)
    got = swap(cross, 2)
    grad_residual, branch_own, mid_part = run(
        turn_kernel,
        "turn",
        [((share, model), f32), ((share, model), bf16), ((1, model), f32)],
        [kept[0], got[0], residual, norm_mid, gd_own],
    )
    branch_all = gather_rel(branch_own)
    branch, dgate_raw, dout, rst, dev, last, head_part = run(
        flow_kernel,
        "flow",
        [
            ((total, model), bf16),
            (wide, bf16),
            (wide, f32),
            (zst_shape, f32),
            *[(shape, bf16) for shape, _ in dev_shapes],
            ((1, DH), f32),
        ],
        [tp, meta, *branch_all, w_out, heads_out, gate_raw, norm_head, qeff, amap],
        smem=(0, 1),
        scratch=[pltpu.VMEM(map_shape, f32), pltpu.VMEM(dev_shapes[0][0], f32)],
    )
    hops = hops_of(dev, last, -1, reach)
    down_near_b = swap(down_send_b, 1)
    ndo, dq, dk = run(
        side_kernel,
        "side",
        [(wide, f32)] * 3,
        [qkv, dout, vnew, states, score],
    )
    down_kept, cross = fold_pair(order, down_keep_a, down_near_a, down_keep_b, down_near_b)
    down_got = swap(cross, 2)
    order.wait(*hops)
    go("hops")
    dc, halo, dbeta = run(
        lambda *r: back_kernel(reach, *r),
        "back",
        [((total + 8, 3 * width), f32), ((8, 3 * width), f32), ((total, LANES), bf16)],
        [meta, *hops, rst, qkv, conv, *taps, beta_raw, inv, states, vnew, ndo, dq, dk],
        smem=(0,),
    )
    incoming = shift(halo, -1)
    go("back")
    gp, last, dtaps = run(
        taps_kernel,
        "taps",
        [(conv_shape, bf16), ((TAIL, 3 * width), f32), ((KW, 3 * width), f32)],
        [meta, dc, ext, *taps],
        smem=(0,),
    )
    (out_own,) = run(
        outblock_kernel,
        "outblk",
        [((share, model), bf16)],
        [tp, meta, down_kept[0], down_got[0], residual],
        smem=(0, 1),
    )
    go("taps")
    gp, send, keep, in_part = run(
        hid_kernel,
        "hid",
        [(conv_shape, bf16), *tp_sums, ((1, model), f32)],
        [tp, gp, last, incoming, dgate_raw, dbeta, w_query, w_key, w_value, w_gate_out, wb, layer_input],
        smem=(0,),
        vmem=12,
    )
    beside = swap(send, 1)
    piece = model // blocks
    fold_rows = piece * width // model
    split = dict(folds=model // width)
    plans_c = [
        Plan(0, ways[2][0], i * fold_rows, piece, lane=i * width, **split) for i in range(3)
    ]
    keep_c, send_c = run(
        lambda *r: grads_c_kernel(plans_c, *r),
        "grads_c",
        sum_shapes(blocks, 3 * fold_rows, model),
        [place, hidden, gp],
        smem=(0,),
        scratch=[pltpu.VMEM((model, 3 * width), f32)],
        vmem=16,
    )
    flows["f3"] = begin(keep_c, send_c, *ways[2], "f3")
    go("hid")
    kept, cross = fold(order, keep, beside, "fold_tp")
    got = swap(cross, 2)
    row8 = ((8, model), f32)
    small, gains = run(
        small_kernel, "small", [row8, row8], [dtaps, dbeta, hidden, in_part, mid_part, head_part]
    )
    gains = plus(order, gains, swap(gains, 1))
    far_gains = swap(gains, 2)
    go("x")
    (grad_in_own,) = run(
        in_kernel,
        "inp",
        [((share, model), bf16)],
        [kept[0], got[0], x_own, norm_in, grad_residual],
    )
    grad_in_all = gather_rel(grad_in_own)
    gains = plus(order, gains, far_gains)
    wo_rows = width // blocks
    out_parts = [Plan(0, ways[3][0], 0, wo_rows)]
    gate_out_parts = [Plan(0, ways[3][0], wo_rows, piece, **split)]
    line_base = wo_rows + fold_rows
    keep_d, send_d = run(
        lambda *r: grads_d_kernel(out_parts + gate_out_parts, ways[3][0], line_base, *r),
        "grads_d",
        sum_shapes(blocks, line_base + 8, model),
        [place, attended, branch, hidden, dgate_raw, small, gains],
        smem=(0,),
        scratch=[
            pltpu.VMEM((width, model), f32),
            pltpu.VMEM((model, width), f32),
            pltpu.VMEM((8, model), f32),
        ],
        vmem=12,
    )
    flows["f4"] = begin(keep_d, send_d, *ways[3], "f4")
    out_all = gather_rel(out_own)
    results = {}

    def settle(name, jobs, used, outs, line_at=None):
        return run(
            lambda *r: settle_kernel(len(used), jobs, line_at, *r),
            name,
            [(o, f32, far) for o in outs[: len(jobs)]] + [(o, f32) for o in outs[len(jobs) :]],
            [place, *[a for flow in used for a in (flows[flow].own, flows[flow].got)]],
            smem=(0,),
            scratch=[
                *[pltpu.VMEM(o, f32) for o in outs[: len(jobs)]],
                pltpu.SemaphoreType.DMA((blocks * sum(len(parts) for parts in jobs),)),
            ],
        )

    def wayed(parts, first_flow=0):
        moved = [Plan(p.index - first_flow, *p.rest()) for p in parts]
        return [(m, ways[p.index][1]) for m, p in zip(moved, parts)]

    def late(parts, flow):
        return [(part, ways[flow][1]) for part in parts]

    for name in STEPS["tail"]:
        if name in flows:
            flows[name].step()
        elif name in ("in", "out"):
            results[name] = run(
                place_kernel,
                "place_" + name,
                [((total, model), f32 if name == "in" else bf16)],
                [tp, *(grad_in_all if name == "in" else out_all)],
                smem=(0,),
            )
        elif name == "s1":
            results[name] = settle(
                "settle_1",
                [wayed(down_parts), wayed(up_parts)],
                ["f1", "f2"],
                [(ffw, model)] * 2,
            )
        elif name == "s2":
            results[name] = settle("settle_2", [wayed(gate_parts, 1)], ["f2"], [(ffw, model)])
        elif name == "s3":
            results[name] = settle(
                "settle_3", [late([part], 2) for part in plans_c], ["f3"], [(model, width)] * 3
            )
        else:
            results[name] = settle(
                "settle_4",
                [late(out_parts, 3), late(gate_out_parts, 3)],
                ["f4"],
                [(width, model), (model, width), (8, model)],
                line_at=(0, ways[3][1], line_base),
            )
    (grad_input,) = results["in"]
    (block_out,) = results["out"]
    grad_down_w, grad_up_w = results["s1"]
    (grad_gate_w,) = results["s2"]
    hidden_sums = results["s3"]
    grad_out_w, grad_gate_out_w, small = results["s4"]
    cut = model // 4
    head_cut = DH // 4
    gain_of = lambda row, size, lane=0: lax.dynamic_slice(
        small, (row, lane + tp_rank * size), (1, size)
    ).reshape(size)
    tap_of = lambda i: small[:KW, i * width : (i + 1) * width]
    return (
        block_out,
        grad_input,
        gain_of(KW + 2, cut),
        hidden_sums[0],
        hidden_sums[1],
        hidden_sums[2],
        tap_of(0),
        tap_of(1),
        tap_of(2),
        small[KW : KW + heads].T,
        grad_gate_out_w,
        gain_of(0, head_cut, 3 * width),
        grad_out_w,
        gain_of(KW + 3, cut),
        grad_gate_w.T,
        grad_up_w.T,
        grad_down_w,
    )


def solution(mesh):
    rows = P("seq", None)
    cols = P(None, "tp")
    return jax.shard_map(
        shards,
        mesh=mesh,
        in_specs=(rows, P(), P(), P(), cols, cols, cols, cols, cols, cols, cols, cols, P(), P("tp", None), P(), cols, cols, P("tp", None), rows),
        out_specs=(rows, rows, P("tp"), cols, cols, cols, cols, cols, cols, cols, cols, P("tp"), P("tp", None), P("tp"), cols, cols, P("tp", None)),
        check_vma=False,
    )
```

```python
import jax
import jax.numpy as jnp
from jax import lax
from jax.experimental import pallas as pl
from jax.experimental.pallas import tpu as pltpu
from jax.sharding import PartitionSpec as P

DH = 128
KW = 4
GROUP = 64
TAIL = 16
LANES = 128

row_epsilon = 1e-06
head_epsilon = 1e-05
unit_epsilon = 1e-06
f32 = jnp.float32
bf16 = jnp.bfloat16


def dot(a, b, ca=1, cb=0):
    return lax.dot_general(a, b, (((ca,), (cb,)), ((), ())), preferred_element_type=f32)


def halves(a):
    high = a.astype(bf16)
    return high, (a - high.astype(f32)).astype(bf16)


def fdot(a, b, ca=1, cb=0):
    ah, al = halves(a)
    bh, bl = halves(b)
    return dot(
        jnp.concatenate([ah, al, ah], axis=ca), jnp.concatenate([bh, bh, bl], axis=cb), ca, cb
    )


def gdot(a, b, ca=1, cb=0):
    return dot(a.astype(bf16), b.astype(bf16), ca, cb)


def iota(shape, axis):
    return lax.broadcasted_iota(jnp.int32, shape, axis)


def rows_of(block, size):
    return pl.ds(pl.multiple_of(block * size, size), size)


COST = 1153500
STEPS = {'hops': ['f2', 'f1'], 'back': ['f1', 'f2'], 'taps': ['f1'], 'hid': [], 'x': ['f2'], 'tail': ['f3', 'in', 'f4', 'out', 'f1', 'f4', 'f3', 'f2', 'f2', 'f4', 'f3', 'f1', 'f4', 'f3', 'f3', 'f4', 's1', 's2', 's4', 's3']}
WAYS = {'f1': ((0, 1, 2), (2, 1, 0)), 'f2': ((1, 0, 2), (2, 0, 1)), 'f3': ((0, 1, 2), (1, 2, 0)), 'f4': ((1, 0, 2), (2, 0, 1))}


class Order:
    def __init__(self):
        self.last = None
        self.also = ()

    def wait(self, *values):
        self.also = values

    def run(self, kernel, name, outs, args, smem=(), smem_out=(), hbm=(), pin=(), scratch=(), flops=COST, vmem=8):
        held = {"far": pltpu.HBM, "near": pltpu.VMEM}
        shapes = [
            held[o[2]](o[0], o[1]) if len(o) > 2 else jax.ShapeDtypeStruct(*o) for o in outs
        ]
        hbm_out = [i for i, o in enumerate(outs) if o[2:] == ("far",)]
        args = list(args)
        if self.last is not None:
            free = [i for i in range(len(args)) if i not in smem]
            at = min(free, key=lambda i: (i in pin, i))
            args[at] = lax.optimization_barrier((args[at], self.last, *self.also))[0]
            self.also = ()
        for i in pin:
            args[i] = pltpu.with_memory_space_constraint(args[i], pltpu.HBM)
        space = lambda i, low, far: pltpu.SMEM if i in low else pltpu.HBM if i in far else pltpu.VMEM
        made = pl.pallas_call(
            kernel,
            name=name,
            out_shape=shapes,
            in_specs=[pl.BlockSpec(memory_space=space(i, smem, hbm)) for i in range(len(args))],
            out_specs=[
                pl.BlockSpec(memory_space=space(i, smem_out, hbm_out)) for i in range(len(outs))
            ],
            scratch_shapes=list(scratch),
            compiler_params=pltpu.CompilerParams(vmem_limit_bytes=vmem << 20),
            cost_estimate=pl.CostEstimate(flops=flops, bytes_accessed=1, transcendentals=0),
        )(*args)
        kept = [i for i in range(len(made)) if i not in smem_out]
        self.last = made[min(kept, key=lambda i: (i in hbm_out, i))]
        return made


def wide_gain(ref):
    return ref[...].astype(f32).reshape(1, ref.shape[0])


def live_mask(meta, block, size):
    parts = size // GROUP
    row = iota((size, 1), 0)
    limit = jnp.full((size, 1), 0, jnp.int32) + meta[1, block * parts]
    for part in range(1, parts):
        limit = jnp.where(row >= part * GROUP, meta[1, block * parts + part] + part * GROUP, limit)
    return row < limit


def rms_rows(values, gain):
    factor = lax.rsqrt(jnp.mean(values * values, axis=-1, keepdims=True) + row_epsilon)
    return values * factor * gain


def beta_col(beta, meta, n, h):
    raw = beta[pl.ds(pl.multiple_of(n * GROUP, GROUP), GROUP), h : h + 1]
    sig = jax.nn.sigmoid(raw)
    live = iota((GROUP, 1), 0) < meta[1, n]
    return jnp.where(live, sig, 0.0), sig, live


def unit(rows):
    return rows * lax.rsqrt(jnp.sum(rows * rows, axis=-1, keepdims=True) + unit_epsilon)


def tri_inverse(systems, block=16):
    size = systems[0].shape[0]
    row = iota((size, size), 0)
    col = iota((size, size), 1)
    eye = (row == col).astype(f32)
    tiles = [[eye[r : r + 8] for r in range(0, size, 8)] for _ in systems]
    lower = [[system[r : r + 8] for r in range(0, size, 8)] for system in systems]
    for step in range(block - 1):
        for low, part in zip(lower, tiles):
            for start in range(0, size, block):
                j = start + step
                line = part[j // 8][j % 8 : j % 8 + 1]
                for r in range((j + 1) // 8, (start + block) // 8):
                    part[r] = part[r] - low[r][:, j : j + 1] * line
    inverses = [jnp.concatenate(part, axis=0) for part in tiles]
    while block < size:
        pick = ((row // block) % 2 == 1) & (col // block == row // block - 1)
        mids = [
            fdot(inverse, jnp.where(pick, system, 0.0))
            for inverse, system in zip(inverses, systems)
        ]
        inverses = [inverse - fdot(mid, inverse) for mid, inverse in zip(mids, inverses)]
        block *= 2
    return inverses


def tap_table(*tables):
    values = [table[...].astype(f32) for table in tables]
    parts = values[0].shape[1] // DH
    return lambda j, c: values[c // parts][j : j + 1, (c % parts) * DH : (c % parts + 1) * DH]


def front_kernel(first, tp, seq_groups, seq_pads, xh, coth, gain, wqh, wkh, wvh, wgh, wb, tail, cq, ck, cv, gate, beta, meta, qkv, wmix, umix, score, zst, dev_low, last, hidden_h, gd_h, x_own, gd_own, ext_h, conv_h, inv_h, amap_h, x, cot, wq, wk, wv, wg, hidden, gd, ext, conv, inv, amap, badd, dev, sems, out_sems):
    loads = [
        pltpu.make_async_copy(src, dst, sems.at[i])
        for i, (src, dst) in enumerate(
            ((xh, x), (wqh, wq), (wkh, wk), (wvh, wv), (wgh, wg), (coth, cot))
        )
    ]
    for load in loads:
        load.start()
    groups = x.shape[0] // GROUP
    for n in range(groups):
        meta[0, n] = 0
        meta[1, n] = 0

    def one(s, start):
        count = seq_groups[s]
        length = count * GROUP - seq_pads[s]
        for n in range(groups):
            gid = first[0] * groups + n
            inside = (gid >= start) & (gid < start + count)
            here = jnp.clip(length - (gid - start) * GROUP, 0, GROUP)
            meta[0, n] = jnp.where(gid == start, 1, meta[0, n])
            meta[1, n] = jnp.where(inside, here, meta[1, n])
        return start + count

    lax.fori_loop(0, seq_groups.shape[0], one, jnp.int32(0))
    width = wq.shape[1]
    heads = width // DH
    tile = 256
    share = x_own.shape[0]
    scale = wide_gain(gain)
    own = rows_of(tp[0], share)
    stores = []

    def store(src, dst):
        copy = pltpu.make_async_copy(src, dst, out_sems.at[len(stores)])
        copy.start()
        stores.append(copy)

    loads[0].wait()
    store(x.at[own], x_own)
    tiles = [slice(t * tile, (t + 1) * tile) for t in range(x.shape[0] // tile)]
    for rows in tiles:
        hidden[rows] = rms_rows(x[rows].astype(f32), scale).astype(bf16)
    store(hidden, hidden_h)
    low = rms_rows(tail[...].astype(f32), scale).astype(bf16)
    for rows in tiles:
        beta[rows] = dot(hidden[rows], wb[...], 1, 1)
    for i, w in enumerate((wq, wk, wv, wg)):
        loads[1 + i].wait()
        lanes = slice(i * width, (i + 1) * width)
        for rows in tiles:
            got = dot(hidden[rows], w[...])
            if i < 3:
                ext[TAIL + rows.start : TAIL + rows.stop, lanes] = got
            else:
                gate[rows] = got
        if i < 3:
            ext[0:TAIL, lanes] = dot(low, w[...])
    store(ext, ext_h)
    loads[5].wait()
    for t, rows in enumerate(tiles):
        live = live_mask(meta, t, tile)
        gd[rows] = jnp.where(live, cot[rows].astype(f32), 0.0).astype(bf16)
    store(gd, gd_h)
    store(gd.at[own], gd_own)
    row = iota((GROUP, 1), 0)
    taps = tap_table(cq, ck, cv)

    def front(n):
        base = pl.multiple_of(n * GROUP, GROUP)
        for c in range(3 * heads):
            lanes = slice(c * DH, (c + 1) * DH)
            win = ext[pl.ds(pl.multiple_of(base + TAIL - 8, 8), GROUP + 8), lanes]
            acc = taps(KW - 1, c) * win[8:]
            for d in range(1, KW):
                part = jnp.where(row < meta[0, n] * d, 0.0, win[8 - d : 8 - d + GROUP])
                acc = acc + taps(KW - 1 - d, c) * part
            conv[pl.ds(base, GROUP), lanes] = acc
            acted = acc * jax.nn.sigmoid(acc)
            qkv[pl.ds(base, GROUP), lanes] = unit(acted) if c < 2 * heads else acted

    pl.loop(0, groups)(front)
    store(conv, conv_h)
    r64 = iota((GROUP, GROUP), 0)
    c64 = iota((GROUP, GROUP), 1)
    eye = (iota((DH, DH), 0) == iota((DH, DH), 1)).astype(f32)

    def load(n, h):
        rows = pl.ds(pl.multiple_of(n * GROUP, GROUP), GROUP)
        return [qkv[rows, (i * heads + h) * DH : (i * heads + h + 1) * DH] for i in range(3)]

    def local(i, _):
        chains = [(j, h) for j in range(groups) for h in range(heads)]
        systems = []
        kept = []
        for n, h in chains:
            q, k, v = load(n, h)
            b = beta_col(beta, meta, n, h)[0]
            both = fdot(jnp.concatenate([k * b, q], axis=0), k, 1, 1)
            systems.append(jnp.where(r64 > c64, both[:GROUP], 0.0))
            score[n * heads + h] = jnp.where(r64 >= c64, both[GROUP:], 0.0)
            kept.append((k, b, v))
        inverses = tri_inverse(systems)
        for (n, h), inverse, (k, b, v) in zip(chains, inverses, kept):
            rows = pl.ds(pl.multiple_of(n * GROUP, GROUP), GROUP)
            inv[n * heads + h] = inverse
            wu = fdot(inverse, jnp.concatenate([k * b, v * b], axis=1))
            wmix[rows, h * DH : (h + 1) * DH] = wu[:, :DH]
            umix[rows, h * DH : (h + 1) * DH] = wu[:, DH:]
            kwu = fdot(k, wu, 0, 0)
            amap[n * heads + h] = eye - kwu[:, :DH]
            badd[n * heads + h] = kwu[:, DH:]
        return 0

    local(0, 0)
    store(inv, inv_h)
    store(amap, amap_h)
    for h in range(heads):
        dev[h, :, :DH] = eye
        dev[h, :, DH:] = jnp.zeros((DH, DH), f32)

    def chain(n, _):
        keep = 1.0 - meta[0, n].astype(f32)
        for h in range(heads):
            start = dev[h] * keep
            zst[n * heads + h] = start
            moved = fdot(amap[n * heads + h], start)
            dev[h, :, :DH] = moved[:, :DH]
            dev[h, :, DH:] = moved[:, DH:] + badd[n * heads + h]
        return 0

    lax.fori_loop(0, groups, chain, 0)
    dev_low[...] = dev[...].astype(bf16)
    last[...] = dev[:, :, DH:].astype(bf16)

    for copy in stores:
        copy.wait()


def local_kernel(qkv, wmix, umix, score, zst, mout, oloc):
    groups = qkv.shape[0] // GROUP
    heads = wmix.shape[1] // DH

    def one(i, _):
        for n, h in [(2 * i + j, h) for j in range(2) for h in range(heads)]:
            rows = pl.ds(pl.multiple_of(n * GROUP, GROUP), GROUP)
            lanes = slice(h * DH, (h + 1) * DH)
            q = qkv[rows, lanes]
            both = fdot(jnp.concatenate([q, wmix[rows, lanes]], axis=0), zst[n * heads + h])
            lower = jnp.concatenate(
                [-both[GROUP:, :DH], umix[rows, lanes] - both[GROUP:, DH:]], axis=1
            )
            made = both[:GROUP] + fdot(score[n * heads + h], lower)
            mout[rows, lanes] = made[:, :DH]
            oloc[rows, lanes] = made[:, DH:]
        return 0

    lax.fori_loop(0, groups // 2, one, 0)


def fold_hops(hops, h):
    state = hops[-1][h].astype(f32)
    for hop in hops[-2::-1]:
        state = hop[h, :, DH:].astype(f32) + fdot(hop[h, :, :DH].astype(f32), state)
    return state


def out_kernel(hop_count, tp, *refs):
    hops, refs = refs[:hop_count], refs[hop_count:]
    mout, oloc, gate, nh, wo, heads_out, att, send, keep, entry = refs
    heads = gate.shape[1] // DH
    states = [fold_hops(hops, h) for h in range(heads)]
    for h in range(heads):
        entry[h] = states[h]
    share = mout.shape[0] // 4
    for rel in range(4):
        rows = rows_of(tp[0] ^ rel, share)
        lows = []
        for h in range(heads):
            lanes = slice(h * DH, (h + 1) * DH)
            o = oloc[rows, lanes] + fdot(mout[rows, lanes], states[h])
            heads_out[rows, lanes] = o
            factor = lax.rsqrt(jnp.mean(o * o, axis=-1, keepdims=True) + head_epsilon)
            g = gate[rows, lanes]
            lows.append((o * factor * wide_gain(nh) * (g * jax.nn.sigmoid(g))).astype(bf16))
        low = jnp.concatenate(lows, axis=1)
        att[rows] = low
        part = dot(low, wo[...])
        if rel % 2:
            send[rel // 2] = part.astype(bf16)
        else:
            keep[rel // 2] = part


def states_kernel(entry, zst, qkv, wmix, umix, score, states, vnew, qeff):
    groups = qkv.shape[0] // GROUP
    heads = wmix.shape[1] // DH

    def one(i, _):
        for n, h in [(2 * i + j, h) for j in range(2) for h in range(heads)]:
            rows = pl.ds(pl.multiple_of(n * GROUP, GROUP), GROUP)
            lanes = slice(h * DH, (h + 1) * DH)
            at = n * heads + h
            s = zst[at, :, DH:] + fdot(zst[at, :, :DH], entry[h])
            states[at] = s
            w = wmix[rows, lanes]
            vnew[rows, lanes] = umix[rows, lanes] - fdot(w, s)
            qeff[rows, lanes] = qkv[rows, lanes] - fdot(score[at], w)
        return 0

    lax.fori_loop(0, groups // 2, one, 0)


def mid_kernel(x, kept, got, gain, residual, second):
    total = x[...].astype(f32) + kept[...] + got[...].astype(f32)
    residual[...] = total
    second[...] = rms_rows(total, wide_gain(gain)).astype(bf16)


def warm_kernel(wgh, wuh, wdh, gdh, wg, wu, wd, gd, grad_inner, sems):
    loads = [
        pltpu.make_async_copy(src, dst, sems.at[i])
        for i, (src, dst) in enumerate(((wdh, wd), (gdh, gd), (wgh, wg), (wuh, wu)))
    ]
    for load in loads:
        load.start()
    loads[0].wait()
    loads[1].wait()
    tile = 256
    for t in range(gd.shape[0] // tile):
        rows = slice(t * tile, (t + 1) * tile)
        grad_inner[rows] = dot(gd[rows], wd[...], 1, 1)
    loads[2].wait()
    loads[3].wait()


def ffn_half(tp, half, sa, sb, wg, wu, wd, grad_inner, sec, inner, dgate, dup, down_keep, down_send, keep, send):
    share = sa.shape[0]
    sec[:share] = sa[...]
    sec[share:] = sb[...]
    gv = dot(sec[...], wg[...], 1, 1)
    uv = dot(sec[...], wu[...], 1, 1)
    sig = jax.nn.sigmoid(gv)
    act = gv * sig
    inn = (act * uv).astype(bf16)
    gi = jnp.concatenate(
        [grad_inner[rows_of(tp[0] ^ (2 * half + j), share)] for j in range(2)], axis=0
    )
    dg = (gi * uv * (sig * (1.0 + gv * (1.0 - sig)))).astype(bf16)
    du = (gi * act).astype(bf16)
    inner[...] = inn
    dgate[...] = dg
    dup[...] = du
    grad = dot(dg, wg[...]) + dot(du, wu[...])
    keep[0] = grad[:share]
    send[0] = grad[share:].astype(bf16)
    down = dot(inn, wd[...])
    down_keep[0] = down[:share]
    down_send[0] = down[share:].astype(bf16)


def ffn_a_kernel(tp, sa, sb, wg, wu, wd, grad_inner, *outs):
    ffn_half(tp, 0, sa, sb, wg, wu, wd, grad_inner, *outs)


def ffn_b_kernel(plans, tp, place, sa, sb, wg, wu, wd, grad_inner, gd, sec_a, inner_a, dgate_a, dup_a, down_keep, down_send, keep, send, *refs):
    sums, (sec, inner, dgate, dup, acc) = refs[:-5], refs[-5:]
    share = sa.shape[0]
    ffn_half(tp, 1, sa, sb, wg, wu, wd, grad_inner, sec, inner, dgate, dup, down_keep, down_send, keep, send)
    near = [jnp.concatenate([gd[rows_of(tp[0] ^ (2 * i + j), share)] for j in range(2)], axis=0) for i in range(2)]
    for pair, plan in (
        (((inner_a[...], near[0]), (inner[...], near[1])), 0),
        (((dgate_a[...], sec_a[...]), (dgate[...], sec[...])), 1),
        (((dup_a[...], sec_a[...]), (dup[...], sec[...])), 2),
    ):
        acc[...] = dot(*pair[0], 0, 0) + dot(*pair[1], 0, 0)
        put(acc, acc.shape[1], (place[0] & 7), plans[plan], sums)


def turn_kernel(kept, got, residual, gain, grad_y, grad_residual, branch, gain_part):
    gs = kept[...] + got[...].astype(f32)
    v = residual[...]
    g = wide_gain(gain)
    r = lax.rsqrt(jnp.mean(v * v, axis=-1, keepdims=True) + row_epsilon)
    gain_part[...] = jnp.sum(gs * v * r, axis=0, keepdims=True)
    e = gs * g
    back = r * e - v * (r * r * r) * jnp.mean(e * v, axis=-1, keepdims=True)
    total = grad_y[...].astype(f32) + back
    grad_residual[...] = total
    branch[...] = total.astype(bf16)


def flow_kernel(tp, meta, b0, b1, b2, b3, wo, heads_out, gate, nh, qeff, amap, branch, dgate, dout, rst, dev_low, last, nh_part, flows, dev):
    share = b0.shape[0]
    heads = gate.shape[1] // DH
    groups = gate.shape[0] // GROUP
    gains = jnp.zeros((1, DH), f32)
    for half, pair in enumerate(((b0, b1), (b2, b3))):
        both = jnp.concatenate([pair[0][...], pair[1][...]], axis=0)
        ga = dot(both, wo[...], 1, 1)
        for j in range(2):
            rows = rows_of(tp[0] ^ (2 * half + j), share)
            branch[rows] = pair[j][...]
            for h in range(heads):
                lanes = slice(h * DH, (h + 1) * DH)
                gz = ga[j * share : (j + 1) * share, lanes]
                o = heads_out[rows, lanes]
                g = gate[rows, lanes]
                gain = wide_gain(nh)
                r = lax.rsqrt(jnp.mean(o * o, axis=-1, keepdims=True) + head_epsilon)
                sig = jax.nn.sigmoid(g)
                act = g * sig
                e = gz * gain * act
                base = gz * o * r
                gains = gains + jnp.sum(base * act, axis=0, keepdims=True)
                dgate[rows, lanes] = (base * gain * (sig * (1.0 + g * (1.0 - sig)))).astype(bf16)
                dout[rows, lanes] = r * e - o * (r * r * r) * jnp.mean(e * o, axis=-1, keepdims=True)
    nh_part[...] = gains

    def local(i, _):
        for n, h in [(2 * i + j, h) for j in range(2) for h in range(heads)]:
            rows = pl.ds(pl.multiple_of(n * GROUP, GROUP), GROUP)
            lanes = slice(h * DH, (h + 1) * DH)
            flows[n * heads + h] = gdot(qeff[rows, lanes], dout[rows, lanes], 0, 0)
        return 0

    lax.fori_loop(0, groups // 2, local, 0)
    eye = (iota((DH, DH), 0) == iota((DH, DH), 1)).astype(f32)
    for h in range(heads):
        dev[h, :, :DH] = eye
        dev[h, :, DH:] = jnp.zeros((DH, DH), f32)

    def chain(i, _):
        n = groups - 1 - i
        keep = 1.0 - meta[0, n].astype(f32)
        for h in range(heads):
            at = n * heads + h
            later = dev[h]
            rst[at] = later
            moved = gdot(amap[at], later, 0, 0)
            dev[h, :, :DH] = moved[:, :DH] * keep
            dev[h, :, DH:] = (moved[:, DH:] + flows[at]) * keep
        return 0

    lax.fori_loop(0, groups, chain, 0)
    dev_low[...] = dev[...].astype(bf16)
    last[...] = dev[:, :, DH:].astype(bf16)


def side_kernel(qkv, dout, vnew, states, score, ndo, dq, dk):
    heads = dout.shape[1] // DH
    groups = dout.shape[0] // GROUP
    lower = iota((GROUP, GROUP), 0) >= iota((GROUP, GROUP), 1)

    def one(i, _):
        for n, h in [(2 * i + j, h) for j in range(2) for h in range(heads)]:
            rows = pl.ds(pl.multiple_of(n * GROUP, GROUP), GROUP)
            lanes = slice(h * DH, (h + 1) * DH)
            at = n * heads + h
            q = qkv[rows, lanes]
            k = qkv[rows, (heads + h) * DH : (heads + h + 1) * DH]
            do = dout[rows, lanes]
            ndo[rows, lanes] = gdot(score[at], do, 0, 0)
            dn = jnp.where(lower, gdot(do, vnew[rows, lanes], 1, 1), 0.0)
            dq[rows, lanes] = gdot(do, states[at], 1, 1) + gdot(dn, k)
            dk[rows, lanes] = gdot(dn, q, 0, 0)
        return 0

    lax.fori_loop(0, groups // 2, one, 0)


def unit_back(a, grad):
    r = lax.rsqrt(jnp.sum(a * a, axis=-1, keepdims=True) + unit_epsilon)
    return r * grad - a * (r * r * r) * jnp.sum(a * grad, axis=-1, keepdims=True)


def back_kernel(hop_count, meta, *refs):
    hops, refs = refs[:hop_count], refs[hop_count:]
    rst, qkv, conv, cq, ck, cv, beta, inv, states, vnew, ndo, dq, dk1, dc, halo, dbeta = refs
    taps = tap_table(cq, ck, cv)
    heads = ndo.shape[1] // DH
    groups = ndo.shape[0] // GROUP
    total = ndo.shape[0]
    exits = [fold_hops(hops, h) for h in range(heads)]
    strict = iota((GROUP, GROUP), 0) > iota((GROUP, GROUP), 1)
    lane = iota((GROUP, LANES), 1)
    dc[total:] = jnp.zeros((8, dc.shape[1]), f32)

    def one(i, _):
        for j in range(2):
            n = 2 * i + j
            rows = pl.ds(pl.multiple_of(n * GROUP, GROUP), GROUP)
            raws = jnp.zeros((GROUP, LANES), f32)
            for h in range(heads):
                at = n * heads + h
                lanes = [slice((p * heads + h) * DH, (p * heads + h + 1) * DH) for p in range(3)]
                k = qkv[rows, lanes[1]]
                v = qkv[rows, lanes[2]]
                b, sig, live = beta_col(beta, meta, n, h)
                ds = rst[at, :, DH:] + gdot(rst[at, :, :DH], exits[h])
                dvn = ndo[rows, lanes[0]] + gdot(k, ds)
                d = gdot(inv[at], dvn, 0, 0)
                vn = vnew[rows, lanes[0]]
                both = gdot(d, jnp.concatenate([states[at], vn], axis=0), 1, 1)
                dstate = both[:, :DH]
                vds = gdot(vn, ds, 1, 1)
                da = jnp.where(strict, -both[:, DH:], 0.0)
                dak = gdot(da, k)
                datk = gdot(da, k * b, 0, 0)
                dk = dk1[rows, lanes[0]] + vds + b * (dak - dstate) + datk
                db = jnp.sum(d * v + (dak - dstate) * k, axis=-1, keepdims=True)
                db = jnp.where(live, db * sig * (1.0 - sig), 0.0)
                raws = jnp.where(lane == h, db, raws)
                grads = (dq[rows, lanes[0]], dk, d * b)
                for p in range(3):
                    c = conv[rows, lanes[p]]
                    s = jax.nn.sigmoid(c)
                    grad = unit_back(c * s, grads[p]) if p < 2 else grads[p]
                    dc[rows, lanes[p]] = grad * (s * (1.0 + c * (1.0 - s)))
            dbeta[rows] = raws.astype(bf16)
        return 0

    lax.fori_loop(0, groups // 2, one, 0)
    zero = jnp.zeros((8, DH), f32)
    for c in range(3 * heads):
        lanes = slice(c * DH, (c + 1) * DH)
        win = dc[0:8, lanes]
        acc = zero
        for d in range(1, KW):
            part = jnp.where(iota((8, 1), 0) < meta[0, 0] * d, 0.0, win)
            j = KW - 1 - d
            acc = acc + taps(j, c) * jnp.concatenate([zero, part], axis=0)[d : d + 8]
        halo[:, lanes] = acc


def taps_kernel(meta, dc, ext, cq, ck, cv, gp, last, dtaps):
    heads = cq.shape[1] // DH
    groups = gp.shape[0] // GROUP
    taps = tap_table(cq, ck, cv)
    dtaps[...] = jnp.zeros(dtaps.shape, f32)

    def masked(win, d, here, after):
        front = jnp.where(iota((GROUP, 1), 0) < here * d, 0.0, win[:GROUP])
        if after is None:
            return front
        back = jnp.where(iota((8, 1), 0) < after * d, 0.0, win[GROUP:])
        return jnp.concatenate([front, back], axis=0)

    def taps_back(n, _):
        base = pl.multiple_of(n * GROUP, GROUP)
        here = meta[0, n]
        after = meta[0, jnp.minimum(n + 1, groups - 1)]
        for c in range(3 * heads):
            lanes = slice(c * DH, (c + 1) * DH)
            win = dc[pl.ds(base, GROUP + 8), lanes]
            old = ext[pl.ds(pl.multiple_of(base + TAIL - 8, 8), GROUP + 8), lanes]
            acc = taps(KW - 1, c) * win[:GROUP]
            dtaps[KW - 1 : KW, lanes] += jnp.sum(win[:GROUP] * old[8:], axis=0, keepdims=True)
            for d in range(1, KW):
                part = masked(win, d, here, after)
                j = KW - 1 - d
                acc = acc + taps(j, c) * part[d : d + GROUP]
                dtaps[j : j + 1, lanes] += jnp.sum(
                    part[:GROUP] * old[8 - d : 8 - d + GROUP], axis=0, keepdims=True
                )
            gp[pl.ds(base, GROUP), lanes] = acc.astype(bf16)

            @pl.when(n == groups - 1)
            def _():
                last[:, lanes] = acc[GROUP - TAIL :]

        return 0

    lax.fori_loop(0, groups, taps_back, 0)


def hid_kernel(tp, gp_in, last, incoming, dgate, dbeta, wq, wk, wv, wg, wb, x, gp, send, keep, gain_part):
    total = gp.shape[0]
    width = wq.shape[1]
    gp[: total - TAIL] = gp_in[: total - TAIL]
    fixed = jnp.concatenate([last[: TAIL - 8], last[TAIL - 8 :] + incoming[...]], axis=0)
    gp[total - TAIL :] = fixed.astype(bf16)
    share = total // 4
    for half in range(2):
        blocks = [rows_of(tp[0] ^ (2 * half + j), share) for j in range(2)]
        cat = lambda ref: jnp.concatenate([ref[b] for b in blocks], axis=0)
        grads = cat(gp)
        acc = dot(cat(dgate), wg[...], 1, 1)
        small = cat(dbeta).astype(f32)
        for h in range(wb.shape[0]):
            acc = acc + small[:, h : h + 1] * wb[h : h + 1].astype(f32)
        for i, w in enumerate((wq, wk, wv)):
            acc = acc + dot(grads[:, i * width : (i + 1) * width], w[...], 1, 1)
        v = cat(x).astype(f32)
        r = lax.rsqrt(jnp.mean(v * v, axis=-1, keepdims=True) + row_epsilon)
        part = jnp.sum(acc * (v * r), axis=0, keepdims=True)
        gain_part[...] = part if half == 0 else gain_part[...] + part
        keep[half] = acc[:share]
        send[half] = acc[share:].astype(bf16)


def in_kernel(kept, got, x, gain, grad_residual, grad_in):
    gh = kept[...] + got[...].astype(f32)
    v = x[...].astype(f32)
    g = wide_gain(gain)
    r = lax.rsqrt(jnp.mean(v * v, axis=-1, keepdims=True) + row_epsilon)
    e = gh * g
    back = r * e - v * (r * r * r) * jnp.mean(e * v, axis=-1, keepdims=True)
    grad_in[...] = (grad_residual[...] + back).astype(bf16)


def outblock_kernel(tp, meta, kept, got, residual, out):
    total = residual[...] + kept[...] + got[...].astype(f32)
    live = live_mask(meta, tp[0], total.shape[0])
    out[...] = jnp.where(live, total, 0.0).astype(bf16)


def place_kernel(tp, a0, a1, a2, a3, out):
    for rel, part in enumerate((a0, a1, a2, a3)):
        out[rows_of(tp[0] ^ rel, part.shape[0])] = part[...].astype(out.dtype)


def swap(value, bit, axis="tp"):
    count = lax.axis_size(axis)
    return lax.ppermute(value, axis, [(i, i ^ bit) for i in range(count)])


def add_kernel(keep, got, kept, send):
    half = kept.shape[0]
    kept[...] = keep[:half] + got[:half].astype(f32)
    send[...] = (keep[half:] + got[half:].astype(f32)).astype(bf16)


def last_kernel(keep, got, own):
    own[...] = (keep[...] + got[...].astype(f32)).astype(bf16)


def pack_kernel(a, b, out):
    half = a.shape[0]
    out[:half] = a[...]
    out[half:] = b[...]


def fold(order, keep, got, name):
    half = (keep.shape[0] // 2, *keep.shape[1:])
    return order.run(add_kernel, name, [(half, f32), (half, bf16)], [keep, got])


def rank_of(m, bits):
    at = 0
    for bit in bits:
        at = 2 * at + ((m >> bit) & 1)
    return at


class Plan:
    def __init__(self, index, bits, base, size, start=0, folds=1, lane=0):
        self.index, self.bits, self.base, self.size = index, bits, base, size
        self.start, self.folds, self.lane = start, folds, lane

    def rest(self):
        return self.bits, self.base, self.size, self.start, self.folds, self.lane


def put(acc, wide, place, plans, sums):
    for part in plans:
        keep, send = sums[2 * part.index : 2 * part.index + 2]
        height = part.size // part.folds
        for m in range(1 << len(part.bits)):
            at = rank_of(m, part.bits[1:])
            low = (m >> part.bits[0]) & 1
            for i in range(part.folds):
                begin = part.start + (m ^ place) * part.size + i * height
                block = acc[pl.ds(pl.multiple_of(begin, 8), height), part.lane : part.lane + wide]
                rows = slice(part.base, part.base + height)
                lanes = slice(i * wide, (i + 1) * wide)
                if low:
                    send[at, rows, lanes] = block.astype(bf16)
                else:
                    keep[at, rows, lanes] = block


def take(out, place, part, bits, near, far, send=None):
    height = part.size // part.folds
    wide = out.shape[1]
    for m in range(1 << len(bits)):
        source = far if (m >> bits[-1]) & 1 else near
        at = rank_of(m, bits[-2::-1])
        start = part.start + (m ^ place) * part.size
        for i in range(part.folds):
            out[pl.ds(pl.multiple_of(start + i * height, 8), height)] = source[
                at, part.base : part.base + height, i * wide : (i + 1) * wide
            ].astype(f32)
        if send is not None:
            send(pl.ds(pl.multiple_of(start, 8), part.size))


class Sum:
    def __init__(self, order, keep, send, scatter, gather, tag):
        self.order, self.tag, self.gather = order, tag, gather
        self.keep, self.left = keep, list(scatter)
        self.swap(send)
        self.own = self.near = None

    def swap(self, send):
        self.got = swap(send, 1 << self.left.pop(0), "seq")

    def step(self):
        order, tag = self.order, self.tag
        if self.own is None and self.left:
            self.keep, send = fold(order, self.keep, self.got, tag + "_fold")
            self.swap(send)
            return
        if self.own is None:
            (self.own,) = order.run(
                last_kernel, tag + "_last", [(self.keep.shape, bf16)], [self.keep, self.got]
            )
            more = 1 << len(self.gather)
            while more < lax.axis_size("seq"):
                other = swap(self.own, more, "seq")
                self.own = (self.own.astype(f32) + other.astype(f32)).astype(bf16)
                more *= 2
            self.left = list(self.gather)
        else:
            twice = (2 * self.own.shape[0], *self.own.shape[1:])
            (self.own,) = order.run(
                pack_kernel, tag + "_pack", [(twice, bf16)], [self.own, self.got]
            )
        self.swap(self.own)


def pair_kernel(keep_a, got_a, keep_b, got_b, kept, send):
    kept[...] = keep_a[...] + got_a[...].astype(f32)
    send[...] = (keep_b[...] + got_b[...].astype(f32)).astype(bf16)


def fold_pair(order, keep_a, got_a, keep_b, got_b):
    shape = keep_a.shape
    return order.run(
        pair_kernel, "fold_tp", [(shape, f32), (shape, bf16)], [keep_a, got_a, keep_b, got_b]
    )


def scatter_first(order, keep, send):
    return fold(order, keep, swap(send, 1), "fold_tp")


def grads_c_kernel(plans, place, hidden, gp, *refs):
    sums, acc = refs[:-1], refs[-1]
    acc[...] = dot(hidden[...], gp[...], 0, 0)
    put(acc, acc.shape[1] // 3, (place[0] & 7), plans, sums)


def grads_d_kernel(plans, way, base, place, attended, branch, hidden, dgate, small, gains, keep, send, acc, acc2, both):
    sums = (keep, send)
    acc[...] = dot(attended[...], branch[...], 0, 0)
    put(acc, acc.shape[1], (place[0] & 7), plans[:1], sums)
    acc2[...] = dot(hidden[...], dgate[...], 0, 0)
    put(acc2, acc2.shape[1], (place[0] & 7), plans[1:], sums)
    both[...] = small[...] + gains[...]
    for m in range(1 << len(way)):
        line = both[pl.ds(m ^ (place[0] & 7), 1)] + jnp.zeros((8, both.shape[1]), f32)
        at = rank_of(m, way[1:])
        if (m >> way[0]) & 1:
            send[at, base : base + 8] = line.astype(bf16)
        else:
            keep[at, base : base + 8] = line


def settle_kernel(count, jobs, line_at, place, *refs):
    pairs, refs = refs[: 2 * count], refs[2 * count :]
    size = len(jobs)
    outs, (staged, sem) = refs[: len(refs) - size - 1], (refs[len(refs) - size - 1 : -1], refs[-1])
    copies = []
    for parts, out, stage in zip(jobs, outs, staged):

        def send(rows):
            copy = pltpu.make_async_copy(stage.at[rows], out.at[rows], sem.at[len(copies)])
            copy.start()
            copies.append(copy)

        for part, way in parts:
            take(
                stage,
                (place[0] & 7),
                part,
                way,
                *pairs[2 * part.index : 2 * part.index + 2],
                send,
            )
    if line_at is not None:
        index, way, base = line_at
        near, far = pairs[2 * index : 2 * index + 2]
        for m in range(1 << len(way)):
            source = far if (m >> way[-1]) & 1 else near
            at = rank_of(m, way[-2::-1])
            outs[-1][pl.ds(m ^ (place[0] & 7), 1)] = source[at, base : base + 8].astype(f32)[:1]
    for copy in copies:
        copy.wait()


def sum_shapes(blocks, rows, cols):
    return [((blocks // 2, rows, cols), f32), ((blocks // 2, rows, cols), bf16)]


def gather_rel(own):
    near = swap(own, 1)
    far = swap(own, 2)
    return own, near, far, swap(far, 1)


def shift(value, steps):
    count = lax.axis_size("seq")
    pairs = [(i, i + steps) for i in range(count) if 0 <= i + steps < count]
    return lax.ppermute(value, "seq", pairs)


def hops_of(dev, last, sign, reach):
    return [shift(dev, sign * k) for k in range(1, reach)] + [shift(last, sign * reach)]


def small_kernel(dtaps, dbeta, hidden, in_part, mid_part, head_part, local, gains):
    wide = dtaps.shape[1]
    local[...] = jnp.zeros(local.shape, f32)
    local[0:KW, :wide] = dtaps[...]
    local[KW : KW + 2] = dot(dbeta[...], hidden[...], 0, 0)[:2]
    gains[...] = jnp.zeros(gains.shape, f32)
    gains[KW + 2 : KW + 3] = in_part[...]
    gains[KW + 3 : KW + 4] = mid_part[...]
    gains[0:1, wide : wide + head_part.shape[1]] = head_part[...]


def plus_kernel(a, b, out):
    out[...] = a[...] + b[...]


def plus(order, a, b):
    return order.run(plus_kernel, "plus", [(a.shape, f32)], [a, b])[0]


def shards(
    layer_input,
    seq_groups,
    seq_pads,
    norm_in,
    w_query,
    w_key,
    w_value,
    conv_query,
    conv_key,
    conv_value,
    w_beta,
    w_gate_out,
    norm_head,
    w_out,
    norm_mid,
    w_gate,
    w_up,
    w_down,
    cotangent,
):
    total, model = layer_input.shape
    width = w_query.shape[1]
    heads = width // DH
    groups = total // GROUP
    share = total // 4
    ffw = w_gate.shape[1]
    seq_count = lax.axis_size("seq")
    reach = max(1, seq_count // 4)
    tp_rank = lax.axis_index("tp")
    tp = tp_rank.astype(jnp.int32).reshape(1)
    blocks = 8
    place = lax.axis_index("seq").astype(jnp.int32).reshape(1)
    taps = (conv_query, conv_key, conv_value)
    wb = w_beta.T
    tail = shift(layer_input[total - TAIL :], 1)
    chains = groups * heads
    wide = (total, width)
    mats = 2 * total * model
    order = Order()
    run = order.run

    def begin(keep, send, scatter, gather, tag):
        made = Sum(order, keep, send, scatter, gather, tag)
        made.place = place
        return made

    weight = pltpu.VMEM((model, width), bf16)
    rows = pltpu.VMEM((total, model), bf16)
    ext_shape = (total + TAIL, 3 * width)
    conv_shape = (total, 3 * width)
    inv_shape = (chains, GROUP, GROUP)
    map_shape = (chains, DH, DH)
    zst_shape = (chains, DH, 2 * DH)
    dev_shapes = [((heads, DH, 2 * DH), f32), ((heads, DH, DH), f32)]
    near = "near"
    far = "far"
    tp_sums = [((2, share, model), bf16), ((2, share, model), f32)]
    (
        gate_raw, beta_raw, meta, qkv, wmix, umix, score, zst, dev, last,
        hidden, grad_down, x_own, gd_own, ext, conv, inv, amap,
    ) = run(
        front_kernel,
        "front",
        [
            (wide, f32, near),
            ((total, heads), f32, near),
            ((2, groups), jnp.int32),
            (conv_shape, f32, near),
            (wide, f32, near),
            (wide, f32, near),
            (inv_shape, f32, near),
            (zst_shape, f32, near),
            *[(shape, bf16) for shape, _ in dev_shapes],
            ((total, model), bf16, far),
            ((total, model), bf16, far),
            ((share, model), bf16, far),
            ((share, model), bf16, far),
            (ext_shape, f32, far),
            (conv_shape, f32, far),
            (inv_shape, f32, far),
            (map_shape, f32, far),
        ],
        [place, tp, seq_groups, seq_pads, layer_input, cotangent, norm_in, w_query, w_key, w_value, w_gate_out, wb, tail, *taps],
        smem=(0, 1, 2, 3),
        smem_out=(2,),
        hbm=(4, 5, 7, 8, 9, 10),
        pin=(2, 3, 4, 5, 6, 7, 8, 9, 10, 11, 13, 14, 15),
        scratch=[
            rows, rows, weight, weight, weight, weight, rows, rows,
            pltpu.VMEM(ext_shape, f32),
            pltpu.VMEM(conv_shape, f32),
            pltpu.VMEM(inv_shape, f32),
            pltpu.VMEM(map_shape, f32),
            pltpu.VMEM(map_shape, f32),
            pltpu.VMEM(dev_shapes[0][0], f32),
            pltpu.SemaphoreType.DMA((6,)),
            pltpu.SemaphoreType.DMA((8,)),
        ],
        vmem=22,
    )
    hops = hops_of(dev, last, 1, reach)
    mout, oloc = run(
        local_kernel, "local", [(wide, f32, near)] * 2, [qkv, wmix, umix, score, zst]
    )
    heads_out, attended, send, keep, entry = run(
        lambda *r: out_kernel(reach, *r),
        "out",
        [(wide, f32, near), (wide, bf16, near), *tp_sums, ((heads, DH, DH), f32)],
        [tp, *hops, mout, oloc, gate_raw, norm_head, w_out],
        smem=(0,),
    )
    kept, cross = scatter_first(order, keep, send)
    got = swap(cross, 2)
    states, vnew, qeff = run(
        states_kernel,
        "states",
        [(map_shape, f32, near), (wide, f32, near), (wide, f32, near)],
        [entry, zst, qkv, wmix, umix, score],
    )
    residual, second_own = run(
        mid_kernel,
        "mid",
        [((share, model), f32, near), ((share, model), bf16)],
        [x_own, kept[0], got[0], norm_mid],
    )
    size = ffw // blocks
    ways = [WAYS[name] for name in ("f1", "f2", "f3", "f4")]
    flows = {}

    def go(slot):
        for name in STEPS[slot]:
            flows[name].step()

    near_up = size // 16 * 8
    far_up = size - near_up
    down_parts = [Plan(0, ways[0][0], 0, size)]
    gate_parts = [Plan(1, ways[1][0], 0, size)]
    up_parts = [
        Plan(0, ways[0][0], size, near_up),
        Plan(1, ways[1][0], size, far_up, start=near_up * blocks),
    ]
    plans_a = (down_parts, gate_parts, up_parts)
    f1_rows, f2_rows = size + near_up, size + far_up
    own_rows, beside_rows = second_own, swap(second_own, 1)
    far_rows = swap(second_own, 2)
    w_shape = (ffw, model)
    wg, wu, wd, gd, grad_inner = run(
        warm_kernel,
        "warm",
        [
            (w_shape, bf16, near),
            (w_shape, bf16, near),
            (w_shape, bf16, near),
            ((total, model), bf16, near),
            ((total, ffw), f32, near),
        ],
        [w_gate.T, w_up.T, w_down, grad_down],
        hbm=(0, 1, 2, 3),
        pin=(0, 1, 2, 3),
        scratch=[pltpu.SemaphoreType.DMA((4,))],
    )
    part = (1, share, model)
    half_ffn = ((2 * share, ffw), bf16)
    half_outs = [(part, f32), (part, bf16)] * 2
    sec_a, inner_a, dgate_a, dup_a, down_keep_a, down_send_a, keep_a, send_a = run(
        ffn_a_kernel,
        "ffn_a",
        [((2 * share, model), bf16), half_ffn, half_ffn, half_ffn, *half_outs],
        [tp, own_rows, beside_rows, wg, wu, wd, grad_inner],
        smem=(0,),
        vmem=12,
    )
    far_rows, sec_a = lax.optimization_barrier((far_rows, sec_a))
    near_a = swap(send_a, 1)
    down_near_a = swap(down_send_a, 1)
    down_keep_b, down_send_b, keep_b, send_b, *sums = run(
        lambda *r: ffn_b_kernel(plans_a, *r),
        "ffn_b",
        [*half_outs, *sum_shapes(blocks, f1_rows, model), *sum_shapes(blocks, f2_rows, model)],
        [tp, place, far_rows, swap(far_rows, 1), wg, wu, wd, grad_inner, gd, sec_a, inner_a, dgate_a, dup_a],
        smem=(0, 1),
        scratch=[
            pltpu.VMEM((2 * share, model), bf16),
            *[pltpu.VMEM((2 * share, ffw), bf16)] * 3,
            pltpu.VMEM((ffw, model), f32),
        ],
        vmem=16,
    )
    near_b = swap(send_b, 1)
    flows["f1"] = begin(sums[0], sums[1], *ways[0], "f1")
    flows["f2"] = begin(sums[2], sums[3], *ways[1], "f2")
    kept, cross = fold_pair(order, keep_a, near_a, keep_b, near_b)
    got = swap(cross, 2)
    grad_residual, branch_own, mid_part = run(
        turn_kernel,
        "turn",
        [((share, model), f32), ((share, model), bf16), ((1, model), f32)],
        [kept[0], got[0], residual, norm_mid, gd_own],
    )
    branch_all = gather_rel(branch_own)
    branch, dgate_raw, dout, rst, dev, last, head_part = run(
        flow_kernel,
        "flow",
        [
            ((total, model), bf16),
            (wide, bf16),
            (wide, f32),
            (zst_shape, f32),
            *[(shape, bf16) for shape, _ in dev_shapes],
            ((1, DH), f32),
        ],
        [tp, meta, *branch_all, w_out, heads_out, gate_raw, norm_head, qeff, amap],
        smem=(0, 1),
        scratch=[pltpu.VMEM(map_shape, f32), pltpu.VMEM(dev_shapes[0][0], f32)],
    )
    hops = hops_of(dev, last, -1, reach)
    down_near_b = swap(down_send_b, 1)
    ndo, dq, dk = run(
        side_kernel,
        "side",
        [(wide, f32)] * 3,
        [qkv, dout, vnew, states, score],
    )
    down_kept, cross = fold_pair(order, down_keep_a, down_near_a, down_keep_b, down_near_b)
    down_got = swap(cross, 2)
    order.wait(*hops)
    go("hops")
    dc, halo, dbeta = run(
        lambda *r: back_kernel(reach, *r),
        "back",
        [((total + 8, 3 * width), f32), ((8, 3 * width), f32), ((total, LANES), bf16)],
        [meta, *hops, rst, qkv, conv, *taps, beta_raw, inv, states, vnew, ndo, dq, dk],
        smem=(0,),
    )
    incoming = shift(halo, -1)
    go("back")
    gp, last, dtaps = run(
        taps_kernel,
        "taps",
        [(conv_shape, bf16), ((TAIL, 3 * width), f32), ((KW, 3 * width), f32)],
        [meta, dc, ext, *taps],
        smem=(0,),
    )
    (out_own,) = run(
        outblock_kernel,
        "outblk",
        [((share, model), bf16)],
        [tp, meta, down_kept[0], down_got[0], residual],
        smem=(0, 1),
    )
    go("taps")
    gp, send, keep, in_part = run(
        hid_kernel,
        "hid",
        [(conv_shape, bf16), *tp_sums, ((1, model), f32)],
        [tp, gp, last, incoming, dgate_raw, dbeta, w_query, w_key, w_value, w_gate_out, wb, layer_input],
        smem=(0,),
        vmem=12,
    )
    beside = swap(send, 1)
    piece = model // blocks
    fold_rows = piece * width // model
    split = dict(folds=model // width)
    plans_c = [
        Plan(0, ways[2][0], i * fold_rows, piece, lane=i * width, **split) for i in range(3)
    ]
    keep_c, send_c = run(
        lambda *r: grads_c_kernel(plans_c, *r),
        "grads_c",
        sum_shapes(blocks, 3 * fold_rows, model),
        [place, hidden, gp],
        smem=(0,),
        scratch=[pltpu.VMEM((model, 3 * width), f32)],
        vmem=16,
    )
    flows["f3"] = begin(keep_c, send_c, *ways[2], "f3")
    go("hid")
    kept, cross = fold(order, keep, beside, "fold_tp")
    got = swap(cross, 2)
    row8 = ((8, model), f32)
    small, gains = run(
        small_kernel, "small", [row8, row8], [dtaps, dbeta, hidden, in_part, mid_part, head_part]
    )
    gains = plus(order, gains, swap(gains, 1))
    far_gains = swap(gains, 2)
    go("x")
    (grad_in_own,) = run(
        in_kernel,
        "inp",
        [((share, model), bf16)],
        [kept[0], got[0], x_own, norm_in, grad_residual],
    )
    grad_in_all = gather_rel(grad_in_own)
    gains = plus(order, gains, far_gains)
    wo_rows = width // blocks
    out_parts = [Plan(0, ways[3][0], 0, wo_rows)]
    gate_out_parts = [Plan(0, ways[3][0], wo_rows, piece, **split)]
    line_base = wo_rows + fold_rows
    keep_d, send_d = run(
        lambda *r: grads_d_kernel(out_parts + gate_out_parts, ways[3][0], line_base, *r),
        "grads_d",
        sum_shapes(blocks, line_base + 8, model),
        [place, attended, branch, hidden, dgate_raw, small, gains],
        smem=(0,),
        scratch=[
            pltpu.VMEM((width, model), f32),
            pltpu.VMEM((model, width), f32),
            pltpu.VMEM((8, model), f32),
        ],
        vmem=12,
    )
    flows["f4"] = begin(keep_d, send_d, *ways[3], "f4")
    out_all = gather_rel(out_own)
    results = {}

    def settle(name, jobs, used, outs, line_at=None):
        return run(
            lambda *r: settle_kernel(len(used), jobs, line_at, *r),
            name,
            [(o, f32, far) for o in outs[: len(jobs)]] + [(o, f32) for o in outs[len(jobs) :]],
            [place, *[a for flow in used for a in (flows[flow].own, flows[flow].got)]],
            smem=(0,),
            scratch=[
                *[pltpu.VMEM(o, f32) for o in outs[: len(jobs)]],
                pltpu.SemaphoreType.DMA((blocks * sum(len(parts) for parts in jobs),)),
            ],
        )

    def wayed(parts, first_flow=0):
        moved = [Plan(p.index - first_flow, *p.rest()) for p in parts]
        return [(m, ways[p.index][1]) for m, p in zip(moved, parts)]

    def late(parts, flow):
        return [(part, ways[flow][1]) for part in parts]

    for name in STEPS["tail"]:
        if name in flows:
            flows[name].step()
        elif name in ("in", "out"):
            results[name] = run(
                place_kernel,
                "place_" + name,
                [((total, model), f32 if name == "in" else bf16)],
                [tp, *(grad_in_all if name == "in" else out_all)],
                smem=(0,),
            )
        elif name == "s1":
            results[name] = settle(
                "settle_1",
                [wayed(down_parts), wayed(up_parts)],
                ["f1", "f2"],
                [(ffw, model)] * 2,
            )
        elif name == "s2":
            results[name] = settle("settle_2", [wayed(gate_parts, 1)], ["f2"], [(ffw, model)])
        elif name == "s3":
            results[name] = settle(
                "settle_3", [late([part], 2) for part in plans_c], ["f3"], [(model, width)] * 3
            )
        else:
            results[name] = settle(
                "settle_4",
                [late(out_parts, 3), late(gate_out_parts, 3)],
                ["f4"],
                [(width, model), (model, width), (8, model)],
                line_at=(0, ways[3][1], line_base),
            )
    (grad_input,) = results["in"]
    (block_out,) = results["out"]
    grad_down_w, grad_up_w = results["s1"]
    (grad_gate_w,) = results["s2"]
    hidden_sums = results["s3"]
    grad_out_w, grad_gate_out_w, small = results["s4"]
    cut = model // 4
    head_cut = DH // 4
    gain_of = lambda row, size, lane=0: lax.dynamic_slice(
        small, (row, lane + tp_rank * size), (1, size)
    ).reshape(size)
    tap_of = lambda i: small[:KW, i * width : (i + 1) * width]
    return (
        block_out,
        grad_input,
        gain_of(KW + 2, cut),
        hidden_sums[0],
        hidden_sums[1],
        hidden_sums[2],
        tap_of(0),
        tap_of(1),
        tap_of(2),
        small[KW : KW + heads].T,
        grad_gate_out_w,
        gain_of(0, head_cut, 3 * width),
        grad_out_w,
        gain_of(KW + 3, cut),
        grad_gate_w.T,
        grad_up_w.T,
        grad_down_w,
    )


def solution(mesh):
    rows = P("seq", None)
    cols = P(None, "tp")
    return jax.shard_map(
        shards,
        mesh=mesh,
        in_specs=(rows, P(), P(), P(), cols, cols, cols, cols, cols, cols, cols, cols, P(), P("tp", None), P(), cols, cols, P("tp", None), rows),
        out_specs=(rows, rows, P("tp"), cols, cols, cols, cols, cols, cols, cols, cols, P("tp"), P("tp", None), P("tp"), cols, cols, P("tp", None)),
        check_vma=False,
    )
```
